128 devices in a mesh: dp: 16 (over z, y), mp: 8 (over x, core).
Axes of the slice: x: 4, y: 4, z: 4, core: 2. Of those that a mesh axis runs over, the one named last changes fastest.
Arguments:
- tokens: bfloat16 [32768, 1536], P(('dp', 'mp')), may hold values from -6 to 6
- lengths: int32 [16, 4], P('dp'), may hold values from 1 to 1024, 2048 in all within a row
- request_adapter: int32 [16, 4], P('dp'), may hold values from 0 to 15
- group_page_slots: int32 [16, 16], P('dp'), may hold values from 0 to 15, as said below
- routes: int32 [32768, 4], P(('dp', 'mp')), may hold values from 0 to 31, all different within a row; in each aligned block of 256 rows (0 to 255, 256 to 511, ...) at most 48 rows name the same one
- attention_gain: float32 [1536], replicated, may hold values from 0.1 to 1.9
- query_key_value_weight: bfloat16 [1536, 2048], P(None, 'mp')
- adapter_down_weight: bfloat16 [16, 1536, 16], P('dp'), may hold values from -0.15625 to 0.15625
- adapter_up_weight: bfloat16 [16, 16, 1536], P('dp'), may hold values from -0.75 to 0.75
- output_weight: bfloat16 [1536, 1536], P(None, 'mp'), may hold values from -0.15625 to 0.15625
- expert_norm_gain: float32 [1536], replicated, may hold values from 0.1 to 1.9
- router: bfloat16 [1536, 32], replicated, may hold values from -0.3125 to 0.3125
- expert_gate_up_weight: bfloat16 [32, 1536, 1536], P('dp'), may hold values from -0.15625 to 0.15625
- expert_down_weight: bfloat16 [32, 768, 1536], P('dp'), may hold values from -0.21875 to 0.21875
Outputs:
- layer_out: bfloat16 [32768, 1536], P(('dp', 'mp'))
- kv_pool: bfloat16 [256, 128, 512], P(('dp', 'mp'))
The draws below stay inside these ranges and needn't reach their ends.
Inputs may be any that keep to these rules, and one draw needn't show every extreme that they name: `lengths`: each row sums to 2048, and its longest length is exactly half of 2048. `group_page_slots`: each row is a permutation of the 16 slots of its group. `routes`: A token names 4 different experts; among the rows of one device no expert is named more than 48 times.
All inputs are finite; a program needn't handle non-finite values.
Results may differ from the reference program's by a relative error of at most 0.02.
The reference program's roundings to bfloat16 on the way count: a program that leaves them out, or rounds other values in their place, can miss the bound.
Values may be sent and summed in bfloat16 or wider, within the bound.
A program may use at most 128 MiB of HBM per device.

```python
import math
import jax
import jax.numpy as jnp
import numpy as np
from jax import lax

MODEL_WIDTH = 1536
QUERY_HEADS = 12
KEY_VALUE_HEADS = 2
HEAD_SIZE = 128
EXPERTS = 32
FFE = 768
TOPK = 4
ADAPTER_COUNT = 16
ADAPTER_RANK = 16
PAGE = 128
SEQS = 4
TOK_DEV = 256
QUERY_COLUMNS = 1536
KVD = 256
CAP = 48
GROUPS = 16
GROUP_TOKENS = 2048
TOKENS = 32768
PG_GRP = 16
PAGES = 256
N_DP = 16
N_MP = 8


def draw_group_page_slots(key, part):
    row_keys = jax.random.split(key, GROUPS)
    return jax.vmap(lambda row_key: jax.random.permutation(row_key, PG_GRP))(row_keys).astype(jnp.int32)


def draw_query_key_value_weight(key, part):
    base_offset = jax.random.normal(key, (MODEL_WIDTH, QUERY_COLUMNS + 2 * KVD), jnp.float32) * MODEL_WIDTH ** (-0.5)
    return base_offset.astype(jnp.bfloat16)


def touch_ends(values, stream_key, low, largest):
    shape = values.shape
    place = [jax.random.randint(jax.random.fold_in(stream_key, axis), (), 0, shape[axis]) for axis in range(len(shape))]
    values = values.at[tuple(place)].set(low)
    longest = shape.index(max(shape))
    place[longest] = (place[longest] + 1) % shape[longest]
    return values.at[tuple(place)].set(largest)


def levels(own_key, dims, cuts, smallest, largest):
    factor_of, own = 1.0, jax.random.fold_in(own_key, 6)
    for dim, blocks in cuts:
        steps = jnp.exp(jax.random.uniform(jax.random.fold_in(own, dim), (blocks,), jnp.float32, smallest / len(cuts), largest / len(cuts)))
        factor_of = factor_of * jnp.repeat(steps, dims[dim] // blocks).reshape([-1 if axis == dim else 1 for axis in range(len(dims))])
    return factor_of


def split_up(count, total, reach, lean):
    loads = [(1 << 20) // math.isqrt(rank ** lean) + 1 for rank in range(2, count + 1)]
    rest, holding = total - reach - (count - 1), [1] * (count - 1)
    while rest > 0:
        candidates = [i for i in range(count - 1) if holding[i] < reach]
        whole, remaining = sum([loads[i] for i in candidates]), rest
        for i in candidates:
            extra = min(reach - holding[i], max(1, remaining * loads[i] // whole), rest)
            holding[i] = holding[i] + extra
            rest = rest - extra
    return np.array([reach] + holding)


def ragged_sizes(rng, amount, total, limit, slope):
    if amount == 2:
        one = jax.random.randint(rng, (), max(1, total - limit), min(limit, total - 1) + 1)
        return jnp.stack([one, total - one])
    sizes = jnp.asarray(split_up(amount, total, limit, slope), jnp.int32)
    twos = (amount - 1) // 2
    source_of, taker = sizes[1:1 + 2 * twos:2], sizes[2:2 + 2 * twos:2]
    margin = jnp.minimum(source_of - 1, limit - taker)
    passed = jax.random.randint(jax.random.fold_in(rng, 1), (twos,), 0, 1 << 20) % (margin + 1)
    sizes = sizes.at[1:1 + 2 * twos:2].set(source_of - passed).at[2:2 + 2 * twos:2].set(taker + passed)
    return sizes[jax.random.permutation(jax.random.fold_in(rng, 2), amount)]


def assign_block(stream_key, own, number, rows, number_of, top, limit, slope):
    sequence = jax.random.permutation(stream_key, number_of)
    packed, ordinary = portions_of(number_of, rows * top, limit, slope, True), portions_of(number_of, rows * top, limit, slope, False)
    places = jnp.arange(number_of)

    def named(sizes, turn):
        used = int((sizes > 0).sum())
        fixed = max(1, used // 4)
        moved = fixed + (places - fixed + turn * (used - fixed)) % max(1, number_of - fixed)
        return jnp.zeros((number_of,), jnp.int32).at[sequence[jnp.where(places < fixed, places, moved)]].set(jnp.asarray(sizes, jnp.int32))

    sizes = jnp.where(number % 4 == 0, named(packed, number // 4), named(ordinary, number - number // 4 - 1))
    mixed = jax.random.permutation(jax.random.fold_in(own, 3), number_of)
    source_of, taker = mixed[0:number_of // 2 * 2:2], mixed[1:number_of // 2 * 2:2]
    slack = jnp.minimum(sizes[source_of] - 1, limit - sizes[taker]) // 2
    slack = jnp.where((source_of == sequence[0]) | (taker == sequence[0]) | (sizes[taker] == 0), 0, jnp.maximum(slack, 0))
    moved = jax.random.randint(jax.random.fold_in(own, 4), (number_of // 2,), 0, 1 << 20) % (slack + 1)
    sizes = sizes.at[source_of].add(-moved).at[taker].add(moved)
    items = jnp.searchsorted(jnp.cumsum(sizes), jnp.arange(rows * top), side="right").astype(jnp.int32)
    table = items.reshape(top, rows).T
    table = table[jax.random.permutation(jax.random.fold_in(own, 1), rows)]
    turn = jax.random.randint(jax.random.fold_in(own, 2), (rows, 1), 0, top)
    return jnp.take_along_axis(table, (jnp.arange(top)[None, :] + turn) % top, axis=1)


def portions_of(number_of, total, most, skew, full):
    loads = [(1 << 20) // math.isqrt(standing ** skew) + 1 for standing in range(1, number_of + 1)]
    largest = most if full else min(most, max(-(-total // number_of), total * loads[0] // sum(loads)))
    least = 1 if total - largest >= number_of - 1 else 0
    counts, surplus = [largest] + [least] * (number_of - 1), total - largest - least * (number_of - 1)
    while surplus > 0:
        movable = [i for i in range(1, number_of) if counts[i] < largest] or [i for i in range(1, number_of) if counts[i] < most]
        whole, left = sum([loads[i] for i in movable]), surplus
        for i in movable:
            more = min(most - counts[i], max(1, left * loads[i] // whole), surplus)
            counts[i] = counts[i] + more
            surplus = surplus - more
    return np.array(counts)


def gaussian(own_key, dims, width, reach, shards=(), kind=jnp.bfloat16):
    factor_of = levels(own_key, dims, shards, -0.22, 0.18) if shards else 1.0
    entries = jax.random.normal(own_key, dims, jnp.float32) * width * factor_of
    return jnp.minimum(jnp.maximum(entries, -reach), reach).astype(kind)


def setup_inputs(seed: int = 0) -> dict:
    key_list = jax.random.split(jax.random.key(seed), 15)
    tokens = gaussian(key_list[0], (TOKENS, MODEL_WIDTH), 1.0, 6.0, ((0, 128),))
    lengths = jax.vmap(lambda own: ragged_sizes(own, SEQS, GROUP_TOKENS, GROUP_TOKENS // 2, 2))(jax.random.split(key_list[1], GROUPS)).reshape((GROUPS, SEQS)).astype(jnp.int32)
    request_adapter = touch_ends(jax.random.randint(key_list[2], (GROUPS, SEQS), 0, ADAPTER_COUNT), jax.random.fold_in(key_list[2], 1), 0, ADAPTER_COUNT - 1).astype(jnp.int32)
    group_page_slots = draw_group_page_slots(jax.random.fold_in(key_list[14], 71), 0)
    routes_keys = jax.random.split(jax.random.fold_in(key_list[4], 1), TOKENS // TOK_DEV)
    routes_turns = jax.random.permutation(jax.random.fold_in(key_list[4], 3), TOKENS // TOK_DEV)
    routes = jax.vmap(lambda own, number: assign_block(jax.random.fold_in(key_list[4], 2), own, number, TOK_DEV, EXPERTS, TOPK, CAP, 1))(routes_keys, routes_turns).reshape((TOKENS, TOPK))
    attention_gain = jnp.clip(1.0 + 0.18 * jax.random.normal(key_list[5], (MODEL_WIDTH,), jnp.float32), 0.1, 1.9)
    query_key_value_weight = draw_query_key_value_weight(jax.random.fold_in(key_list[14], 71), 0)
    adapter_down_weight = gaussian(key_list[7], (ADAPTER_COUNT, MODEL_WIDTH, ADAPTER_RANK), MODEL_WIDTH ** -0.5, 0.15625, ((0, 16),))
    adapter_up_weight = gaussian(key_list[8], (ADAPTER_COUNT, ADAPTER_RANK, QUERY_COLUMNS), (4 * ADAPTER_RANK) ** -0.5, 0.75, ((0, 16),))
    output_weight = gaussian(key_list[9], (QUERY_COLUMNS, MODEL_WIDTH), QUERY_COLUMNS ** -0.5, 0.15625, ((1, 8),))
    expert_norm_gain = jnp.clip(1.0 + 0.18 * jax.random.normal(key_list[10], (MODEL_WIDTH,), jnp.float32), 0.1, 1.9)
    router = gaussian(key_list[11], (MODEL_WIDTH, EXPERTS), (MODEL_WIDTH // 4) ** -0.5, 0.3125)
    expert_gate_up_weight = gaussian(key_list[12], (EXPERTS, MODEL_WIDTH, 2 * FFE), MODEL_WIDTH ** -0.5, 0.15625, ((0, 16),))
    expert_down_weight = gaussian(key_list[13], (EXPERTS, FFE, MODEL_WIDTH), FFE ** -0.5, 0.21875, ((0, 16),))
    return {"tokens": tokens, "lengths": lengths, "request_adapter": request_adapter, "group_page_slots": group_page_slots, "routes": routes, "attention_gain": attention_gain, "query_key_value_weight": query_key_value_weight, "adapter_down_weight": adapter_down_weight, "adapter_up_weight": adapter_up_weight, "output_weight": output_weight, "expert_norm_gain": expert_norm_gain, "router": router, "expert_gate_up_weight": expert_gate_up_weight, "expert_down_weight": expert_down_weight}


eps = 1e-06
neg_fill = -1e+30

def rms_norm(values, gains):
    widened = values.astype(jnp.float32)
    inv_rms = lax.rsqrt(lax.optimization_barrier(jnp.mean(widened * widened, axis=-1, keepdims=True)) + eps)
    return (widened * inv_rms * gains.astype(jnp.float32)).astype(jnp.bfloat16)

def segment_ids(length_row, offset, count):
    seq_ends = jnp.cumsum(length_row.astype(jnp.int32))
    positions = offset + jnp.arange(count, dtype=jnp.int32)
    return lax.optimization_barrier(jnp.sum((positions[:, None] >= seq_ends[None, :]).astype(jnp.int32), axis=1))

def single_group(group_entries, attention_gain, query_key_value_weight, adapter_down_weight, adapter_up_weight, output_weight):
    group_tokens, length_row, adapter_row, page_row = group_entries
    query_seg = segment_ids(length_row, 0, GROUP_TOKENS)
    normalized_input = rms_norm(group_tokens, attention_gain)
    complete_query_key_value = jnp.dot(normalized_input, query_key_value_weight, preferred_element_type=jnp.float32)
    seq_match = (query_seg[:, None] == jnp.arange(SEQS, dtype=jnp.int32)[None, :]).astype(jnp.int32)
    token_adapter = lax.optimization_barrier(jnp.sum(seq_match * adapter_row.astype(jnp.int32)[None, :], axis=1))
    flattened_down = jnp.transpose(adapter_down_weight, (1, 0, 2)).reshape(MODEL_WIDTH, ADAPTER_COUNT * ADAPTER_RANK)
    adapter_middle = jnp.dot(normalized_input, flattened_down, preferred_element_type=jnp.float32).reshape(GROUP_TOKENS, ADAPTER_COUNT, ADAPTER_RANK)
    adapter_selected = token_adapter[:, None] == jnp.arange(ADAPTER_COUNT, dtype=jnp.int32)[None, :]
    adapter_middle = jnp.where(adapter_selected[:, :, None], adapter_middle, 0.0).astype(jnp.bfloat16).reshape(GROUP_TOKENS, ADAPTER_COUNT * ADAPTER_RANK)
    adapter_query = jnp.dot(adapter_middle, adapter_up_weight.reshape(ADAPTER_COUNT * ADAPTER_RANK, QUERY_COLUMNS), preferred_element_type=jnp.float32)
    query_rows = (complete_query_key_value[:, :QUERY_COLUMNS] + adapter_query).astype(jnp.bfloat16)
    key_value = complete_query_key_value[:, QUERY_COLUMNS:].astype(jnp.bfloat16)
    positions = jnp.arange(GROUP_TOKENS, dtype=jnp.int32)
    allowed = (query_seg[:, None] == query_seg[None, :]) & (positions[None, :] <= positions[:, None])
    group_share = QUERY_HEADS // KEY_VALUE_HEADS
    pieces = []
    for head_position in range(KEY_VALUE_HEADS):
        lo_col = head_position * group_share * HEAD_SIZE
        q_head = query_rows[:, lo_col:lo_col + group_share * HEAD_SIZE].reshape(GROUP_TOKENS, group_share, HEAD_SIZE).astype(jnp.float32)
        k_head = key_value[:, head_position * HEAD_SIZE:(head_position + 1) * HEAD_SIZE].astype(jnp.float32)
        v_head = key_value[:, KVD + head_position * HEAD_SIZE:KVD + (head_position + 1) * HEAD_SIZE].astype(jnp.float32)
        scores = jnp.einsum('tgd,sd->tgs', q_head, k_head) * HEAD_SIZE ** (-0.5)
        scores = jnp.where(allowed[:, None, :], scores, neg_fill)
        row_max = lax.optimization_barrier(jnp.max(scores, axis=2, keepdims=True))
        expd = jnp.exp(scores - row_max)
        probs = (expd / lax.optimization_barrier(jnp.sum(expd, axis=2, keepdims=True))).astype(jnp.bfloat16)
        mixed = jnp.einsum('tgs,sd->tgd', probs.astype(jnp.float32), v_head)
        pieces.append(mixed.astype(jnp.bfloat16).reshape(GROUP_TOKENS, group_share * HEAD_SIZE))
    attended = jnp.concatenate(pieces, axis=1)
    projected = jnp.dot(attended, output_weight, preferred_element_type=jnp.float32)
    residual = (group_tokens.astype(jnp.float32) + projected).astype(jnp.bfloat16)
    pool_group = jnp.zeros((PG_GRP, PAGE, 2 * KVD), jnp.bfloat16)
    pool_group = pool_group.at[page_row.astype(jnp.int32)].set(key_value.reshape(PG_GRP, PAGE, 2 * KVD))
    return (residual, pool_group)

def reference(tokens, lengths, request_adapter, group_page_slots, routes, attention_gain, query_key_value_weight, adapter_down_weight, adapter_up_weight, output_weight, expert_norm_gain, router, expert_gate_up_weight, expert_down_weight):
    grouped = tokens.reshape(GROUPS, GROUP_TOKENS, MODEL_WIDTH)

    def run_group(group_entries):
        return single_group(group_entries, attention_gain, query_key_value_weight, adapter_down_weight, adapter_up_weight, output_weight)
    residual, pool = lax.map(run_group, (grouped, lengths, request_adapter, group_page_slots))
    residual = residual.reshape(TOKENS, MODEL_WIDTH)
    pool = pool.reshape(PAGES, PAGE, 2 * KVD)
    ffn_in = rms_norm(residual, expert_norm_gain)
    logits = jnp.dot(ffn_in, router, preferred_element_type=jnp.float32)
    chosen = jnp.take_along_axis(logits, routes.astype(jnp.int32), axis=1)
    route_weights = jax.nn.softmax(chosen, axis=1)
    flat_routes = routes.reshape(-1).astype(jnp.int32)
    flat_weight = route_weights.reshape(-1)
    bound = N_DP * N_MP * CAP

    def one_expert(mixture, expert_index):
        is_hit = flat_routes == expert_index
        pair_index = jnp.nonzero(is_hit, size=bound, fill_value=0)[0].astype(jnp.int32)
        is_live = (jnp.arange(bound, dtype=jnp.int32) < jnp.sum(is_hit.astype(jnp.int32))).astype(jnp.float32)
        token_index = pair_index // TOPK
        pair_rows = ffn_in[token_index]
        gate_up = jnp.dot(pair_rows, expert_gate_up_weight[expert_index], preferred_element_type=jnp.float32)
        active = (jnp.maximum(gate_up[:, :FFE], 0.0) * gate_up[:, FFE:]).astype(jnp.bfloat16)
        produced = jnp.dot(active, expert_down_weight[expert_index], preferred_element_type=jnp.float32).astype(jnp.bfloat16)
        produced = lax.optimization_barrier(produced).astype(jnp.float32)
        pair_weight = flat_weight[pair_index] * is_live
        return (mixture.at[token_index].add(produced * pair_weight[:, None]), None)
    mixture, _ = lax.scan(one_expert, jnp.zeros((TOKENS, MODEL_WIDTH), jnp.float32), jnp.arange(EXPERTS, dtype=jnp.int32))
    layer_out = (residual.astype(jnp.float32) + mixture).astype(jnp.bfloat16)
    return (layer_out, pool)
```

```python
import functools

import jax
import jax.numpy as jnp
from jax import lax
from jax.experimental import pallas as pl
from jax.experimental.pallas import tpu as pltpu
from jax.sharding import PartitionSpec as P

HEAD_SIZE = 128
PAGE = 128
CAP = 48
SPAN = 1024

eps = 1e-06
neg_fill = -1e30


def rms_norm(values, gains):
    widened = values.astype(jnp.float32)
    inv_rms = lax.rsqrt(jnp.mean(widened * widened, axis=-1, keepdims=True) + eps)
    return (widened * inv_rms * gains).astype(jnp.bfloat16)


def attention_kernel(start_ref, low_ref, q_ref, k_ref, v_ref, o_ref, bias_ref):
    start = pl.multiple_of(start_ref[0], 256)
    window = bias_ref.shape[1]
    rows = bias_ref.shape[0]

    @pl.when(pl.program_id(0) == 0)
    def _():
        key = lax.broadcasted_iota(jnp.int32, (rows, window), 1) + start
        query = lax.broadcasted_iota(jnp.int32, (rows, window), 0) + start_ref[1]
        allowed = (key >= low_ref[...]) & (key <= query)
        bias_ref[...] = jnp.where(allowed, 0.0, neg_fill)

    keys = k_ref[pl.ds(start, window), :]
    values = v_ref[pl.ds(start, window), :]
    scores = lax.dot_general(
        q_ref[...], keys, (((1,), (1,)), ((), ())), preferred_element_type=jnp.float32
    )
    scores = scores + bias_ref[...]
    row_max = jnp.max(scores, axis=1, keepdims=True)
    expd = jnp.exp((scores - row_max) * HEAD_SIZE ** (-0.5))
    total = jnp.sum(expd, axis=1, keepdims=True)
    mixed = jnp.dot(expd.astype(jnp.bfloat16), values, preferred_element_type=jnp.float32)
    o_ref[...] = (mixed / total).astype(jnp.bfloat16)


def attend(query_rows, group_kv, low, start, first):
    rows, width = query_rows.shape
    group_len, kv_cols = group_kv.shape
    n_kv = kv_cols // 2 // HEAD_SIZE
    share = width // HEAD_SIZE // n_kv
    window = min(group_len, rows + SPAN)
    heads = width // HEAD_SIZE
    return pl.pallas_call(
        attention_kernel,
        grid_spec=pltpu.PrefetchScalarGridSpec(
            num_scalar_prefetch=1,
            grid=(heads,),
            in_specs=[
                pl.BlockSpec((rows, 1), lambda h, s: (0, 0)),
                pl.BlockSpec((rows, HEAD_SIZE), lambda h, s: (0, h)),
                pl.BlockSpec((group_len, HEAD_SIZE), lambda h, s: (0, h // share)),
                pl.BlockSpec((group_len, HEAD_SIZE), lambda h, s: (0, n_kv + h // share)),
            ],
            out_specs=pl.BlockSpec((rows, HEAD_SIZE), lambda h, s: (0, h)),
            scratch_shapes=[pltpu.VMEM((rows, window), jnp.float32)],
        ),
        out_shape=jax.ShapeDtypeStruct((rows, width), jnp.bfloat16),
        cost_estimate=pl.CostEstimate(
            flops=4 * rows * window * width, bytes_accessed=4 << 20, transcendentals=rows * window * heads
        ),
        name="attention",
    )(jnp.stack([start, first]), low, query_rows, group_kv, group_kv)


def shards(
    tokens,
    lengths,
    request_adapter,
    group_page_slots,
    routes,
    attention_gain,
    query_key_value_weight,
    adapter_down_weight,
    adapter_up_weight,
    output_weight,
    expert_norm_gain,
    router,
    expert_gate_up_weight,
    expert_down_weight,
):
    tokens_per_shard, model_columns = tokens.shape
    mp_index = lax.axis_index("mp")
    group_start = mp_index * tokens_per_shard
    n_exp = router.shape[1]

    full_qkv = lax.all_gather(query_key_value_weight, "mp", axis=1, tiled=True)
    packed = jnp.concatenate([adapter_down_weight[0].T, adapter_up_weight[0]], axis=0)
    rank = adapter_up_weight.shape[1]
    adapters = lax.all_gather(packed, "dp", axis=0, tiled=False)
    adapter_total = adapters.shape[0]
    down = adapters[:, :rank].reshape(adapter_total * rank, model_columns)
    up = adapters[:, rank:].reshape(adapter_total * rank, adapter_up_weight.shape[2])
    full_out = lax.all_gather(output_weight, "mp", axis=1, tiled=True)

    seq_ends = jnp.sum(
        jnp.where(
            jnp.arange(lengths.shape[1])[:, None] <= jnp.arange(lengths.shape[1])[None, :],
            lengths[0][:, None],
            0,
        ),
        axis=0,
    )
    positions = group_start + jnp.arange(tokens_per_shard, dtype=jnp.int32)
    passed = positions[:, None] >= seq_ends[None, :]
    query_seg = jnp.sum(passed.astype(jnp.int32), axis=1)
    low = jnp.max(jnp.where(passed, seq_ends[None, :], 0), axis=1, keepdims=True)
    seq_match = query_seg[:, None] == jnp.arange(lengths.shape[1], dtype=jnp.int32)[None, :]
    token_adapter = jnp.sum(jnp.where(seq_match, request_adapter[0][None, :], 0), axis=1)

    normed = rms_norm(tokens, attention_gain)
    qkv = jnp.dot(normed, full_qkv, preferred_element_type=jnp.float32)
    query_width = up.shape[1]
    key_value = qkv[:, query_width:].astype(jnp.bfloat16)
    group_kv = lax.all_gather(key_value, "mp", axis=0, tiled=True)

    middle = lax.dot_general(
        normed, down, (((1,), (1,)), ((), ())), preferred_element_type=jnp.float32
    )
    owner = jnp.arange(adapter_total * rank, dtype=jnp.int32) // rank
    middle = jnp.where(token_adapter[:, None] == owner[None, :], middle, 0.0).astype(jnp.bfloat16)
    adapter_query = jnp.dot(middle, up, preferred_element_type=jnp.float32)
    query_rows = (qkv[:, :query_width] + adapter_query).astype(jnp.bfloat16)

    group_len = group_kv.shape[0]
    window = min(group_len, tokens_per_shard + SPAN)
    start = jnp.maximum(group_start + tokens_per_shard - window, 0)
    attended = attend(query_rows, group_kv, low, start, group_start)
    projected = jnp.dot(attended, full_out, preferred_element_type=jnp.float32)
    residual = (tokens.astype(jnp.float32) + projected).astype(jnp.bfloat16)

    pages_dev = tokens_per_shard // PAGE
    pages_grp = group_page_slots.shape[1]
    my_slots = mp_index * pages_dev + jnp.arange(pages_dev, dtype=jnp.int32)
    slot_match = (group_page_slots[0][None, :] == my_slots[:, None]).astype(jnp.int32)
    source_page = jnp.sum(slot_match * jnp.arange(pages_grp, dtype=jnp.int32)[None, :], axis=1)
    pages = group_kv.reshape(pages_grp, PAGE, group_kv.shape[1])
    pool = jnp.concatenate(
        [lax.dynamic_slice_in_dim(pages, source_page[i], 1, axis=0) for i in range(pages_dev)], axis=0
    )

    ffn_in = rms_norm(residual, expert_norm_gain)
    logits = jnp.dot(ffn_in, router, preferred_element_type=jnp.float32)
    hits = jnp.any(routes[:, :, None] == jnp.arange(n_exp, dtype=jnp.int32)[None, None, :], axis=1)
    peak = jnp.max(jnp.where(hits, logits, neg_fill), axis=1, keepdims=True)
    expl = jnp.where(hits, jnp.exp(jnp.where(hits, logits, peak) - peak), 0.0)
    route_weights = expl / jnp.sum(expl, axis=1, keepdims=True)
    before = (
        jnp.arange(tokens_per_shard)[None, :] < jnp.arange(tokens_per_shard)[:, None]
    ).astype(jnp.bfloat16)
    place = jnp.dot(before, hits.astype(jnp.bfloat16), preferred_element_type=jnp.float32)
    place = jnp.where(hits, place, -1.0).T
    chosen = place[:, None, :] == jnp.arange(CAP, dtype=jnp.int32).astype(jnp.float32)[None, :, None]
    send_map = chosen.astype(jnp.bfloat16).reshape(n_exp * CAP, tokens_per_shard)
    send_rows = jnp.dot(send_map, ffn_in, preferred_element_type=jnp.float32).astype(jnp.bfloat16)
    high = route_weights.astype(jnp.bfloat16)
    rest = (route_weights - high.astype(jnp.float32)).astype(jnp.bfloat16)
    zero = jnp.zeros((), jnp.bfloat16)
    back_high = jnp.where(chosen, high.T[:, None, :], zero).reshape(n_exp * CAP, tokens_per_shard)
    back_rest = jnp.where(chosen, rest.T[:, None, :], zero).reshape(n_exp * CAP, tokens_per_shard)

    n_dp = lax.axis_size("dp")
    exp_local = n_exp // n_dp
    outgoing = send_rows.reshape(n_dp, exp_local, CAP, model_columns)
    arrived = lax.all_to_all(outgoing, "dp", split_axis=0, concat_axis=0, tiled=True)
    gate_up = jnp.einsum(
        "secd,edf->secf", arrived, expert_gate_up_weight, preferred_element_type=jnp.float32
    )
    hidden_units = expert_down_weight.shape[1]
    active = (jnp.maximum(gate_up[..., :hidden_units], 0.0) * gate_up[..., hidden_units:]).astype(
        jnp.bfloat16
    )
    produced = jnp.einsum(
        "secf,efd->secd", active, expert_down_weight, preferred_element_type=jnp.float32
    ).astype(jnp.bfloat16)
    returned = lax.all_to_all(produced, "dp", split_axis=0, concat_axis=0, tiled=True)
    returned = returned.reshape(n_exp * CAP, model_columns)
    first_dim = (((0,), (0,)), ((), ()))
    mixture = lax.dot_general(back_high, returned, first_dim, preferred_element_type=jnp.float32)
    mixture = mixture + lax.dot_general(back_rest, returned, first_dim, preferred_element_type=jnp.float32)
    layer_out = (residual.astype(jnp.float32) + mixture).astype(jnp.bfloat16)
    return (layer_out, pool)


def solution(mesh):
    return jax.shard_map(
        shards,
        mesh=mesh,
        in_specs=(
            P(("dp", "mp"), None),
            P("dp", None),
            P("dp", None),
            P("dp", None),
            P(("dp", "mp"), None),
            P(),
            P(None, "mp"),
            P("dp", None, None),
            P("dp", None, None),
            P(None, "mp"),
            P(),
            P(),
            P("dp", None, None),
            P("dp", None, None),
        ),
        out_specs=(P(("dp", "mp"), None), P(("dp", "mp"), None, None)),
        check_vma=False,
    )
```

```python
import jax
import jax.numpy as jnp
from jax import lax
from jax.experimental import pallas as pl
from jax.experimental.pallas import tpu as pltpu
from jax.sharding import PartitionSpec as P

HEAD_SIZE = 128
PAGE = 128
CAP = 48
SPAN = 1024

eps = 1e-06
neg_fill = -1e30


def rms_norm(values, gains):
    widened = values.astype(jnp.float32)
    inv_rms = lax.rsqrt(jnp.mean(widened * widened, axis=-1, keepdims=True) + eps)
    return (widened * inv_rms * gains).astype(jnp.bfloat16)


MESH = pl.DeviceIdType.MESH


class Ring:
    def __init__(self, buf, own, send, recv):
        me = lax.axis_index("mp")
        n = lax.axis_size("mp")
        chips = n // 2
        x, core = me // 2, lax.rem(me, 2)
        self.right = lax.rem(x + 1, chips) * 2 + core
        self.left = lax.rem(x + chips - 1, chips) * 2 + core
        self.far = lax.rem(x + 2, chips) * 2 + core
        self.me = me
        self.partner = x * 2 + 1 - core
        self.buf, self.own, self.send, self.recv = buf, own, send, recv
        self.half = buf.shape[1] // 2

    def other(self, slot):
        return slot + 1 - 2 * lax.rem(slot, 2)

    def copy(self, i, slot, part, target, own=False):
        rows = pl.ds(part * self.half, self.half)
        return pltpu.make_async_remote_copy(
            src_ref=self.own.at[rows] if own else self.buf.at[slot, rows],
            dst_ref=self.buf.at[slot, rows],
            send_sem=self.send.at[i],
            recv_sem=self.recv.at[i],
            device_id={"mp": target},
            device_id_type=MESH,
        )

    def begin(self):
        me = self.me
        self.copy(0, me, 0, self.right, True).start()
        self.copy(1, me, 1, self.left, True).start()
        self.copy(2, me, 1, self.right, True).start()
        self.copy(3, me, 0, self.left, True).start()
        self.copy(4, me, 0, self.partner, True).start()
        self.copy(5, me, 1, self.partner, True).start()

    def got(self, i, slot, part):
        self.copy(i, slot, part, self.partner).wait_recv()

    def got_partner(self):
        self.got(4, self.partner, 0)
        self.got(5, self.partner, 1)

    def forward_near(self):
        self.got(0, self.left, 0)
        self.copy(6, self.left, 0, self.right).start()
        self.copy(7, self.left, 0, self.partner).start()
        self.got(1, self.right, 1)
        self.copy(8, self.right, 1, self.left).start()
        self.copy(9, self.right, 1, self.partner).start()

    def forward_rest(self):
        self.got(2, self.left, 1)
        self.copy(10, self.left, 1, self.partner).start()
        self.got(3, self.right, 0)
        self.copy(11, self.right, 0, self.partner).start()

    def got_near(self):
        self.got(7, self.other(self.left), 0)
        self.got(10, self.other(self.left), 1)
        self.got(9, self.other(self.right), 1)
        self.got(11, self.other(self.right), 0)

    def forward_far(self):
        self.got(6, self.far, 0)
        self.copy(12, self.far, 0, self.partner).start()
        self.got(8, self.far, 1)
        self.copy(13, self.far, 1, self.partner).start()

    def got_far(self):
        self.got(12, self.other(self.far), 0)
        self.got(13, self.other(self.far), 1)

    def drain(self):
        for i in range(14):
            self.copy(i, self.me, 0, self.partner, True).wait_send()


HOPS = 14


def front_kernel(
    tokens_ref,
    gain_ref,
    weight_ref,
    packed_ref,
    adapter_ref,
    low_ref,
    out_weight_ref,
    residual_ref,
    kv_ref,
    weights,
    adapters,
    out_weights,
    qkv,
    query,
    attended,
    bias,
    normed,
    middle,
    weight_send,
    weight_recv,
    kv_send,
    kv_recv,
    out_send,
    out_recv,
    adapter_send,
    adapter_recv,
    local_sem,
):
    dp, mp = lax.axis_index("dp"), lax.axis_index("mp")
    n_dp = lax.axis_size("dp")
    n_mp = lax.axis_size("mp")
    rows, columns = tokens_ref.shape
    wide = weight_ref.shape[1]
    q_blocks = qkv.shape[0] - 2
    rank = packed_ref.shape[0] // 2

    ring = Ring(weights, weight_ref, weight_send, weight_recv)
    kv_ring = Ring(kv_ref, kv_ref.at[mp], kv_send, kv_recv)
    out_ring = Ring(out_weights, out_weight_ref, out_send, out_recv)

    barrier = pltpu.get_barrier_semaphore()
    for peer in (ring.left, ring.right, ring.partner):
        pl.semaphore_signal(barrier, inc=1, device_id={"mp": peer}, device_id_type=MESH)

    @pl.loop(1, n_dp)
    def _(k):
        peer = lax.rem(dp + k, n_dp)
        pl.semaphore_signal(barrier, inc=1, device_id={"dp": peer}, device_id_type=MESH)

    pl.semaphore_wait(barrier, 3 + n_dp - 1)

    def adapter_copy(k, slot, peer):
        return pltpu.make_async_remote_copy(
            src_ref=packed_ref,
            dst_ref=adapters.at[slot],
            send_sem=adapter_send.at[k],
            recv_sem=adapter_recv.at[slot],
            device_id={"dp": peer},
            device_id_type=MESH,
        )

    ring.begin()

    @pl.loop(1, n_dp)
    def _(k):
        adapter_copy(k, dp, lax.rem(dp + k, n_dp)).start()

    own_out = pltpu.make_async_copy(out_weight_ref, out_weights.at[mp], local_sem)
    own_out.start()
    adapters[dp] = packed_ref[...]

    widened = tokens_ref[...].astype(jnp.float32)
    inv_rms = lax.rsqrt(jnp.mean(widened * widened, axis=1, keepdims=True) + eps)
    normed[...] = (widened * inv_rms * gain_ref[...]).astype(jnp.bfloat16)

    window = bias.shape[1]
    first = jnp.maximum(mp + 1 - window // rows, 0)
    key = lax.broadcasted_iota(jnp.int32, (rows, window), 1) + first * rows
    place = lax.broadcasted_iota(jnp.int32, (rows, window), 0) + mp * rows
    bias[...] = jnp.where((key >= low_ref[...]) & (key <= place), 0.0, neg_fill)

    def project(slot):
        qkv[slot] = jnp.dot(normed[...], weights[slot], preferred_element_type=jnp.float32)

    qkv[mp] = jnp.dot(normed[...], weight_ref[...], preferred_element_type=jnp.float32)
    ring.got_partner()
    project(ring.partner)
    ring.forward_near()
    ring.forward_rest()
    project(ring.left)
    project(ring.right)

    @pl.loop(1, n_dp)
    def _(k):
        source = lax.rem(dp + k, n_dp)
        adapter_copy(k, source, source).wait_recv()

    down = adapters[:, :rank, :].reshape(n_dp * rank, columns)
    mid = lax.dot_general(
        normed[...], down, (((1,), (1,)), ((), ())), preferred_element_type=jnp.float32
    )
    owner = lax.broadcasted_iota(jnp.int32, (rows, n_dp * rank), 1) // rank
    middle[...] = jnp.where(owner == adapter_ref[...], mid, 0.0).astype(jnp.bfloat16)

    ring.got_near()
    project(ring.other(ring.left))
    project(ring.other(ring.right))
    ring.forward_far()
    project(ring.far)
    ring.got_far()
    project(ring.other(ring.far))

    kv_ref[mp, :, :wide] = qkv[q_blocks].astype(jnp.bfloat16)
    kv_ref[mp, :, wide:] = qkv[q_blocks + 1].astype(jnp.bfloat16)

    def finish_query(j):
        up = adapters[:, rank:, j * wide : (j + 1) * wide].reshape(n_dp * rank, wide)
        extra = jnp.dot(middle[...], up, preferred_element_type=jnp.float32)
        query[j] = (qkv[j] + extra).astype(jnp.bfloat16)

    finish_query(0)
    kv_ring.begin()
    for j in range(1, q_blocks):
        finish_query(j)
    kv_ring.forward_near()
    out_ring.begin()
    kv_ring.got_partner()
    kv_ring.forward_rest()
    kv_ring.got_near()
    kv_ring.forward_far()
    kv_ring.got_far()

    n_kv = 2
    share = q_blocks // n_kv
    for kv_head in range(n_kv):
        k_cols = slice(kv_head * HEAD_SIZE, (kv_head + 1) * HEAD_SIZE)
        v_cols = slice(wide + kv_head * HEAD_SIZE, wide + (kv_head + 1) * HEAD_SIZE)

        @pl.loop(0, share)
        def _(step):
            block = step + kv_head * share
            for lane in range(wide // HEAD_SIZE):
                cols = slice(lane * HEAD_SIZE, (lane + 1) * HEAD_SIZE)
                keys = kv_ref[pl.ds(first, window // rows), :, k_cols].reshape(window, HEAD_SIZE)
                values = kv_ref[pl.ds(first, window // rows), :, v_cols].reshape(window, HEAD_SIZE)
                scores = lax.dot_general(
                    query[block, :, cols],
                    keys,
                    (((1,), (1,)), ((), ())),
                    preferred_element_type=jnp.float32,
                )
                scores = scores + bias[...]
                row_max = jnp.max(scores, axis=1, keepdims=True)
                expd = jnp.exp((scores - row_max) * HEAD_SIZE ** (-0.5))
                total = jnp.sum(expd, axis=1, keepdims=True)
                mixed = jnp.dot(
                    expd.astype(jnp.bfloat16), values, preferred_element_type=jnp.float32
                )
                attended[block, :, cols] = (mixed / total).astype(jnp.bfloat16)

        if kv_head == 0:
            out_ring.forward_near()

    out_ring.forward_rest()
    out_ring.got_partner()
    out_ring.got_near()
    out_ring.forward_far()
    out_ring.got_far()
    own_out.wait()

    own_rows = out_weights.shape[1]
    for lo in range(0, n_mp, 2):
        part = out_weights[lo : lo + 2].reshape(2 * own_rows, columns)
        total = tokens_ref[:, lo * own_rows : (lo + 2) * own_rows].astype(jnp.float32)
        for j in range(q_blocks):
            total += lax.dot_general(
                attended[j],
                part[:, j * wide : (j + 1) * wide],
                (((1,), (1,)), ((), ())),
                preferred_element_type=jnp.float32,
            )
        residual_ref[:, lo * own_rows : (lo + 2) * own_rows] = total.astype(jnp.bfloat16)

    ring.drain()
    kv_ring.drain()
    out_ring.drain()

    @pl.loop(1, n_dp)
    def _(k):
        adapter_copy(k, dp, lax.rem(dp + k, n_dp)).wait_send()


def front(tokens, gain, weight, packed, adapter, low, out_weight):
    n_dp, n_mp = lax.axis_size("dp"), lax.axis_size("mp")
    rows, columns = tokens.shape
    depth, wide = weight.shape
    q_blocks = columns // wide
    window = min(n_mp * rows, rows + SPAN)
    dma = pltpu.SemaphoreType.DMA
    vmem = pl.BlockSpec(memory_space=pltpu.VMEM)
    return pl.pallas_call(
        front_kernel,
        in_specs=[vmem] * 7,
        out_specs=[vmem] * 2,
        out_shape=[
            jax.ShapeDtypeStruct((rows, columns), jnp.bfloat16),
            jax.ShapeDtypeStruct((n_mp, rows, 2 * wide), jnp.bfloat16),
        ],
        scratch_shapes=[
            pltpu.VMEM((n_mp, depth, wide), jnp.bfloat16),
            pltpu.VMEM((n_dp,) + packed.shape, jnp.bfloat16),
            pltpu.VMEM((n_mp,) + out_weight.shape, jnp.bfloat16),
            pltpu.VMEM((n_mp, rows, wide), jnp.float32),
            pltpu.VMEM((q_blocks, rows, wide), jnp.bfloat16),
            pltpu.VMEM((q_blocks, rows, wide), jnp.bfloat16),
            pltpu.VMEM((rows, window), jnp.float32),
            pltpu.VMEM((rows, columns), jnp.bfloat16),
            pltpu.VMEM((rows, n_dp * packed.shape[0] // 2), jnp.bfloat16),
            dma((HOPS,)),
            dma((HOPS,)),
            dma((HOPS,)),
            dma((HOPS,)),
            dma((HOPS,)),
            dma((HOPS,)),
            dma((n_dp,)),
            dma((n_dp,)),
            dma(()),
        ],
        compiler_params=pltpu.CompilerParams(
            collective_id=0, has_side_effects=True, vmem_limit_bytes=60 << 20
        ),
        name="front",
    )(tokens, gain, weight, packed, adapter, low, out_weight)


def shards(
    tokens,
    lengths,
    request_adapter,
    group_page_slots,
    routes,
    attention_gain,
    query_key_value_weight,
    adapter_down_weight,
    adapter_up_weight,
    output_weight,
    expert_norm_gain,
    router,
    expert_gate_up_weight,
    expert_down_weight,
):
    tokens_per_shard, model_columns = tokens.shape
    mp_index = lax.axis_index("mp")
    group_start = mp_index * tokens_per_shard
    n_exp = router.shape[1]

    packed = jnp.concatenate([adapter_down_weight[0].T, adapter_up_weight[0]], axis=0)

    seq_ends = jnp.sum(
        jnp.where(
            jnp.arange(lengths.shape[1])[:, None] <= jnp.arange(lengths.shape[1])[None, :],
            lengths[0][:, None],
            0,
        ),
        axis=0,
    )
    positions = group_start + jnp.arange(tokens_per_shard, dtype=jnp.int32)
    passed = positions[:, None] >= seq_ends[None, :]
    query_seg = jnp.sum(passed.astype(jnp.int32), axis=1)
    low = jnp.max(jnp.where(passed, seq_ends[None, :], 0), axis=1, keepdims=True)
    seq_match = query_seg[:, None] == jnp.arange(lengths.shape[1], dtype=jnp.int32)[None, :]
    token_adapter = jnp.sum(jnp.where(seq_match, request_adapter[0][None, :], 0), axis=1)

    residual, group_kv = front(
        tokens,
        attention_gain[None, :],
        query_key_value_weight,
        packed,
        token_adapter[:, None],
        low,
        output_weight.T,
    )

    pages_dev = tokens_per_shard // PAGE
    pages_grp = group_page_slots.shape[1]
    my_slots = mp_index * pages_dev + jnp.arange(pages_dev, dtype=jnp.int32)
    slot_match = (group_page_slots[0][None, :] == my_slots[:, None]).astype(jnp.int32)
    source_page = jnp.sum(slot_match * jnp.arange(pages_grp, dtype=jnp.int32)[None, :], axis=1)
    pages = group_kv.reshape(pages_grp, PAGE, group_kv.shape[2])
    pool = jnp.concatenate(
        [lax.dynamic_slice_in_dim(pages, source_page[i], 1, axis=0) for i in range(pages_dev)], axis=0
    )

    ffn_in = rms_norm(residual, expert_norm_gain)
    logits = jnp.dot(ffn_in, router, preferred_element_type=jnp.float32)
    hits = jnp.any(routes[:, :, None] == jnp.arange(n_exp, dtype=jnp.int32)[None, None, :], axis=1)
    peak = jnp.max(jnp.where(hits, logits, neg_fill), axis=1, keepdims=True)
    expl = jnp.where(hits, jnp.exp(jnp.where(hits, logits, peak) - peak), 0.0)
    route_weights = expl / jnp.sum(expl, axis=1, keepdims=True)
    before = (
        jnp.arange(tokens_per_shard)[None, :] < jnp.arange(tokens_per_shard)[:, None]
    ).astype(jnp.bfloat16)
    place = jnp.dot(before, hits.astype(jnp.bfloat16), preferred_element_type=jnp.float32)
    place = jnp.where(hits, place, -1.0).T
    chosen = place[:, None, :] == jnp.arange(CAP, dtype=jnp.int32).astype(jnp.float32)[None, :, None]
    send_map = chosen.astype(jnp.bfloat16).reshape(n_exp * CAP, tokens_per_shard)
    send_rows = jnp.dot(send_map, ffn_in, preferred_element_type=jnp.float32).astype(jnp.bfloat16)
    high = route_weights.astype(jnp.bfloat16)
    rest = (route_weights - high.astype(jnp.float32)).astype(jnp.bfloat16)
    zero = jnp.zeros((), jnp.bfloat16)
    back_high = jnp.where(chosen, high.T[:, None, :], zero).reshape(n_exp * CAP, tokens_per_shard)
    back_rest = jnp.where(chosen, rest.T[:, None, :], zero).reshape(n_exp * CAP, tokens_per_shard)

    n_dp = lax.axis_size("dp")
    exp_local = n_exp // n_dp
    outgoing = send_rows.reshape(n_dp, exp_local, CAP, model_columns)
    arrived = lax.all_to_all(outgoing, "dp", split_axis=0, concat_axis=0, tiled=True)
    gate_up = jnp.einsum(
        "secd,edf->secf", arrived, expert_gate_up_weight, preferred_element_type=jnp.float32
    )
    hidden_units = expert_down_weight.shape[1]
    active = (jnp.maximum(gate_up[..., :hidden_units], 0.0) * gate_up[..., hidden_units:]).astype(
        jnp.bfloat16
    )
    produced = jnp.einsum(
        "secf,efd->secd", active, expert_down_weight, preferred_element_type=jnp.float32
    ).astype(jnp.bfloat16)
    returned = lax.all_to_all(produced, "dp", split_axis=0, concat_axis=0, tiled=True)
    returned = returned.reshape(n_exp * CAP, model_columns)
    first_dim = (((0,), (0,)), ((), ()))
    mixture = lax.dot_general(back_high, returned, first_dim, preferred_element_type=jnp.float32)
    mixture = mixture + lax.dot_general(back_rest, returned, first_dim, preferred_element_type=jnp.float32)
    layer_out = (residual.astype(jnp.float32) + mixture).astype(jnp.bfloat16)
    return (layer_out, pool)


def solution(mesh):
    return jax.shard_map(
        shards,
        mesh=mesh,
        in_specs=(
            P(("dp", "mp"), None),
            P("dp", None),
            P("dp", None),
            P("dp", None),
            P(("dp", "mp"), None),
            P(),
            P(None, "mp"),
            P("dp", None, None),
            P("dp", None, None),
            P(None, "mp"),
            P(),
            P(),
            P("dp", None, None),
            P("dp", None, None),
        ),
        out_specs=(P(("dp", "mp"), None), P(("dp", "mp"), None, None)),
        check_vma=False,
    )
```

```python
import jax
import jax.numpy as jnp
from jax import lax
from jax.experimental import pallas as pl
from jax.experimental.pallas import tpu as pltpu
from jax.sharding import PartitionSpec as P

HEAD_SIZE = 128
PAGE = 128
CAP = 48
SPAN = 1024

eps = 1e-06
neg_fill = -1e30


def rms_norm(values, gains):
    widened = values.astype(jnp.float32)
    inv_rms = lax.rsqrt(jnp.mean(widened * widened, axis=-1, keepdims=True) + eps)
    return (widened * inv_rms * gains).astype(jnp.bfloat16)


MESH = pl.DeviceIdType.MESH


class Ring:
    def __init__(self, buf, own, send, recv):
        me = lax.axis_index("mp")
        n = lax.axis_size("mp")
        chips = n // 2
        x, core = me // 2, lax.rem(me, 2)
        self.right = lax.rem(x + 1, chips) * 2 + core
        self.left = lax.rem(x + chips - 1, chips) * 2 + core
        self.far = lax.rem(x + 2, chips) * 2 + core
        self.me = me
        self.partner = x * 2 + 1 - core
        self.buf, self.own, self.send, self.recv = buf, own, send, recv
        self.half = buf.shape[1] // 2

    def other(self, slot):
        return slot + 1 - 2 * lax.rem(slot, 2)

    def copy(self, i, slot, part, target, own=False):
        rows = pl.ds(part * self.half, self.half)
        return pltpu.make_async_remote_copy(
            src_ref=self.own.at[rows] if own else self.buf.at[slot, rows],
            dst_ref=self.buf.at[slot, rows],
            send_sem=self.send.at[i],
            recv_sem=self.recv.at[i],
            device_id={"mp": target},
            device_id_type=MESH,
        )

    def begin(self):
        me = self.me
        self.copy(0, me, 0, self.right, True).start()
        self.copy(1, me, 1, self.left, True).start()
        self.copy(2, me, 1, self.right, True).start()
        self.copy(3, me, 0, self.left, True).start()
        self.copy(4, me, 0, self.partner, True).start()
        self.copy(5, me, 1, self.partner, True).start()

    def got(self, i, slot, part):
        self.copy(i, slot, part, self.partner).wait_recv()

    def got_partner(self):
        self.got(4, self.partner, 0)
        self.got(5, self.partner, 1)

    def forward_near(self):
        self.got(0, self.left, 0)
        self.copy(6, self.left, 0, self.right).start()
        self.copy(7, self.left, 0, self.partner).start()
        self.got(1, self.right, 1)
        self.copy(8, self.right, 1, self.left).start()
        self.copy(9, self.right, 1, self.partner).start()

    def forward_rest(self):
        self.got(2, self.left, 1)
        self.copy(10, self.left, 1, self.partner).start()
        self.got(3, self.right, 0)
        self.copy(11, self.right, 0, self.partner).start()

    def got_near(self):
        self.got(7, self.other(self.left), 0)
        self.got(10, self.other(self.left), 1)
        self.got(9, self.other(self.right), 1)
        self.got(11, self.other(self.right), 0)

    def forward_far(self):
        self.got(6, self.far, 0)
        self.copy(12, self.far, 0, self.partner).start()
        self.got(8, self.far, 1)
        self.copy(13, self.far, 1, self.partner).start()

    def got_far(self):
        self.got(12, self.other(self.far), 0)
        self.got(13, self.other(self.far), 1)

    def drain(self):
        for i in range(14):
            self.copy(i, self.me, 0, self.partner, True).wait_send()


HOPS = 14


def front_kernel(
    tokens_ref,
    gain_ref,
    weight_ref,
    packed_ref,
    adapter_ref,
    low_ref,
    out_weight_ref,
    residual_ref,
    kv_ref,
    weights,
    adapters,
    out_weights,
    qkv,
    query,
    attended,
    bias,
    normed,
    middle,
    weight_send,
    weight_recv,
    kv_send,
    kv_recv,
    out_send,
    out_recv,
    adapter_send,
    adapter_recv,
    local_sem,
):
    dp, mp = lax.axis_index("dp"), lax.axis_index("mp")
    n_dp = lax.axis_size("dp")
    n_mp = lax.axis_size("mp")
    rows, columns = tokens_ref.shape
    wide = weight_ref.shape[1]
    q_blocks = qkv.shape[0] - 2
    rank = packed_ref.shape[0] // 2

    ring = Ring(weights, weight_ref, weight_send, weight_recv)
    kv_ring = Ring(kv_ref, kv_ref.at[mp], kv_send, kv_recv)
    out_ring = Ring(out_weights, out_weight_ref, out_send, out_recv)

    barrier = pltpu.get_barrier_semaphore()
    for peer in (ring.left, ring.right, ring.partner):
        pl.semaphore_signal(barrier, inc=1, device_id={"mp": peer}, device_id_type=MESH)

    @pl.loop(1, n_dp)
    def _(k):
        peer = lax.rem(dp + k, n_dp)
        pl.semaphore_signal(barrier, inc=1, device_id={"dp": peer}, device_id_type=MESH)

    pl.semaphore_wait(barrier, 3 + n_dp - 1)

    def adapter_copy(k, slot, peer):
        return pltpu.make_async_remote_copy(
            src_ref=packed_ref,
            dst_ref=adapters.at[slot],
            send_sem=adapter_send.at[k],
            recv_sem=adapter_recv.at[slot],
            device_id={"dp": peer},
            device_id_type=MESH,
        )

    ring.begin()

    @pl.loop(1, n_dp)
    def _(k):
        adapter_copy(k, dp, lax.rem(dp + k, n_dp)).start()

    own_out = pltpu.make_async_copy(out_weight_ref, out_weights.at[mp], local_sem)
    own_out.start()
    adapters[dp] = packed_ref[...]

    widened = tokens_ref[...].astype(jnp.float32)
    inv_rms = lax.rsqrt(jnp.mean(widened * widened, axis=1, keepdims=True) + eps)
    normed[...] = (widened * inv_rms * gain_ref[...]).astype(jnp.bfloat16)

    window = bias.shape[1]
    first = jnp.maximum(mp + 1 - window // rows, 0)
    key = lax.broadcasted_iota(jnp.int32, (rows, window), 1) + first * rows
    place = lax.broadcasted_iota(jnp.int32, (rows, window), 0) + mp * rows
    bias[...] = jnp.where((key >= low_ref[...]) & (key <= place), 0.0, neg_fill)

    def project(slot):
        qkv[slot] = jnp.dot(normed[...], weights[slot], preferred_element_type=jnp.float32)

    qkv[mp] = jnp.dot(normed[...], weight_ref[...], preferred_element_type=jnp.float32)
    ring.got_partner()
    project(ring.partner)
    ring.forward_near()
    ring.forward_rest()
    project(ring.left)
    project(ring.right)

    @pl.loop(1, n_dp)
    def _(k):
        source = lax.rem(dp + k, n_dp)
        adapter_copy(k, source, source).wait_recv()

    down = adapters[:, :rank, :].reshape(n_dp * rank, columns)
    mid = lax.dot_general(
        normed[...], down, (((1,), (1,)), ((), ())), preferred_element_type=jnp.float32
    )
    owner = lax.broadcasted_iota(jnp.int32, (rows, n_dp * rank), 1) // rank
    middle[...] = jnp.where(owner == adapter_ref[...], mid, 0.0).astype(jnp.bfloat16)

    ring.got_near()
    project(ring.other(ring.left))
    project(ring.other(ring.right))
    ring.forward_far()
    project(ring.far)
    ring.got_far()
    project(ring.other(ring.far))

    kv_ref[mp, :, :wide] = qkv[q_blocks].astype(jnp.bfloat16)
    kv_ref[mp, :, wide:] = qkv[q_blocks + 1].astype(jnp.bfloat16)

    def finish_query(j):
        up = adapters[:, rank:, j * wide : (j + 1) * wide].reshape(n_dp * rank, wide)
        extra = jnp.dot(middle[...], up, preferred_element_type=jnp.float32)
        query[j] = (qkv[j] + extra).astype(jnp.bfloat16)

    finish_query(0)
    kv_ring.begin()
    for j in range(1, q_blocks):
        finish_query(j)
    kv_ring.forward_near()
    out_ring.begin()
    kv_ring.got_partner()
    kv_ring.forward_rest()
    kv_ring.got_near()
    kv_ring.forward_far()
    kv_ring.got_far()

    n_kv = 2
    share = q_blocks // n_kv
    for kv_head in range(n_kv):
        k_cols = slice(kv_head * HEAD_SIZE, (kv_head + 1) * HEAD_SIZE)
        v_cols = slice(wide + kv_head * HEAD_SIZE, wide + (kv_head + 1) * HEAD_SIZE)

        @pl.loop(0, share)
        def _(step):
            block = step + kv_head * share
            for lane in range(wide // HEAD_SIZE):
                cols = slice(lane * HEAD_SIZE, (lane + 1) * HEAD_SIZE)
                keys = kv_ref[pl.ds(first, window // rows), :, k_cols].reshape(window, HEAD_SIZE)
                values = kv_ref[pl.ds(first, window // rows), :, v_cols].reshape(window, HEAD_SIZE)
                scores = lax.dot_general(
                    query[block, :, cols],
                    keys,
                    (((1,), (1,)), ((), ())),
                    preferred_element_type=jnp.float32,
                )
                scores = scores + bias[...]
                row_max = jnp.max(scores, axis=1, keepdims=True)
                expd = jnp.exp((scores - row_max) * HEAD_SIZE ** (-0.5))
                total = jnp.sum(expd, axis=1, keepdims=True)
                mixed = jnp.dot(
                    expd.astype(jnp.bfloat16), values, preferred_element_type=jnp.float32
                )
                attended[block, :, cols] = (mixed / total).astype(jnp.bfloat16)

        if kv_head == 0:
            out_ring.forward_near()

    out_ring.forward_rest()
    out_ring.got_partner()
    out_ring.got_near()
    out_ring.forward_far()
    out_ring.got_far()
    own_out.wait()

    own_rows = out_weights.shape[1]
    for lo in range(0, n_mp, 2):
        part = out_weights[lo : lo + 2].reshape(2 * own_rows, columns)
        total = tokens_ref[:, lo * own_rows : (lo + 2) * own_rows].astype(jnp.float32)
        for j in range(q_blocks):
            total += lax.dot_general(
                attended[j],
                part[:, j * wide : (j + 1) * wide],
                (((1,), (1,)), ((), ())),
                preferred_element_type=jnp.float32,
            )
        residual_ref[:, lo * own_rows : (lo + 2) * own_rows] = total.astype(jnp.bfloat16)

    ring.drain()
    kv_ring.drain()
    out_ring.drain()

    @pl.loop(1, n_dp)
    def _(k):
        adapter_copy(k, dp, lax.rem(dp + k, n_dp)).wait_send()


def front(tokens, gain, weight, packed, adapter, low, out_weight):
    n_dp, n_mp = lax.axis_size("dp"), lax.axis_size("mp")
    rows, columns = tokens.shape
    depth, wide = weight.shape
    q_blocks = columns // wide
    window = min(n_mp * rows, rows + SPAN)
    dma = pltpu.SemaphoreType.DMA
    vmem = pl.BlockSpec(memory_space=pltpu.VMEM)
    return pl.pallas_call(
        front_kernel,
        in_specs=[vmem] * 7,
        out_specs=[vmem] * 2,
        out_shape=[
            jax.ShapeDtypeStruct((rows, columns), jnp.bfloat16),
            jax.ShapeDtypeStruct((n_mp, rows, 2 * wide), jnp.bfloat16),
        ],
        scratch_shapes=[
            pltpu.VMEM((n_mp, depth, wide), jnp.bfloat16),
            pltpu.VMEM((n_dp,) + packed.shape, jnp.bfloat16),
            pltpu.VMEM((n_mp,) + out_weight.shape, jnp.bfloat16),
            pltpu.VMEM((n_mp, rows, wide), jnp.float32),
            pltpu.VMEM((q_blocks, rows, wide), jnp.bfloat16),
            pltpu.VMEM((q_blocks, rows, wide), jnp.bfloat16),
            pltpu.VMEM((rows, window), jnp.float32),
            pltpu.VMEM((rows, columns), jnp.bfloat16),
            pltpu.VMEM((rows, n_dp * packed.shape[0] // 2), jnp.bfloat16),
            dma((HOPS,)),
            dma((HOPS,)),
            dma((HOPS,)),
            dma((HOPS,)),
            dma((HOPS,)),
            dma((HOPS,)),
            dma((n_dp,)),
            dma((n_dp,)),
            dma(()),
        ],
        compiler_params=pltpu.CompilerParams(
            collective_id=0, has_side_effects=True, vmem_limit_bytes=60 << 20
        ),
        name="front",
    )(tokens, gain, weight, packed, adapter, low, out_weight)


ORDER = (0, 10, 11, 9, 14, 6, 2, 8, 5, 7, 13, 15, 1, 3, 4, 12)
PIECE = 16


def expert_kernel(
    ffn_ref,
    map_ref,
    back_ref,
    rest_ref,
    residual_ref,
    up_hbm,
    down_hbm,
    out_ref,
    sent,
    arrived,
    produced,
    returned,
    up,
    down,
    active,
    back,
    total,
    go_send,
    go_recv,
    back_send,
    back_recv,
    local_sem,
):
    dp = lax.axis_index("dp")
    n_local, n_dp, cap, columns = sent.shape
    side = 4
    z, y = dp // side, lax.rem(dp, side)
    slots = n_dp * cap
    hidden = down.shape[1]
    rows = ffn_ref.shape[0]
    tile = 512

    def toward(k):
        return lax.rem(z + k // side, side) * side + lax.rem(y + k % side, side)

    def source(k):
        return (
            lax.rem(z + side - k // side, side) * side + lax.rem(y + side - k % side, side)
        )

    owners = [toward(k) for k in ORDER]

    barrier = pltpu.get_barrier_semaphore()

    @pl.loop(1, n_dp)
    def _(k):
        peer = lax.rem(dp + k, n_dp)
        pl.semaphore_signal(barrier, inc=1, device_id={"dp": peer}, device_id_type=MESH)

    up_copy = pltpu.make_async_copy(up_hbm, up, local_sem.at[0])
    down_copy = pltpu.make_async_copy(down_hbm, down, local_sem.at[1])
    up_copy.start()
    down_copy.start()

    def transfer(src, dst, send, recv, e, pos, piece, peer):
        part = pl.ds(piece * PIECE, PIECE)
        return pltpu.make_async_remote_copy(
            src_ref=src.at[e, pos, part],
            dst_ref=dst.at[e, pos, part],
            send_sem=send.at[e],
            recv_sem=recv.at[e],
            device_id={"dp": peer},
            device_id_type=MESH,
        )

    def whole(src, dst, send, recv, e):
        return pltpu.make_async_remote_copy(
            src_ref=src.at[e, 1:],
            dst_ref=dst.at[e, 1:],
            send_sem=send.at[e],
            recv_sem=recv.at[e],
            device_id={"dp": owners[1]},
            device_id_type=MESH,
        )

    def pack(e):
        pick = jnp.concatenate([map_ref[owner, e] for owner in owners], axis=0)

        @pl.loop(0, columns // tile)
        def _(j):
            cols = pl.ds(pl.multiple_of(j * tile, tile), tile)
            got = jnp.dot(pick, ffn_ref[:, cols], preferred_element_type=jnp.float32)
            sent[e, :, :, cols] = got.astype(jnp.bfloat16).reshape(n_dp, cap, tile)

    def dispatch(e):
        for piece in range(cap // PIECE):
            for pos in range(1, n_dp):
                transfer(sent, arrived, go_send, go_recv, e, pos, piece, owners[pos]).start()

    def give_back(e):
        for piece in range(cap // PIECE):
            for pos in range(1, n_dp):
                peer = source(ORDER[pos])
                transfer(produced, returned, back_send, back_recv, e, pos, piece, peer).start()

    def compute(e):
        arrived[e, 0] = sent[e, 0]

        @pl.loop(0, hidden // 256)
        def _(j):
            gate_cols = pl.ds(pl.multiple_of(j * 256, 256), 256)
            up_cols = pl.ds(pl.multiple_of(hidden + j * 256, 256), 256)
            given = arrived[e].reshape(slots, columns)
            gate = jnp.dot(given, up[e, :, gate_cols], preferred_element_type=jnp.float32)
            lift = jnp.dot(given, up[e, :, up_cols], preferred_element_type=jnp.float32)
            active[:, gate_cols] = (jnp.maximum(gate, 0.0) * lift).astype(jnp.bfloat16)

        @pl.loop(0, columns // 256)
        def _(j):
            cols = pl.ds(pl.multiple_of(j * 256, 256), 256)
            made = jnp.dot(active[...], down[e, :, cols], preferred_element_type=jnp.float32)
            produced[e, :, :, cols] = made.astype(jnp.bfloat16).reshape(n_dp, cap, 256)

        returned[e, 0] = produced[e, 0]

    def combine(e):
        @pl.loop(0, columns // tile)
        def _(j):
            cols = pl.ds(pl.multiple_of(j * tile, tile), tile)
            given = returned[e, :, :, cols].reshape(slots, tile)
            mixed = jnp.dot(back[e, 0], given, preferred_element_type=jnp.float32)
            mixed += jnp.dot(back[e, 1], given, preferred_element_type=jnp.float32)
            if e == 0:
                total[:, cols] = residual_ref[:, cols].astype(jnp.float32) + mixed
            else:
                out_ref[:, cols] = (total[:, cols] + mixed).astype(jnp.bfloat16)

    pack(0)
    pl.semaphore_wait(barrier, n_dp - 1)
    dispatch(0)
    pack(1)
    for e in range(n_local):
        for i, ref in enumerate((back_ref, rest_ref)):
            joined = jnp.concatenate([ref[owner, e] for owner in owners], axis=0)
            back[e, i] = joined.T
        if e == 0:
            dispatch(1)
    up_copy.wait()
    down_copy.wait()
    for e in range(n_local):
        whole(sent, arrived, go_send, go_recv, e).wait_recv()
        compute(e)
        give_back(e)
    for e in range(n_local):
        whole(produced, returned, back_send, back_recv, e).wait_recv()
        combine(e)
    for e in range(n_local):
        whole(sent, arrived, go_send, go_recv, e).wait_send()
        whole(produced, returned, back_send, back_recv, e).wait_send()


def experts(ffn_in, send_map, back_high, back_rest, residual, gate_up_weight, down_weight):
    rows, columns = ffn_in.shape
    n_dp = lax.axis_size("dp")
    n_local, hidden = down_weight.shape[:2]
    dma = pltpu.SemaphoreType.DMA
    vmem = pl.BlockSpec(memory_space=pltpu.VMEM)
    hbm = pl.BlockSpec(memory_space=pl.ANY)
    block = (n_local, n_dp, CAP, columns)
    maps = [m.reshape(n_dp, n_local, CAP, rows) for m in (send_map, back_high, back_rest)]
    return pl.pallas_call(
        expert_kernel,
        in_specs=[vmem] * 5 + [hbm] * 2,
        out_specs=vmem,
        out_shape=jax.ShapeDtypeStruct((rows, columns), jnp.bfloat16),
        scratch_shapes=[
            pltpu.VMEM(block, jnp.bfloat16),
            pltpu.VMEM(block, jnp.bfloat16),
            pltpu.VMEM(block, jnp.bfloat16),
            pltpu.VMEM(block, jnp.bfloat16),
            pltpu.VMEM(gate_up_weight.shape, jnp.bfloat16),
            pltpu.VMEM(down_weight.shape, jnp.bfloat16),
            pltpu.VMEM((n_dp * CAP, hidden), jnp.bfloat16),
            pltpu.VMEM((n_local, 2, rows, n_dp * CAP), jnp.bfloat16),
            pltpu.VMEM((rows, columns), jnp.float32),
            dma((n_local,)),
            dma((n_local,)),
            dma((n_local,)),
            dma((n_local,)),
            dma((2,)),
        ],
        compiler_params=pltpu.CompilerParams(
            collective_id=1, has_side_effects=True, vmem_limit_bytes=60 << 20
        ),
        name="experts",
    )(ffn_in, *maps, residual, gate_up_weight, down_weight)


def shards(
    tokens,
    lengths,
    request_adapter,
    group_page_slots,
    routes,
    attention_gain,
    query_key_value_weight,
    adapter_down_weight,
    adapter_up_weight,
    output_weight,
    expert_norm_gain,
    router,
    expert_gate_up_weight,
    expert_down_weight,
):
    tokens_per_shard, model_columns = tokens.shape
    mp_index = lax.axis_index("mp")
    group_start = mp_index * tokens_per_shard
    n_exp = router.shape[1]

    packed = jnp.concatenate([adapter_down_weight[0].T, adapter_up_weight[0]], axis=0)

    seq_ends = jnp.sum(
        jnp.where(
            jnp.arange(lengths.shape[1])[:, None] <= jnp.arange(lengths.shape[1])[None, :],
            lengths[0][:, None],
            0,
        ),
        axis=0,
    )
    positions = group_start + jnp.arange(tokens_per_shard, dtype=jnp.int32)
    passed = positions[:, None] >= seq_ends[None, :]
    query_seg = jnp.sum(passed.astype(jnp.int32), axis=1)
    low = jnp.max(jnp.where(passed, seq_ends[None, :], 0), axis=1, keepdims=True)
    seq_match = query_seg[:, None] == jnp.arange(lengths.shape[1], dtype=jnp.int32)[None, :]
    token_adapter = jnp.sum(jnp.where(seq_match, request_adapter[0][None, :], 0), axis=1)

    residual, group_kv = front(
        tokens,
        attention_gain[None, :],
        query_key_value_weight,
        packed,
        token_adapter[:, None],
        low,
        output_weight.T,
    )

    pages_dev = tokens_per_shard // PAGE
    pages_grp = group_page_slots.shape[1]
    my_slots = mp_index * pages_dev + jnp.arange(pages_dev, dtype=jnp.int32)
    slot_match = (group_page_slots[0][None, :] == my_slots[:, None]).astype(jnp.int32)
    source_page = jnp.sum(slot_match * jnp.arange(pages_grp, dtype=jnp.int32)[None, :], axis=1)
    pages = group_kv.reshape(pages_grp, PAGE, group_kv.shape[2])
    pool = jnp.concatenate(
        [lax.dynamic_slice_in_dim(pages, source_page[i], 1, axis=0) for i in range(pages_dev)], axis=0
    )

    ffn_in = rms_norm(residual, expert_norm_gain)
    logits = jnp.dot(ffn_in, router, preferred_element_type=jnp.float32)
    hits = jnp.any(routes[:, :, None] == jnp.arange(n_exp, dtype=jnp.int32)[None, None, :], axis=1)
    peak = jnp.max(jnp.where(hits, logits, neg_fill), axis=1, keepdims=True)
    expl = jnp.where(hits, jnp.exp(jnp.where(hits, logits, peak) - peak), 0.0)
    route_weights = expl / jnp.sum(expl, axis=1, keepdims=True)
    before = (
        jnp.arange(tokens_per_shard)[None, :] < jnp.arange(tokens_per_shard)[:, None]
    ).astype(jnp.bfloat16)
    place = jnp.dot(before, hits.astype(jnp.bfloat16), preferred_element_type=jnp.float32)
    place = jnp.where(hits, place, -1.0).T
    chosen = place[:, None, :] == jnp.arange(CAP, dtype=jnp.int32).astype(jnp.float32)[None, :, None]
    send_map = chosen.astype(jnp.bfloat16).reshape(n_exp * CAP, tokens_per_shard)
    high = route_weights.astype(jnp.bfloat16)
    rest = (route_weights - high.astype(jnp.float32)).astype(jnp.bfloat16)
    zero = jnp.zeros((), jnp.bfloat16)
    back_high = jnp.where(chosen, high.T[:, None, :], zero).reshape(n_exp * CAP, tokens_per_shard)
    back_rest = jnp.where(chosen, rest.T[:, None, :], zero).reshape(n_exp * CAP, tokens_per_shard)

    layer_out = experts(
        ffn_in, send_map, back_high, back_rest, residual, expert_gate_up_weight, expert_down_weight
    )
    return (layer_out, pool)


def solution(mesh):
    return jax.shard_map(
        shards,
        mesh=mesh,
        in_specs=(
            P(("dp", "mp"), None),
            P("dp", None),
            P("dp", None),
            P("dp", None),
            P(("dp", "mp"), None),
            P(),
            P(None, "mp"),
            P("dp", None, None),
            P("dp", None, None),
            P(None, "mp"),
            P(),
            P(),
            P("dp", None, None),
            P("dp", None, None),
        ),
        out_specs=(P(("dp", "mp"), None), P(("dp", "mp"), None, None)),
        check_vma=False,
    )
```

```python
import jax
import jax.numpy as jnp
from jax import lax
from jax.experimental import pallas as pl
from jax.experimental.pallas import tpu as pltpu
from jax.sharding import PartitionSpec as P

HEAD_SIZE = 128
PAGE = 128
CAP = 48
SPAN = 1024

eps = 1e-06
neg_fill = -1e30


MESH = pl.DeviceIdType.MESH


class Ring:
    def __init__(self, buf, own, send, recv):
        me = lax.axis_index("mp")
        n = lax.axis_size("mp")
        chips = n // 2
        x, core = me // 2, lax.rem(me, 2)
        self.right = lax.rem(x + 1, chips) * 2 + core
        self.left = lax.rem(x + chips - 1, chips) * 2 + core
        self.far = lax.rem(x + 2, chips) * 2 + core
        self.me = me
        self.partner = x * 2 + 1 - core
        self.buf, self.own, self.send, self.recv = buf, own, send, recv
        self.half = buf.shape[1] // 2

    def other(self, slot):
        return slot + 1 - 2 * lax.rem(slot, 2)

    def copy(self, i, slot, part, target, own=False):
        rows = pl.ds(part * self.half, self.half)
        return pltpu.make_async_remote_copy(
            src_ref=self.own.at[rows] if own else self.buf.at[slot, rows],
            dst_ref=self.buf.at[slot, rows],
            send_sem=self.send.at[i],
            recv_sem=self.recv.at[i],
            device_id={"mp": target},
            device_id_type=MESH,
        )

    def begin(self):
        me = self.me
        self.copy(0, me, 0, self.right, True).start()
        self.copy(1, me, 1, self.left, True).start()
        self.copy(2, me, 1, self.right, True).start()
        self.copy(3, me, 0, self.left, True).start()
        self.copy(4, me, 0, self.partner, True).start()
        self.copy(5, me, 1, self.partner, True).start()

    def got(self, i, slot, part):
        self.copy(i, slot, part, self.partner).wait_recv()

    def got_partner(self):
        self.got(4, self.partner, 0)
        self.got(5, self.partner, 1)

    def forward_near(self):
        self.got(0, self.left, 0)
        self.copy(6, self.left, 0, self.right).start()
        self.copy(7, self.left, 0, self.partner).start()
        self.got(1, self.right, 1)
        self.copy(8, self.right, 1, self.left).start()
        self.copy(9, self.right, 1, self.partner).start()

    def forward_rest(self):
        self.got(2, self.left, 1)
        self.copy(10, self.left, 1, self.partner).start()
        self.got(3, self.right, 0)
        self.copy(11, self.right, 0, self.partner).start()

    def got_near(self):
        self.got(7, self.other(self.left), 0)
        self.got(10, self.other(self.left), 1)
        self.got(9, self.other(self.right), 1)
        self.got(11, self.other(self.right), 0)

    def forward_far(self):
        self.got(6, self.far, 0)
        self.copy(12, self.far, 0, self.partner).start()
        self.got(8, self.far, 1)
        self.copy(13, self.far, 1, self.partner).start()

    def got_far(self):
        self.got(12, self.other(self.far), 0)
        self.got(13, self.other(self.far), 1)

    def drain(self):
        for i in range(14):
            self.copy(i, self.me, 0, self.partner, True).wait_send()


HOPS = 14


def front_kernel(
    tokens_ref,
    gain_ref,
    weight_ref,
    down_ref,
    up_ref,
    lengths_ref,
    request_ref,
    out_weight_ref,
    residual_ref,
    kv_ref,
    weights,
    adapters,
    out_weights,
    qkv,
    query,
    attended,
    bias,
    normed,
    middle,
    packed_ref,
    weight_send,
    weight_recv,
    kv_send,
    kv_recv,
    out_send,
    out_recv,
    adapter_send,
    adapter_recv,
    local_sem,
):
    dp, mp = lax.axis_index("dp"), lax.axis_index("mp")
    n_dp = lax.axis_size("dp")
    n_mp = lax.axis_size("mp")
    rows, columns = tokens_ref.shape
    wide = weight_ref.shape[1]
    q_blocks = qkv.shape[0] - 2
    rank = up_ref.shape[1]

    ring = Ring(weights, weight_ref, weight_send, weight_recv)
    kv_ring = Ring(kv_ref, kv_ref.at[mp], kv_send, kv_recv)
    out_ring = Ring(out_weights, out_weight_ref, out_send, out_recv)

    barrier = pltpu.get_barrier_semaphore()
    for peer in (ring.left, ring.right, ring.partner):
        pl.semaphore_signal(barrier, inc=1, device_id={"mp": peer}, device_id_type=MESH)

    @pl.loop(1, n_dp)
    def _(k):
        peer = lax.rem(dp + k, n_dp)
        pl.semaphore_signal(barrier, inc=1, device_id={"dp": peer}, device_id_type=MESH)

    pl.semaphore_wait(barrier, 3 + n_dp - 1)

    def adapter_copy(k, slot, peer):
        return pltpu.make_async_remote_copy(
            src_ref=packed_ref,
            dst_ref=adapters.at[slot],
            send_sem=adapter_send.at[k],
            recv_sem=adapter_recv.at[slot],
            device_id={"dp": peer},
            device_id_type=MESH,
        )

    ring.begin()

    packed_ref[rank:, :] = up_ref[0]
    packed_ref[:rank, :] = down_ref[0].astype(jnp.float32).T.astype(jnp.bfloat16)

    own_out = pltpu.make_async_copy(out_weight_ref, out_weights.at[mp], local_sem)
    own_out.start()

    widened = tokens_ref[...].astype(jnp.float32)
    inv_rms = lax.rsqrt(jnp.mean(widened * widened, axis=1, keepdims=True) + eps)
    normed[...] = (widened * inv_rms * gain_ref[...][None, :]).astype(jnp.bfloat16)

    @pl.loop(1, n_dp)
    def _(k):
        adapter_copy(k, dp, lax.rem(dp + k, n_dp)).start()

    adapters[dp] = packed_ref[...]

    place = lax.broadcasted_iota(jnp.int32, (rows, 1), 0) + mp * rows
    low = jnp.zeros((rows, 1), jnp.int32)
    adapter = jnp.zeros((rows, 1), jnp.int32) + request_ref[:, 0:1]
    ends = jnp.zeros((1, 1), jnp.int32)
    for r in range(1, lengths_ref.shape[1]):
        ends = ends + lengths_ref[:, r - 1 : r]
        passed = place >= ends
        low = jnp.where(passed, ends, low)
        adapter = jnp.where(passed, request_ref[:, r : r + 1], adapter)

    window = bias.shape[1]
    first = jnp.maximum(mp + 1 - window // rows, 0)
    key = lax.broadcasted_iota(jnp.int32, (rows, window), 1) + first * rows
    bias[...] = jnp.where((key >= low) & (key <= place), 0.0, neg_fill)

    def project(slot):
        qkv[slot] = jnp.dot(normed[...], weights[slot], preferred_element_type=jnp.float32)

    qkv[mp] = jnp.dot(normed[...], weight_ref[...], preferred_element_type=jnp.float32)
    ring.got_partner()
    project(ring.partner)
    ring.forward_near()
    ring.forward_rest()
    project(ring.left)
    project(ring.right)

    @pl.loop(1, n_dp)
    def _(k):
        source = lax.rem(dp + k, n_dp)
        adapter_copy(k, source, source).wait_recv()

    down = adapters[:, :rank, :].reshape(n_dp * rank, columns)
    mid = lax.dot_general(
        normed[...], down, (((1,), (1,)), ((), ())), preferred_element_type=jnp.float32
    )
    owner = lax.broadcasted_iota(jnp.int32, (rows, n_dp * rank), 1) // rank
    middle[...] = jnp.where(owner == adapter, mid, 0.0).astype(jnp.bfloat16)

    ring.got_near()
    project(ring.other(ring.left))
    project(ring.other(ring.right))
    ring.forward_far()
    project(ring.far)
    ring.got_far()
    project(ring.other(ring.far))

    kv_ref[mp, :, :wide] = qkv[q_blocks].astype(jnp.bfloat16)
    kv_ref[mp, :, wide:] = qkv[q_blocks + 1].astype(jnp.bfloat16)

    def finish_query(j):
        up = adapters[:, rank:, j * wide : (j + 1) * wide].reshape(n_dp * rank, wide)
        extra = jnp.dot(middle[...], up, preferred_element_type=jnp.float32)
        query[j] = (qkv[j] + extra).astype(jnp.bfloat16)

    finish_query(0)
    kv_ring.begin()
    for j in range(1, q_blocks):
        finish_query(j)
    kv_ring.forward_near()
    out_ring.begin()
    kv_ring.got_partner()
    kv_ring.forward_rest()
    kv_ring.got_near()
    kv_ring.forward_far()
    kv_ring.got_far()

    n_kv = 2
    share = q_blocks // n_kv
    for kv_head in range(n_kv):
        k_cols = slice(kv_head * HEAD_SIZE, (kv_head + 1) * HEAD_SIZE)
        v_cols = slice(wide + kv_head * HEAD_SIZE, wide + (kv_head + 1) * HEAD_SIZE)

        @pl.loop(0, share)
        def _(step):
            block = step + kv_head * share
            for lane in range(wide // HEAD_SIZE):
                cols = slice(lane * HEAD_SIZE, (lane + 1) * HEAD_SIZE)
                keys = kv_ref[pl.ds(first, window // rows), :, k_cols].reshape(window, HEAD_SIZE)
                values = kv_ref[pl.ds(first, window // rows), :, v_cols].reshape(window, HEAD_SIZE)
                scores = lax.dot_general(
                    query[block, :, cols],
                    keys,
                    (((1,), (1,)), ((), ())),
                    preferred_element_type=jnp.float32,
                )
                scores = scores + bias[...]
                row_max = jnp.max(scores, axis=1, keepdims=True)
                expd = jnp.exp((scores - row_max) * HEAD_SIZE ** (-0.5))
                total = jnp.sum(expd, axis=1, keepdims=True)
                mixed = jnp.dot(
                    expd.astype(jnp.bfloat16), values, preferred_element_type=jnp.float32
                )
                attended[block, :, cols] = (mixed / total).astype(jnp.bfloat16)

        if kv_head == 0:
            out_ring.forward_near()

    out_ring.forward_rest()
    out_ring.got_partner()
    out_ring.got_near()
    out_ring.forward_far()
    out_ring.got_far()
    own_out.wait()

    own_rows = out_weights.shape[1]
    for lo in range(0, n_mp, 2):
        part = out_weights[lo : lo + 2].reshape(2 * own_rows, columns)
        total = tokens_ref[:, lo * own_rows : (lo + 2) * own_rows].astype(jnp.float32)
        for j in range(q_blocks):
            total += lax.dot_general(
                attended[j],
                part[:, j * wide : (j + 1) * wide],
                (((1,), (1,)), ((), ())),
                preferred_element_type=jnp.float32,
            )
        residual_ref[:, lo * own_rows : (lo + 2) * own_rows] = total.astype(jnp.bfloat16)

    ring.drain()
    kv_ring.drain()
    out_ring.drain()

    @pl.loop(1, n_dp)
    def _(k):
        adapter_copy(k, dp, lax.rem(dp + k, n_dp)).wait_send()


def front(tokens, gain, weight, down, up, lengths, request, out_weight):
    n_dp, n_mp = lax.axis_size("dp"), lax.axis_size("mp")
    rows, columns = tokens.shape
    depth, wide = weight.shape
    q_blocks = columns // wide
    rank = up.shape[1]
    window = min(n_mp * rows, rows + SPAN)
    dma = pltpu.SemaphoreType.DMA
    vmem = pl.BlockSpec(memory_space=pltpu.VMEM)
    return pl.pallas_call(
        front_kernel,
        in_specs=[vmem] * 8,
        out_specs=[vmem] * 2,
        out_shape=[
            jax.ShapeDtypeStruct((rows, columns), jnp.bfloat16),
            jax.ShapeDtypeStruct((n_mp, rows, 2 * wide), jnp.bfloat16),
        ],
        scratch_shapes=[
            pltpu.VMEM((n_mp, depth, wide), jnp.bfloat16),
            pltpu.VMEM((n_dp, 2 * rank, columns), jnp.bfloat16),
            pltpu.VMEM((n_mp,) + out_weight.shape, jnp.bfloat16),
            pltpu.VMEM((n_mp, rows, wide), jnp.float32),
            pltpu.VMEM((q_blocks, rows, wide), jnp.bfloat16),
            pltpu.VMEM((q_blocks, rows, wide), jnp.bfloat16),
            pltpu.VMEM((rows, window), jnp.float32),
            pltpu.VMEM((rows, columns), jnp.bfloat16),
            pltpu.VMEM((rows, n_dp * rank), jnp.bfloat16),
            pltpu.VMEM((2 * rank, columns), jnp.bfloat16),
            dma((HOPS,)),
            dma((HOPS,)),
            dma((HOPS,)),
            dma((HOPS,)),
            dma((HOPS,)),
            dma((HOPS,)),
            dma((n_dp,)),
            dma((n_dp,)),
            dma(()),
        ],
        compiler_params=pltpu.CompilerParams(
            collective_id=0, has_side_effects=True, vmem_limit_bytes=60 << 20
        ),
        name="front",
    )(tokens, gain, weight, down, up, lengths, request, out_weight)


ORDER = (0, 10, 11, 9, 14, 6, 2, 8, 5, 7, 13, 15, 1, 3, 4, 12)
PIECE = 16


def expert_kernel(
    residual_ref,
    gain_ref,
    router_ref,
    routes_ref,
    page_slots_ref,
    kv_hbm,
    up_hbm,
    down_hbm,
    out_ref,
    pool_ref,
    sent,
    arrived,
    produced,
    returned,
    up,
    down,
    active,
    back,
    total,
    ffn_ref,
    pages,
    flat,
    places,
    high,
    rest,
    go_send,
    go_recv,
    back_send,
    back_recv,
    local_sem,
):
    dp = lax.axis_index("dp")
    n_local, n_dp, cap, columns = sent.shape
    side = 4
    z, y = dp // side, lax.rem(dp, side)
    slots = n_dp * cap
    hidden = down.shape[1]
    rows = ffn_ref.shape[0]
    n_exp = n_local * n_dp
    tile = 512

    def toward(k):
        return lax.rem(z + k // side, side) * side + lax.rem(y + k % side, side)

    def source(k):
        return (
            lax.rem(z + side - k // side, side) * side + lax.rem(y + side - k % side, side)
        )

    owners = [toward(k) for k in ORDER]

    barrier = pltpu.get_barrier_semaphore()

    @pl.loop(1, n_dp)
    def _(k):
        peer = lax.rem(dp + k, n_dp)
        pl.semaphore_signal(barrier, inc=1, device_id={"dp": peer}, device_id_type=MESH)

    up_copy = pltpu.make_async_copy(up_hbm, up, local_sem.at[0])
    down_copy = pltpu.make_async_copy(down_hbm, down, local_sem.at[1])
    kv_copy = pltpu.make_async_copy(kv_hbm, pages, local_sem.at[2])
    up_copy.start()
    down_copy.start()
    kv_copy.start()

    def flip(values):
        flat[:, : values.shape[1]] = values
        return flat[...].T[: values.shape[1]]

    def spread(table, e):
        return [
            jnp.broadcast_to(table[pl.ds(owner * n_local + e, 1), :], (cap, rows))
            for owner in owners
        ]

    count = lax.broadcasted_iota(jnp.int32, (cap, rows), 0).astype(jnp.float32)
    flat[...] = jnp.zeros_like(flat)
    wanted = flip(routes_ref[...].astype(jnp.float32))
    named = lax.broadcasted_iota(jnp.int32, (n_exp, rows), 0).astype(jnp.float32)
    hits = wanted[0:1] == named
    for k in range(1, routes_ref.shape[1]):
        hits = hits | (wanted[k : k + 1] == named)
    early = lax.broadcasted_iota(jnp.int32, (rows, rows), 0)
    late = lax.broadcasted_iota(jnp.int32, (rows, rows), 1)
    before = jnp.where(early < late, 1.0, 0.0).astype(jnp.bfloat16)
    marks = jnp.where(hits, 1.0, 0.0)
    ranks = jnp.dot(marks.astype(jnp.bfloat16), before, preferred_element_type=jnp.float32)
    places[...] = jnp.where(hits, ranks, -1.0)

    widened = residual_ref[...].astype(jnp.float32)
    inv_rms = lax.rsqrt(jnp.mean(widened * widened, axis=1, keepdims=True) + eps)
    ffn_ref[...] = (widened * inv_rms * gain_ref[...][None, :]).astype(jnp.bfloat16)

    def transfer(src, dst, send, recv, e, pos, piece, peer):
        part = pl.ds(piece * PIECE, PIECE)
        return pltpu.make_async_remote_copy(
            src_ref=src.at[e, pos, part],
            dst_ref=dst.at[e, pos, part],
            send_sem=send.at[e],
            recv_sem=recv.at[e],
            device_id={"dp": peer},
            device_id_type=MESH,
        )

    def whole(src, dst, send, recv, e):
        return pltpu.make_async_remote_copy(
            src_ref=src.at[e, 1:],
            dst_ref=dst.at[e, 1:],
            send_sem=send.at[e],
            recv_sem=recv.at[e],
            device_id={"dp": owners[1]},
            device_id_type=MESH,
        )

    def pack(e):
        pick = jnp.concatenate(
            [jnp.where(row == count, 1.0, 0.0).astype(jnp.bfloat16) for row in spread(places, e)],
            axis=0,
        )

        @pl.loop(0, columns // tile)
        def _(j):
            cols = pl.ds(pl.multiple_of(j * tile, tile), tile)
            got = jnp.dot(pick, ffn_ref[:, cols], preferred_element_type=jnp.float32)
            sent[e, :, :, cols] = got.astype(jnp.bfloat16).reshape(n_dp, cap, tile)

    def dispatch(e):
        for piece in range(cap // PIECE):
            for pos in range(1, n_dp):
                transfer(sent, arrived, go_send, go_recv, e, pos, piece, owners[pos]).start()

    def give_back(e):
        for piece in range(cap // PIECE):
            for pos in range(1, n_dp):
                peer = source(ORDER[pos])
                transfer(produced, returned, back_send, back_recv, e, pos, piece, peer).start()

    def compute(e):
        arrived[e, 0] = sent[e, 0]

        @pl.loop(0, hidden // 256)
        def _(j):
            gate_cols = pl.ds(pl.multiple_of(j * 256, 256), 256)
            up_cols = pl.ds(pl.multiple_of(hidden + j * 256, 256), 256)
            given = arrived[e].reshape(slots, columns)
            gate = jnp.dot(given, up[e, :, gate_cols], preferred_element_type=jnp.float32)
            lift = jnp.dot(given, up[e, :, up_cols], preferred_element_type=jnp.float32)
            active[:, gate_cols] = (jnp.maximum(gate, 0.0) * lift).astype(jnp.bfloat16)

        @pl.loop(0, columns // 256)
        def _(j):
            cols = pl.ds(pl.multiple_of(j * 256, 256), 256)
            made = jnp.dot(active[...], down[e, :, cols], preferred_element_type=jnp.float32)
            produced[e, :, :, cols] = made.astype(jnp.bfloat16).reshape(n_dp, cap, 256)

        returned[e, 0] = produced[e, 0]

    def combine(e):
        @pl.loop(0, columns // tile)
        def _(j):
            cols = pl.ds(pl.multiple_of(j * tile, tile), tile)
            given = returned[e, :, :, cols].reshape(slots, tile)
            mixed = jnp.dot(back[e, 0], given, preferred_element_type=jnp.float32)
            mixed += jnp.dot(back[e, 1], given, preferred_element_type=jnp.float32)
            if e == 0:
                total[:, cols] = residual_ref[:, cols].astype(jnp.float32) + mixed
            else:
                out_ref[:, cols] = (total[:, cols] + mixed).astype(jnp.bfloat16)

    pack(0)
    pl.semaphore_wait(barrier, n_dp - 1)
    dispatch(0)
    pack(1)
    logits = flip(jnp.dot(ffn_ref[...], router_ref[...], preferred_element_type=jnp.float32))
    dispatch(1)
    peak = jnp.max(jnp.where(hits, logits, neg_fill), axis=0, keepdims=True)
    expl = jnp.where(hits, jnp.exp(jnp.where(hits, logits, peak) - peak), 0.0)
    shares = expl / jnp.sum(expl, axis=0, keepdims=True)
    high[...] = shares.astype(jnp.bfloat16).astype(jnp.float32)
    rest[...] = shares - high[...]
    for e in range(n_local):
        chosen = [row == count for row in spread(places, e)]
        for i, table in enumerate((high, rest)):
            joined = jnp.concatenate(
                [jnp.where(c, row, 0.0) for c, row in zip(chosen, spread(table, e))], axis=0
            )
            back[e, i] = joined.T.astype(jnp.bfloat16)

    kv_copy.wait()
    held = pool_ref.shape[0]
    for i in range(held):
        mine = lax.axis_index("mp") * held + i

        def pick_page(p, page):
            here = page_slots_ref[pl.ds(p, 1), 0:1] == mine
            return jnp.where(here, pages[p].astype(jnp.float32), page)

        page = lax.fori_loop(
            0, pages.shape[0], pick_page, jnp.zeros(pages.shape[1:], jnp.float32)
        )
        pool_ref[i] = page.astype(jnp.bfloat16)

    up_copy.wait()
    down_copy.wait()
    for e in range(n_local):
        whole(sent, arrived, go_send, go_recv, e).wait_recv()
        compute(e)
        give_back(e)
    for e in range(n_local):
        whole(produced, returned, back_send, back_recv, e).wait_recv()
        combine(e)
    for e in range(n_local):
        whole(sent, arrived, go_send, go_recv, e).wait_send()
        whole(produced, returned, back_send, back_recv, e).wait_send()


def experts(
    residual, gain, router, routes, page_slots, group_kv, held, gate_up_weight, down_weight
):
    rows, columns = residual.shape
    n_dp = lax.axis_size("dp")
    n_local, hidden = down_weight.shape[:2]
    n_exp = router.shape[1]
    dma = pltpu.SemaphoreType.DMA
    vmem = pl.BlockSpec(memory_space=pltpu.VMEM)
    hbm = pl.BlockSpec(memory_space=pl.ANY)
    block = (n_local, n_dp, CAP, columns)
    return pl.pallas_call(
        expert_kernel,
        in_specs=[vmem] * 5 + [hbm] * 3,
        out_specs=[vmem] * 2,
        out_shape=[
            jax.ShapeDtypeStruct((rows, columns), jnp.bfloat16),
            jax.ShapeDtypeStruct((held,) + group_kv.shape[1:], jnp.bfloat16),
        ],
        scratch_shapes=[
            pltpu.VMEM(block, jnp.bfloat16),
            pltpu.VMEM(block, jnp.bfloat16),
            pltpu.VMEM(block, jnp.bfloat16),
            pltpu.VMEM(block, jnp.bfloat16),
            pltpu.VMEM(gate_up_weight.shape, jnp.bfloat16),
            pltpu.VMEM(down_weight.shape, jnp.bfloat16),
            pltpu.VMEM((n_dp * CAP, hidden), jnp.bfloat16),
            pltpu.VMEM((n_local, 2, rows, n_dp * CAP), jnp.bfloat16),
            pltpu.VMEM((rows, columns), jnp.float32),
            pltpu.VMEM((rows, columns), jnp.bfloat16),
            pltpu.VMEM(group_kv.shape, jnp.bfloat16),
            pltpu.VMEM((rows, 128), jnp.float32),
            pltpu.VMEM((n_exp, rows), jnp.float32),
            pltpu.VMEM((n_exp, rows), jnp.float32),
            pltpu.VMEM((n_exp, rows), jnp.float32),
            dma((n_local,)),
            dma((n_local,)),
            dma((n_local,)),
            dma((n_local,)),
            dma((3,)),
        ],
        compiler_params=pltpu.CompilerParams(
            collective_id=1, has_side_effects=True, vmem_limit_bytes=60 << 20
        ),
        name="experts",
    )(residual, gain, router, routes, page_slots, group_kv, gate_up_weight, down_weight)


def shards(
    tokens,
    lengths,
    request_adapter,
    group_page_slots,
    routes,
    attention_gain,
    query_key_value_weight,
    adapter_down_weight,
    adapter_up_weight,
    output_weight,
    expert_norm_gain,
    router,
    expert_gate_up_weight,
    expert_down_weight,
):
    residual, group_kv = front(
        tokens,
        attention_gain,
        query_key_value_weight,
        adapter_down_weight,
        adapter_up_weight,
        lengths,
        request_adapter,
        output_weight.T,
    )
    pages_grp = group_page_slots.shape[1]
    layer_out, pool = experts(
        residual,
        expert_norm_gain,
        router,
        routes,
        group_page_slots.reshape(pages_grp, 1),
        group_kv.reshape(pages_grp, PAGE, group_kv.shape[2]),
        tokens.shape[0] // PAGE,
        expert_gate_up_weight,
        expert_down_weight,
    )
    return (layer_out, pool)


def solution(mesh):
    return jax.shard_map(
        shards,
        mesh=mesh,
        in_specs=(
            P(("dp", "mp"), None),
            P("dp", None),
            P("dp", None),
            P("dp", None),
            P(("dp", "mp"), None),
            P(),
            P(None, "mp"),
            P("dp", None, None),
            P("dp", None, None),
            P(None, "mp"),
            P(),
            P(),
            P("dp", None, None),
            P("dp", None, None),
        ),
        out_specs=(P(("dp", "mp"), None), P(("dp", "mp"), None, None)),
        check_vma=False,
    )
```

```python
import jax
import jax.numpy as jnp
from jax import lax
from jax.experimental import pallas as pl
from jax.experimental.pallas import tpu as pltpu
from jax.sharding import PartitionSpec as P

HEAD_SIZE = 128
PAGE = 128
CAP = 48
SPAN = 1024

eps = 1e-06
neg_fill = -1e30


MESH = pl.DeviceIdType.MESH


class Ring:
    def __init__(self, buf, own, send, recv, span):
        me = lax.axis_index("mp")
        n = lax.axis_size("mp")
        chips = n // 2
        x, core = me // 2, lax.rem(me, 2)
        self.right = lax.rem(x + 1, chips) * 2 + core
        self.left = lax.rem(x + chips - 1, chips) * 2 + core
        self.far = lax.rem(x + 2, chips) * 2 + core
        self.me = me
        self.partner = x * 2 + 1 - core
        self.buf, self.own, self.send, self.recv = buf, own, send, recv
        self.half = span // 2

    def other(self, slot):
        return slot + 1 - 2 * lax.rem(slot, 2)

    def copy(self, i, slot, part, target, own=False):
        rows = pl.ds(part * self.half, self.half)
        return pltpu.make_async_remote_copy(
            src_ref=self.own.at[rows] if own else self.buf.at[slot, rows],
            dst_ref=self.buf.at[slot, rows],
            send_sem=self.send.at[i],
            recv_sem=self.recv.at[i],
            device_id={"mp": target},
            device_id_type=MESH,
        )

    def begin(self):
        me = self.me
        self.copy(0, me, 0, self.right, True).start()
        self.copy(1, me, 1, self.left, True).start()
        self.copy(2, me, 1, self.right, True).start()
        self.copy(3, me, 0, self.left, True).start()
        self.copy(4, me, 0, self.partner, True).start()
        self.copy(5, me, 1, self.partner, True).start()

    def got(self, i, slot, part):
        self.copy(i, slot, part, self.partner).wait_recv()

    def got_partner(self):
        self.got(4, self.partner, 0)
        self.got(5, self.partner, 1)

    def forward_near(self):
        self.got(0, self.left, 0)
        self.copy(6, self.left, 0, self.right).start()
        self.copy(7, self.left, 0, self.partner).start()
        self.got(1, self.right, 1)
        self.copy(8, self.right, 1, self.left).start()
        self.copy(9, self.right, 1, self.partner).start()

    def forward_rest(self):
        self.got(2, self.left, 1)
        self.copy(10, self.left, 1, self.partner).start()
        self.got(3, self.right, 0)
        self.copy(11, self.right, 0, self.partner).start()

    def got_near(self):
        self.got(7, self.other(self.left), 0)
        self.got(10, self.other(self.left), 1)
        self.got(9, self.other(self.right), 1)
        self.got(11, self.other(self.right), 0)

    def forward_far(self):
        self.got(6, self.far, 0)
        self.copy(12, self.far, 0, self.partner).start()
        self.got(8, self.far, 1)
        self.copy(13, self.far, 1, self.partner).start()

    def got_far(self):
        self.got(12, self.other(self.far), 0)
        self.got(13, self.other(self.far), 1)

    def drain(self):
        for i in range(14):
            self.copy(i, self.me, 0, self.partner, True).wait_send()


HOPS = 14
SIDE = 4


class Spread:
    def __init__(self, ring, buf, own, base, send, recv):
        dp = lax.axis_index("dp")
        self.index = (dp // SIDE, lax.rem(dp, SIDE))
        self.ring, self.buf, self.own, self.base = ring, buf, own, base
        self.chunk = (buf.shape[1] - base) // SIDE
        self.wide = buf.shape[2] // 2
        self.send, self.recv = send, recv
        self.slots = (ring.left, ring.right, ring.far)

    def piece(self, ref, part, index):
        rows = pl.ds(self.base + index * self.chunk, self.chunk)
        return ref.at[rows, pl.ds(part * self.wide, self.wide)]

    def across(self, i, slot, part, target, own=False):
        index = self.index[part]
        return pltpu.make_async_remote_copy(
            src_ref=self.piece(self.own if own else self.buf.at[slot], part, index),
            dst_ref=self.piece(self.buf.at[slot], part, index),
            send_sem=self.send.at[i],
            recv_sem=self.recv.at[i],
            device_id={"mp": target},
            device_id_type=MESH,
        )

    def along(self, s, part, d, back=False):
        z, y = self.index
        step = SIDE - d if back else d
        peer = (
            lax.rem(z + step, SIDE) * SIDE + y if part == 0 else z * SIDE + lax.rem(y + step, SIDE)
        )
        index = lax.rem(self.index[part] + step, SIDE) if back else self.index[part]
        ref = self.piece(self.buf.at[self.slots[s]], part, index)
        i = 6 + (s * 2 + part) * 3 + d - 1
        return pltpu.make_async_remote_copy(
            src_ref=ref,
            dst_ref=ref,
            send_sem=self.send.at[i],
            recv_sem=self.recv.at[i],
            device_id={"dp": peer},
            device_id_type=MESH,
        )

    def hand(self, i, slot, own=False):
        rows = pl.ds(self.base, SIDE * self.chunk)
        return pltpu.make_async_remote_copy(
            src_ref=self.own.at[rows] if own else self.buf.at[slot, rows],
            dst_ref=self.buf.at[slot, rows],
            send_sem=self.send.at[i],
            recv_sem=self.recv.at[i],
            device_id={"mp": self.ring.partner},
            device_id_type=MESH,
        )

    def begin(self):
        ring = self.ring
        self.across(0, ring.me, 0, ring.right, True).start()
        self.across(1, ring.me, 1, ring.left, True).start()
        self.across(2, ring.me, 1, ring.right, True).start()
        self.across(3, ring.me, 0, ring.left, True).start()
        self.hand(27, ring.me, True).start()

    def push(self, s, part):
        for d in (2, 1, 3):
            self.along(s, part, d).start()

    def near(self):
        ring = self.ring
        self.across(0, ring.left, 0, ring.right).wait_recv()
        self.across(4, ring.left, 0, ring.right).start()
        self.push(0, 0)
        self.across(1, ring.right, 1, ring.left).wait_recv()
        self.across(5, ring.right, 1, ring.left).start()
        self.push(1, 1)
        self.across(2, ring.left, 1, ring.right).wait_recv()
        self.push(0, 1)
        self.across(3, ring.right, 0, ring.left).wait_recv()
        self.push(1, 0)

    def distant(self):
        ring = self.ring
        self.across(4, ring.far, 0, ring.right).wait_recv()
        self.push(2, 0)
        self.across(5, ring.far, 1, ring.left).wait_recv()
        self.push(2, 1)

    def finish(self, s):
        for part in (0, 1):
            for d in (1, 2, 3):
                self.along(s, part, d, True).wait_recv()
        self.hand(24 + s, self.slots[s]).start()

    def got(self, s):
        self.hand(24 + s, self.ring.other(self.slots[s])).wait_recv()

    def got_partner(self):
        self.hand(27, self.ring.partner).wait_recv()

    def drain(self):
        ring = self.ring
        for i in range(6):
            self.across(i, ring.me, (0, 1, 1, 0, 0, 1)[i], ring.right, True).wait_send()
        for s in range(3):
            for part in (0, 1):
                for d in (1, 2, 3):
                    self.along(s, part, d).wait_send()
            self.hand(24 + s, self.slots[s]).wait_send()
        self.hand(27, ring.me, True).wait_send()


PASSES = 28


def front_kernel(
    tokens_ref,
    gain_ref,
    weight_ref,
    down_ref,
    up_ref,
    lengths_ref,
    request_ref,
    out_weight_ref,
    residual_ref,
    kv_ref,
    weights,
    adapters,
    out_weights,
    qkv,
    query,
    attended,
    bias,
    normed,
    middle,
    packed_ref,
    weight_send,
    weight_recv,
    low_send,
    low_recv,
    kv_send,
    kv_recv,
    out_send,
    out_recv,
    adapter_send,
    adapter_recv,
    pair_sem,
    local_sem,
):
    dp, mp = lax.axis_index("dp"), lax.axis_index("mp")
    n_dp = lax.axis_size("dp")
    n_mp = lax.axis_size("mp")
    rows, columns = tokens_ref.shape
    wide = weight_ref.shape[1]
    q_blocks = qkv.shape[0] - 2
    rank = up_ref.shape[1]

    depth = weight_ref.shape[0]
    core = lax.rem(mp, 2)
    ring = Ring(weights, weight_ref, weight_send, weight_recv, depth // 2)
    low_rows = Spread(ring, weights, weight_ref, depth // 2, low_send, low_recv)
    kv_ring = Ring(kv_ref, kv_ref.at[mp], kv_send, kv_recv, rows)
    out_rows = Spread(ring, out_weights, out_weight_ref, 0, out_send, out_recv)

    barrier = pltpu.get_barrier_semaphore()
    for peer in (ring.left, ring.right, ring.partner):
        pl.semaphore_signal(barrier, inc=1, device_id={"mp": peer}, device_id_type=MESH)

    @pl.loop(1, n_dp)
    def _(k):
        peer = lax.rem(dp + k, n_dp)
        pl.semaphore_signal(barrier, inc=1, device_id={"dp": peer}, device_id_type=MESH)

    pl.semaphore_wait(barrier, 3 + n_dp - 1)

    def adapter_copy(k, slot, peer):
        return pltpu.make_async_remote_copy(
            src_ref=packed_ref.at[core],
            dst_ref=adapters.at[core, slot],
            send_sem=adapter_send.at[k],
            recv_sem=adapter_recv.at[slot],
            device_id={"dp": peer},
            device_id_type=MESH,
        )

    def adapter_pair(kind):
        return pltpu.make_async_remote_copy(
            src_ref=adapters.at[kind],
            dst_ref=adapters.at[kind],
            send_sem=pair_sem.at[0],
            recv_sem=pair_sem.at[1],
            device_id={"mp": ring.partner},
            device_id_type=MESH,
        )

    low_rows.begin()
    ring.begin()

    packed_ref[0] = down_ref[0]
    packed_ref[1] = up_ref[0]
    own_out = pltpu.make_async_copy(out_weight_ref, out_weights.at[mp], local_sem)
    own_out.start()

    widened = tokens_ref[...].astype(jnp.float32)
    inv_rms = lax.rsqrt(jnp.mean(widened * widened, axis=1, keepdims=True) + eps)
    normed[...] = (widened * inv_rms * gain_ref[...][None, :]).astype(jnp.bfloat16)
    adapters[core, dp] = packed_ref[core]

    low_rows.near()

    @pl.loop(1, n_dp)
    def _(k):
        adapter_copy(k, dp, lax.rem(dp + k, n_dp)).start()

    place = lax.broadcasted_iota(jnp.int32, (rows, 1), 0) + mp * rows
    low = jnp.zeros((rows, 1), jnp.int32)
    adapter = jnp.zeros((rows, 1), jnp.int32) + request_ref[:, 0:1]
    ends = jnp.zeros((1, 1), jnp.int32)
    for r in range(1, lengths_ref.shape[1]):
        ends = ends + lengths_ref[:, r - 1 : r]
        passed = place >= ends
        low = jnp.where(passed, ends, low)
        adapter = jnp.where(passed, request_ref[:, r : r + 1], adapter)

    window = bias.shape[1]
    first = jnp.maximum(mp + 1 - window // rows, 0)
    key = lax.broadcasted_iota(jnp.int32, (rows, window), 1) + first * rows
    bias[...] = jnp.where((key >= low) & (key <= place), 0.0, neg_fill)

    def project(slot):
        qkv[slot] = jnp.dot(normed[...], weights[slot], preferred_element_type=jnp.float32)

    qkv[mp] = jnp.dot(normed[...], weight_ref[...], preferred_element_type=jnp.float32)
    low_rows.distant()
    ring.forward_near()
    ring.got_partner()
    low_rows.got_partner()
    project(ring.partner)
    low_rows.finish(0)
    low_rows.finish(1)
    ring.forward_rest()
    project(ring.left)
    project(ring.right)
    low_rows.finish(2)
    ring.forward_far()
    out_rows.begin()
    project(ring.far)
    ring.got_near()
    low_rows.got(0)
    low_rows.got(1)
    project(ring.other(ring.left))
    project(ring.other(ring.right))
    ring.got_far()
    low_rows.got(2)
    project(ring.other(ring.far))

    kv_ref[mp, :, :wide] = qkv[q_blocks].astype(jnp.bfloat16)
    kv_ref[mp, :, wide:] = qkv[q_blocks + 1].astype(jnp.bfloat16)

    @pl.loop(1, n_dp)
    def _(k):
        source = lax.rem(dp + k, n_dp)
        adapter_copy(k, source, source).wait_recv()

    adapter_pair(core).start()
    kv_ring.begin()
    adapter_pair(1 - core).wait_recv()

    down = adapters[0].reshape(n_dp * rank, columns)
    mid = lax.dot_general(
        normed[...], down, (((1,), (1,)), ((), ())), preferred_element_type=jnp.float32
    )
    owner = lax.broadcasted_iota(jnp.int32, (rows, n_dp * rank), 1) // rank
    middle[...] = jnp.where(owner == adapter, mid, 0.0).astype(jnp.bfloat16)

    def finish_query(j):
        up = adapters[1, :, :, j * wide : (j + 1) * wide].reshape(n_dp * rank, wide)
        extra = jnp.dot(middle[...], up, preferred_element_type=jnp.float32)
        query[j] = (qkv[j] + extra).astype(jnp.bfloat16)

    finish_query(0)
    finish_query(1)
    out_rows.near()
    kv_ring.forward_near()
    for j in range(2, q_blocks):
        finish_query(j)
    kv_ring.got_partner()
    kv_ring.forward_rest()
    out_rows.distant()
    kv_ring.got_near()
    kv_ring.forward_far()
    kv_ring.got_far()

    n_kv = 2
    share = q_blocks // n_kv
    for kv_head in range(n_kv):
        k_cols = slice(kv_head * HEAD_SIZE, (kv_head + 1) * HEAD_SIZE)
        v_cols = slice(wide + kv_head * HEAD_SIZE, wide + (kv_head + 1) * HEAD_SIZE)

        @pl.loop(0, share)
        def _(step):
            block = step + kv_head * share
            for lane in range(wide // HEAD_SIZE):
                cols = slice(lane * HEAD_SIZE, (lane + 1) * HEAD_SIZE)
                keys = kv_ref[pl.ds(first, window // rows), :, k_cols].reshape(window, HEAD_SIZE)
                values = kv_ref[pl.ds(first, window // rows), :, v_cols].reshape(window, HEAD_SIZE)
                scores = lax.dot_general(
                    query[block, :, cols],
                    keys,
                    (((1,), (1,)), ((), ())),
                    preferred_element_type=jnp.float32,
                )
                scores = scores + bias[...]
                row_max = jnp.max(scores, axis=1, keepdims=True)
                expd = jnp.exp((scores - row_max) * HEAD_SIZE ** (-0.5))
                total = jnp.sum(expd, axis=1, keepdims=True)
                mixed = jnp.dot(
                    expd.astype(jnp.bfloat16), values, preferred_element_type=jnp.float32
                )
                attended[block, :, cols] = (mixed / total).astype(jnp.bfloat16)

        if kv_head == 0:
            out_rows.finish(0)
            out_rows.finish(1)

    out_rows.finish(2)
    out_rows.got_partner()
    for s in range(3):
        out_rows.got(s)
    own_out.wait()

    own_rows = out_weights.shape[1]
    for lo in range(0, n_mp, 2):
        part = out_weights[lo : lo + 2].reshape(2 * own_rows, columns)
        total = tokens_ref[:, lo * own_rows : (lo + 2) * own_rows].astype(jnp.float32)
        for j in range(q_blocks):
            total += lax.dot_general(
                attended[j],
                part[:, j * wide : (j + 1) * wide],
                (((1,), (1,)), ((), ())),
                preferred_element_type=jnp.float32,
            )
        residual_ref[:, lo * own_rows : (lo + 2) * own_rows] = total.astype(jnp.bfloat16)

    ring.drain()
    kv_ring.drain()
    out_rows.drain()
    low_rows.drain()
    adapter_pair(core).wait_send()

    @pl.loop(1, n_dp)
    def _(k):
        adapter_copy(k, dp, lax.rem(dp + k, n_dp)).wait_send()


def front(tokens, gain, weight, down, up, lengths, request, out_weight):
    n_dp, n_mp = lax.axis_size("dp"), lax.axis_size("mp")
    rows, columns = tokens.shape
    depth, wide = weight.shape
    q_blocks = columns // wide
    rank = up.shape[1]
    window = min(n_mp * rows, rows + SPAN)
    dma = pltpu.SemaphoreType.DMA
    vmem = pl.BlockSpec(memory_space=pltpu.VMEM)
    return pl.pallas_call(
        front_kernel,
        in_specs=[vmem] * 8,
        out_specs=[vmem] * 2,
        out_shape=[
            jax.ShapeDtypeStruct((rows, columns), jnp.bfloat16),
            jax.ShapeDtypeStruct((n_mp, rows, 2 * wide), jnp.bfloat16),
        ],
        scratch_shapes=[
            pltpu.VMEM((n_mp, depth, wide), jnp.bfloat16),
            pltpu.VMEM((2, n_dp, rank, columns), jnp.bfloat16),
            pltpu.VMEM((n_mp,) + out_weight.shape, jnp.bfloat16),
            pltpu.VMEM((n_mp, rows, wide), jnp.float32),
            pltpu.VMEM((q_blocks, rows, wide), jnp.bfloat16),
            pltpu.VMEM((q_blocks, rows, wide), jnp.bfloat16),
            pltpu.VMEM((rows, window), jnp.float32),
            pltpu.VMEM((rows, columns), jnp.bfloat16),
            pltpu.VMEM((rows, n_dp * rank), jnp.bfloat16),
            pltpu.VMEM((2, rank, columns), jnp.bfloat16),
            dma((HOPS,)),
            dma((HOPS,)),
            dma((PASSES,)),
            dma((PASSES,)),
            dma((HOPS,)),
            dma((HOPS,)),
            dma((PASSES,)),
            dma((PASSES,)),
            dma((n_dp,)),
            dma((n_dp,)),
            dma((2,)),
            dma(()),
        ],
        compiler_params=pltpu.CompilerParams(
            collective_id=0, has_side_effects=True, vmem_limit_bytes=60 << 20
        ),
        name="front",
    )(tokens, gain, weight, down, up, lengths, request, out_weight)


ORDER = (0, 10, 11, 9, 14, 6, 2, 8, 5, 7, 13, 15, 1, 3, 4, 12)
PIECE = 16


def expert_kernel(
    residual_ref,
    gain_ref,
    router_ref,
    routes_ref,
    page_slots_ref,
    kv_hbm,
    up_hbm,
    down_hbm,
    out_ref,
    pool_ref,
    sent,
    arrived,
    produced,
    returned,
    up,
    down,
    active,
    back,
    total,
    ffn_ref,
    pages,
    places,
    high,
    rest,
    go_send,
    go_recv,
    back_send,
    back_recv,
    local_sem,
):
    dp = lax.axis_index("dp")
    n_local, n_dp, cap, columns = sent.shape
    side = 4
    z, y = dp // side, lax.rem(dp, side)
    slots = n_dp * cap
    hidden = down.shape[1]
    rows = ffn_ref.shape[0]
    n_exp = n_local * n_dp
    tile = 512

    def toward(k):
        return lax.rem(z + k // side, side) * side + lax.rem(y + k % side, side)

    def source(k):
        return (
            lax.rem(z + side - k // side, side) * side + lax.rem(y + side - k % side, side)
        )

    owners = [toward(k) for k in ORDER]

    barrier = pltpu.get_barrier_semaphore()

    @pl.loop(1, n_dp)
    def _(k):
        peer = lax.rem(dp + k, n_dp)
        pl.semaphore_signal(barrier, inc=1, device_id={"dp": peer}, device_id_type=MESH)

    up_copy = pltpu.make_async_copy(up_hbm, up, local_sem.at[0])
    down_copy = pltpu.make_async_copy(down_hbm, down, local_sem.at[1])
    kv_copy = pltpu.make_async_copy(kv_hbm, pages, local_sem.at[2])
    up_copy.start()
    down_copy.start()
    kv_copy.start()

    def spread(table, e):
        return [
            jnp.broadcast_to(table[pl.ds(owner * n_local + e, 1), :], (cap, rows))
            for owner in owners
        ]

    count = lax.broadcasted_iota(jnp.int32, (cap, rows), 0).astype(jnp.float32)
    wanted = routes_ref[...]
    named = lax.broadcasted_iota(jnp.int32, (n_exp, rows), 0)
    hits = wanted[0:1] == named
    for k in range(1, routes_ref.shape[0]):
        hits = hits | (wanted[k : k + 1] == named)
    early = lax.broadcasted_iota(jnp.int32, (rows, rows), 0)
    late = lax.broadcasted_iota(jnp.int32, (rows, rows), 1)
    before = jnp.where(early < late, 1.0, 0.0).astype(jnp.bfloat16)
    marks = jnp.where(hits, 1.0, 0.0)
    ranks = jnp.dot(marks.astype(jnp.bfloat16), before, preferred_element_type=jnp.float32)
    places[...] = jnp.where(hits, ranks, -1.0)

    widened = residual_ref[...].astype(jnp.float32)
    inv_rms = lax.rsqrt(jnp.mean(widened * widened, axis=1, keepdims=True) + eps)
    ffn_ref[...] = (widened * inv_rms * gain_ref[...][None, :]).astype(jnp.bfloat16)

    def transfer(src, dst, send, recv, e, pos, piece, peer):
        part = pl.ds(piece * PIECE, PIECE)
        return pltpu.make_async_remote_copy(
            src_ref=src.at[e, pos, part],
            dst_ref=dst.at[e, pos, part],
            send_sem=send.at[e],
            recv_sem=recv.at[e],
            device_id={"dp": peer},
            device_id_type=MESH,
        )

    def whole(src, dst, send, recv, e):
        return pltpu.make_async_remote_copy(
            src_ref=src.at[e, 1:],
            dst_ref=dst.at[e, 1:],
            send_sem=send.at[e],
            recv_sem=recv.at[e],
            device_id={"dp": owners[1]},
            device_id_type=MESH,
        )

    def pack(e):
        pick = jnp.concatenate(
            [jnp.where(row == count, 1.0, 0.0).astype(jnp.bfloat16) for row in spread(places, e)],
            axis=0,
        )

        @pl.loop(0, columns // tile)
        def _(j):
            cols = pl.ds(pl.multiple_of(j * tile, tile), tile)
            got = jnp.dot(pick, ffn_ref[:, cols], preferred_element_type=jnp.float32)
            sent[e, :, :, cols] = got.astype(jnp.bfloat16).reshape(n_dp, cap, tile)

    def dispatch(e):
        for piece in range(cap // PIECE):
            for pos in range(1, n_dp):
                transfer(sent, arrived, go_send, go_recv, e, pos, piece, owners[pos]).start()

    def give_back(e):
        for piece in range(cap // PIECE):
            for pos in range(1, n_dp):
                peer = source(ORDER[pos])
                transfer(produced, returned, back_send, back_recv, e, pos, piece, peer).start()

    def compute(e):
        arrived[e, 0] = sent[e, 0]

        @pl.loop(0, hidden // 256)
        def _(j):
            gate_cols = pl.ds(pl.multiple_of(j * 256, 256), 256)
            up_cols = pl.ds(pl.multiple_of(hidden + j * 256, 256), 256)
            given = arrived[e].reshape(slots, columns)
            gate = jnp.dot(given, up[e, :, gate_cols], preferred_element_type=jnp.float32)
            lift = jnp.dot(given, up[e, :, up_cols], preferred_element_type=jnp.float32)
            active[:, gate_cols] = (jnp.maximum(gate, 0.0) * lift).astype(jnp.bfloat16)

        @pl.loop(0, columns // 256)
        def _(j):
            cols = pl.ds(pl.multiple_of(j * 256, 256), 256)
            made = jnp.dot(active[...], down[e, :, cols], preferred_element_type=jnp.float32)
            produced[e, :, :, cols] = made.astype(jnp.bfloat16).reshape(n_dp, cap, 256)

        returned[e, 0] = produced[e, 0]

    def combine(e):
        @pl.loop(0, columns // tile)
        def _(j):
            cols = pl.ds(pl.multiple_of(j * tile, tile), tile)
            given = returned[e, :, :, cols].reshape(slots, tile)
            mixed = jnp.dot(back[e, 0], given, preferred_element_type=jnp.float32)
            mixed += jnp.dot(back[e, 1], given, preferred_element_type=jnp.float32)
            if e == 0:
                total[:, cols] = residual_ref[:, cols].astype(jnp.float32) + mixed
            else:
                out_ref[:, cols] = (total[:, cols] + mixed).astype(jnp.bfloat16)

    pack(0)
    pl.semaphore_wait(barrier, n_dp - 1)
    dispatch(0)
    pack(1)
    logits = lax.dot_general(
        router_ref[...], ffn_ref[...], (((1,), (1,)), ((), ())), preferred_element_type=jnp.float32
    )
    dispatch(1)
    peak = jnp.max(jnp.where(hits, logits, neg_fill), axis=0, keepdims=True)
    expl = jnp.where(hits, jnp.exp(jnp.where(hits, logits, peak) - peak), 0.0)
    shares = expl / jnp.sum(expl, axis=0, keepdims=True)
    high[...] = shares.astype(jnp.bfloat16).astype(jnp.float32)
    rest[...] = shares - high[...]
    for e in range(n_local):
        chosen = [row == count for row in spread(places, e)]
        for i, table in enumerate((high, rest)):
            joined = jnp.concatenate(
                [jnp.where(c, row, 0.0) for c, row in zip(chosen, spread(table, e))], axis=0
            )
            back[e, i] = joined.T.astype(jnp.bfloat16)

    kv_copy.wait()
    held = pool_ref.shape[0]
    order = lax.broadcasted_iota(jnp.int32, page_slots_ref.shape, 1)
    for i in range(held):
        mine = lax.axis_index("mp") * held + i

        def pick_page(p, page):
            slot = jnp.sum(jnp.where(order == p, page_slots_ref[...], 0), axis=1, keepdims=True)
            here = slot == mine
            return jnp.where(here, pages[p].astype(jnp.float32), page)

        page = lax.fori_loop(
            0, pages.shape[0], pick_page, jnp.zeros(pages.shape[1:], jnp.float32)
        )
        pool_ref[i] = page.astype(jnp.bfloat16)

    up_copy.wait()
    down_copy.wait()
    for e in range(n_local):
        whole(sent, arrived, go_send, go_recv, e).wait_recv()
        compute(e)
        give_back(e)
    for e in range(n_local):
        whole(produced, returned, back_send, back_recv, e).wait_recv()
        combine(e)
    for e in range(n_local):
        whole(sent, arrived, go_send, go_recv, e).wait_send()
        whole(produced, returned, back_send, back_recv, e).wait_send()


def experts(
    residual, gain, router, routes, page_slots, group_kv, held, gate_up_weight, down_weight
):
    rows, columns = residual.shape
    n_dp = lax.axis_size("dp")
    n_local, hidden = down_weight.shape[:2]
    n_exp = router.shape[0]
    dma = pltpu.SemaphoreType.DMA
    vmem = pl.BlockSpec(memory_space=pltpu.VMEM)
    hbm = pl.BlockSpec(memory_space=pl.ANY)
    block = (n_local, n_dp, CAP, columns)
    return pl.pallas_call(
        expert_kernel,
        in_specs=[vmem] * 5 + [hbm] * 3,
        out_specs=[vmem] * 2,
        out_shape=[
            jax.ShapeDtypeStruct((rows, columns), jnp.bfloat16),
            jax.ShapeDtypeStruct((held,) + group_kv.shape[1:], jnp.bfloat16),
        ],
        scratch_shapes=[
            pltpu.VMEM(block, jnp.bfloat16),
            pltpu.VMEM(block, jnp.bfloat16),
            pltpu.VMEM(block, jnp.bfloat16),
            pltpu.VMEM(block, jnp.bfloat16),
            pltpu.VMEM(gate_up_weight.shape, jnp.bfloat16),
            pltpu.VMEM(down_weight.shape, jnp.bfloat16),
            pltpu.VMEM((n_dp * CAP, hidden), jnp.bfloat16),
            pltpu.VMEM((n_local, 2, rows, n_dp * CAP), jnp.bfloat16),
            pltpu.VMEM((rows, columns), jnp.float32),
            pltpu.VMEM((rows, columns), jnp.bfloat16),
            pltpu.VMEM(group_kv.shape, jnp.bfloat16),
            pltpu.VMEM((n_exp, rows), jnp.float32),
            pltpu.VMEM((n_exp, rows), jnp.float32),
            pltpu.VMEM((n_exp, rows), jnp.float32),
            dma((n_local,)),
            dma((n_local,)),
            dma((n_local,)),
            dma((n_local,)),
            dma((3,)),
        ],
        compiler_params=pltpu.CompilerParams(
            collective_id=1, has_side_effects=True, vmem_limit_bytes=60 << 20
        ),
        name="experts",
    )(residual, gain, router, routes, page_slots, group_kv, gate_up_weight, down_weight)


def shards(
    tokens,
    lengths,
    request_adapter,
    group_page_slots,
    routes,
    attention_gain,
    query_key_value_weight,
    adapter_down_weight,
    adapter_up_weight,
    output_weight,
    expert_norm_gain,
    router,
    expert_gate_up_weight,
    expert_down_weight,
):
    residual, group_kv = front(
        tokens,
        attention_gain,
        query_key_value_weight,
        adapter_down_weight.transpose(0, 2, 1),
        adapter_up_weight,
        lengths,
        request_adapter,
        output_weight.T,
    )
    pages_grp = group_page_slots.shape[1]
    layer_out, pool = experts(
        residual,
        expert_norm_gain,
        router.T,
        routes.T,
        group_page_slots,
        group_kv.reshape(pages_grp, PAGE, group_kv.shape[2]),
        tokens.shape[0] // PAGE,
        expert_gate_up_weight,
        expert_down_weight,
    )
    return (layer_out, pool)


def solution(mesh):
    return jax.shard_map(
        shards,
        mesh=mesh,
        in_specs=(
            P(("dp", "mp"), None),
            P("dp", None),
            P("dp", None),
            P("dp", None),
            P(("dp", "mp"), None),
            P(),
            P(None, "mp"),
            P("dp", None, None),
            P("dp", None, None),
            P(None, "mp"),
            P(),
            P(),
            P("dp", None, None),
            P("dp", None, None),
        ),
        out_specs=(P(("dp", "mp"), None), P(("dp", "mp"), None, None)),
        check_vma=False,
    )
```

```python
import jax
import jax.numpy as jnp
from jax import lax
from jax.experimental import pallas as pl
from jax.experimental.pallas import tpu as pltpu
from jax.sharding import PartitionSpec as P

HEAD_SIZE = 128
PAGE = 128
CAP = 48
SPAN = 1024

eps = 1e-06
neg_fill = -1e30


MESH = pl.DeviceIdType.MESH


class Ring:
    def __init__(self, buf, own, send, recv, span):
        me = lax.axis_index("mp")
        n = lax.axis_size("mp")
        chips = n // 2
        x, core = me // 2, lax.rem(me, 2)
        self.right = lax.rem(x + 1, chips) * 2 + core
        self.left = lax.rem(x + chips - 1, chips) * 2 + core
        self.far = lax.rem(x + 2, chips) * 2 + core
        self.me = me
        self.partner = x * 2 + 1 - core
        self.buf, self.own, self.send, self.recv = buf, own, send, recv
        self.half = span // 2

    def other(self, slot):
        return slot + 1 - 2 * lax.rem(slot, 2)

    def copy(self, i, slot, part, target, own=False):
        rows = pl.ds(part * self.half, self.half)
        return pltpu.make_async_remote_copy(
            src_ref=self.own.at[rows] if own else self.buf.at[slot, rows],
            dst_ref=self.buf.at[slot, rows],
            send_sem=self.send.at[i],
            recv_sem=self.recv.at[i],
            device_id={"mp": target},
            device_id_type=MESH,
        )

    def begin(self):
        me = self.me
        self.copy(0, me, 0, self.right, True).start()
        self.copy(1, me, 1, self.left, True).start()
        self.copy(2, me, 1, self.right, True).start()
        self.copy(3, me, 0, self.left, True).start()
        self.copy(4, me, 0, self.partner, True).start()
        self.copy(5, me, 1, self.partner, True).start()

    def got(self, i, slot, part):
        self.copy(i, slot, part, self.partner).wait_recv()

    def got_partner(self):
        self.got(4, self.partner, 0)
        self.got(5, self.partner, 1)

    def forward_near(self):
        self.got(0, self.left, 0)
        self.copy(6, self.left, 0, self.right).start()
        self.copy(7, self.left, 0, self.partner).start()
        self.got(1, self.right, 1)
        self.copy(8, self.right, 1, self.left).start()
        self.copy(9, self.right, 1, self.partner).start()

    def forward_rest(self):
        self.got(2, self.left, 1)
        self.copy(10, self.left, 1, self.partner).start()
        self.got(3, self.right, 0)
        self.copy(11, self.right, 0, self.partner).start()

    def got_near(self):
        self.got(7, self.other(self.left), 0)
        self.got(10, self.other(self.left), 1)
        self.got(9, self.other(self.right), 1)
        self.got(11, self.other(self.right), 0)

    def forward_far(self):
        self.got(6, self.far, 0)
        self.copy(12, self.far, 0, self.partner).start()
        self.got(8, self.far, 1)
        self.copy(13, self.far, 1, self.partner).start()

    def got_far(self):
        self.got(12, self.other(self.far), 0)
        self.got(13, self.other(self.far), 1)

    def drain(self):
        for i in range(14):
            self.copy(i, self.me, 0, self.partner, True).wait_send()


HOPS = 14
SIDE = 4


class Spread:
    def __init__(self, ring, buf, own, base, send, recv):
        dp = lax.axis_index("dp")
        self.index = (dp // SIDE, lax.rem(dp, SIDE))
        self.ring, self.buf, self.own, self.base = ring, buf, own, base
        self.chunk = (buf.shape[1] - base) // SIDE
        self.wide = buf.shape[2] // 2
        self.send, self.recv = send, recv
        self.slots = (ring.left, ring.right, ring.far)

    def piece(self, ref, part, index):
        rows = pl.ds(self.base + index * self.chunk, self.chunk)
        return ref.at[rows, pl.ds(part * self.wide, self.wide)]

    def across(self, i, slot, part, target, own=False):
        index = self.index[part]
        return pltpu.make_async_remote_copy(
            src_ref=self.piece(self.own if own else self.buf.at[slot], part, index),
            dst_ref=self.piece(self.buf.at[slot], part, index),
            send_sem=self.send.at[i],
            recv_sem=self.recv.at[i],
            device_id={"mp": target},
            device_id_type=MESH,
        )

    def along(self, s, part, d, back=False):
        z, y = self.index
        step = SIDE - d if back else d
        peer = (
            lax.rem(z + step, SIDE) * SIDE + y if part == 0 else z * SIDE + lax.rem(y + step, SIDE)
        )
        index = lax.rem(self.index[part] + step, SIDE) if back else self.index[part]
        ref = self.piece(self.buf.at[self.slots[s]], part, index)
        i = 6 + (s * 2 + part) * 3 + d - 1
        return pltpu.make_async_remote_copy(
            src_ref=ref,
            dst_ref=ref,
            send_sem=self.send.at[i],
            recv_sem=self.recv.at[i],
            device_id={"dp": peer},
            device_id_type=MESH,
        )

    def hand(self, i, slot, own=False):
        rows = pl.ds(self.base, SIDE * self.chunk)
        return pltpu.make_async_remote_copy(
            src_ref=self.own.at[rows] if own else self.buf.at[slot, rows],
            dst_ref=self.buf.at[slot, rows],
            send_sem=self.send.at[i],
            recv_sem=self.recv.at[i],
            device_id={"mp": self.ring.partner},
            device_id_type=MESH,
        )

    def begin(self):
        ring = self.ring
        self.across(0, ring.me, 0, ring.right, True).start()
        self.across(1, ring.me, 1, ring.left, True).start()
        self.across(2, ring.me, 1, ring.right, True).start()
        self.across(3, ring.me, 0, ring.left, True).start()
        self.hand(27, ring.me, True).start()

    def push(self, s, part):
        for d in (2, 1, 3):
            self.along(s, part, d).start()

    def near(self):
        ring = self.ring
        self.across(0, ring.left, 0, ring.right).wait_recv()
        self.across(4, ring.left, 0, ring.right).start()
        self.push(0, 0)
        self.across(1, ring.right, 1, ring.left).wait_recv()
        self.across(5, ring.right, 1, ring.left).start()
        self.push(1, 1)
        self.across(2, ring.left, 1, ring.right).wait_recv()
        self.push(0, 1)
        self.across(3, ring.right, 0, ring.left).wait_recv()
        self.push(1, 0)

    def distant(self):
        ring = self.ring
        self.across(4, ring.far, 0, ring.right).wait_recv()
        self.push(2, 0)
        self.across(5, ring.far, 1, ring.left).wait_recv()
        self.push(2, 1)

    def finish(self, s):
        for part in (0, 1):
            for d in (1, 2, 3):
                self.along(s, part, d, True).wait_recv()
        self.hand(24 + s, self.slots[s]).start()

    def got(self, s):
        self.hand(24 + s, self.ring.other(self.slots[s])).wait_recv()

    def got_partner(self):
        self.hand(27, self.ring.partner).wait_recv()

    def drain(self):
        ring = self.ring
        for i in range(6):
            self.across(i, ring.me, (0, 1, 1, 0, 0, 1)[i], ring.right, True).wait_send()
        for s in range(3):
            for part in (0, 1):
                for d in (1, 2, 3):
                    self.along(s, part, d).wait_send()
            self.hand(24 + s, self.slots[s]).wait_send()
        self.hand(27, ring.me, True).wait_send()


PASSES = 28


def front_kernel(
    tokens_ref,
    gain_ref,
    weight_ref,
    down_ref,
    up_ref,
    lengths_ref,
    request_ref,
    out_weight_ref,
    residual_ref,
    kv_ref,
    weights,
    adapters,
    out_weights,
    qkv,
    query,
    attended,
    bias,
    normed,
    middle,
    packed_ref,
    weight_send,
    weight_recv,
    low_send,
    low_recv,
    kv_send,
    kv_recv,
    out_send,
    out_recv,
    adapter_send,
    adapter_recv,
    pair_sem,
    local_sem,
):
    dp, mp = lax.axis_index("dp"), lax.axis_index("mp")
    n_dp = lax.axis_size("dp")
    n_mp = lax.axis_size("mp")
    rows, columns = tokens_ref.shape
    wide = weight_ref.shape[1]
    q_blocks = qkv.shape[0] - 2
    rank = up_ref.shape[1]

    depth = weight_ref.shape[0]
    core = lax.rem(mp, 2)
    ring = Ring(weights, weight_ref, weight_send, weight_recv, depth // 2)
    low_rows = Spread(ring, weights, weight_ref, depth // 2, low_send, low_recv)
    kv_ring = Ring(kv_ref, kv_ref.at[mp], kv_send, kv_recv, rows)
    out_rows = Spread(ring, out_weights, out_weight_ref, 0, out_send, out_recv)

    barrier = pltpu.get_barrier_semaphore()
    for peer in (ring.left, ring.right, ring.partner):
        pl.semaphore_signal(barrier, inc=1, device_id={"mp": peer}, device_id_type=MESH)

    @pl.loop(1, n_dp)
    def _(k):
        peer = lax.rem(dp + k, n_dp)
        pl.semaphore_signal(barrier, inc=1, device_id={"dp": peer}, device_id_type=MESH)

    pl.semaphore_wait(barrier, 3 + n_dp - 1)

    def adapter_copy(k, slot, peer):
        return pltpu.make_async_remote_copy(
            src_ref=packed_ref.at[core],
            dst_ref=adapters.at[core, slot],
            send_sem=adapter_send.at[k],
            recv_sem=adapter_recv.at[slot],
            device_id={"dp": peer},
            device_id_type=MESH,
        )

    def adapter_pair(kind):
        return pltpu.make_async_remote_copy(
            src_ref=adapters.at[kind],
            dst_ref=adapters.at[kind],
            send_sem=pair_sem.at[0],
            recv_sem=pair_sem.at[1],
            device_id={"mp": ring.partner},
            device_id_type=MESH,
        )

    low_rows.begin()
    ring.begin()

    packed_ref[0] = down_ref[0]
    packed_ref[1] = up_ref[0]
    own_out = pltpu.make_async_copy(out_weight_ref, out_weights.at[mp], local_sem)
    own_out.start()

    widened = tokens_ref[...].astype(jnp.float32)
    inv_rms = lax.rsqrt(jnp.mean(widened * widened, axis=1, keepdims=True) + eps)
    normed[...] = (widened * inv_rms * gain_ref[...][None, :]).astype(jnp.bfloat16)
    adapters[core, dp] = packed_ref[core]

    low_rows.near()

    @pl.loop(1, n_dp)
    def _(k):
        adapter_copy(k, dp, lax.rem(dp + k, n_dp)).start()

    place = lax.broadcasted_iota(jnp.int32, (rows, 1), 0) + mp * rows
    low = jnp.zeros((rows, 1), jnp.int32)
    adapter = jnp.zeros((rows, 1), jnp.int32) + request_ref[:, 0:1]
    ends = jnp.zeros((1, 1), jnp.int32)
    for r in range(1, lengths_ref.shape[1]):
        ends = ends + lengths_ref[:, r - 1 : r]
        passed = place >= ends
        low = jnp.where(passed, ends, low)
        adapter = jnp.where(passed, request_ref[:, r : r + 1], adapter)

    window = bias.shape[1]
    first = jnp.maximum(mp + 1 - window // rows, 0)
    key = lax.broadcasted_iota(jnp.int32, (rows, window), 1) + first * rows
    bias[...] = jnp.where((key >= low) & (key <= place), 0.0, neg_fill)

    def project(slot):
        qkv[slot] = jnp.dot(normed[...], weights[slot], preferred_element_type=jnp.float32)

    qkv[mp] = jnp.dot(normed[...], weight_ref[...], preferred_element_type=jnp.float32)
    low_rows.distant()
    ring.forward_near()
    ring.got_partner()
    low_rows.got_partner()
    project(ring.partner)
    low_rows.finish(0)
    low_rows.finish(1)
    ring.forward_rest()
    project(ring.left)
    project(ring.right)
    low_rows.finish(2)
    ring.forward_far()
    out_rows.begin()
    project(ring.far)
    ring.got_near()
    low_rows.got(0)
    low_rows.got(1)
    project(ring.other(ring.left))
    project(ring.other(ring.right))
    ring.got_far()
    low_rows.got(2)
    project(ring.other(ring.far))

    kv_ref[mp, :, :wide] = qkv[q_blocks].astype(jnp.bfloat16)
    kv_ref[mp, :, wide:] = qkv[q_blocks + 1].astype(jnp.bfloat16)

    @pl.loop(1, n_dp)
    def _(k):
        source = lax.rem(dp + k, n_dp)
        adapter_copy(k, source, source).wait_recv()

    adapter_pair(core).start()
    kv_ring.begin()
    adapter_pair(1 - core).wait_recv()

    down = adapters[0].reshape(n_dp * rank, columns)
    mid = lax.dot_general(
        normed[...], down, (((1,), (1,)), ((), ())), preferred_element_type=jnp.float32
    )
    owner = lax.broadcasted_iota(jnp.int32, (rows, n_dp * rank), 1) // rank
    middle[...] = jnp.where(owner == adapter, mid, 0.0).astype(jnp.bfloat16)

    def finish_query(j):
        up = adapters[1, :, :, j * wide : (j + 1) * wide].reshape(n_dp * rank, wide)
        extra = jnp.dot(middle[...], up, preferred_element_type=jnp.float32)
        query[j] = (qkv[j] + extra).astype(jnp.bfloat16)

    finish_query(0)
    finish_query(1)
    out_rows.near()
    kv_ring.forward_near()
    for j in range(2, q_blocks):
        finish_query(j)
    kv_ring.got_partner()
    kv_ring.forward_rest()
    out_rows.distant()
    kv_ring.got_near()
    kv_ring.forward_far()
    kv_ring.got_far()

    n_kv = 2
    share = q_blocks // n_kv
    for kv_head in range(n_kv):
        k_cols = slice(kv_head * HEAD_SIZE, (kv_head + 1) * HEAD_SIZE)
        v_cols = slice(wide + kv_head * HEAD_SIZE, wide + (kv_head + 1) * HEAD_SIZE)

        @pl.loop(0, share)
        def _(step):
            block = step + kv_head * share
            for lane in range(wide // HEAD_SIZE):
                cols = slice(lane * HEAD_SIZE, (lane + 1) * HEAD_SIZE)
                keys = kv_ref[pl.ds(first, window // rows), :, k_cols].reshape(window, HEAD_SIZE)
                values = kv_ref[pl.ds(first, window // rows), :, v_cols].reshape(window, HEAD_SIZE)
                scores = lax.dot_general(
                    query[block, :, cols],
                    keys,
                    (((1,), (1,)), ((), ())),
                    preferred_element_type=jnp.float32,
                )
                scores = scores + bias[...]
                row_max = jnp.max(scores, axis=1, keepdims=True)
                expd = jnp.exp((scores - row_max) * HEAD_SIZE ** (-0.5))
                total = jnp.sum(expd, axis=1, keepdims=True)
                mixed = jnp.dot(
                    expd.astype(jnp.bfloat16), values, preferred_element_type=jnp.float32
                )
                attended[block, :, cols] = (mixed / total).astype(jnp.bfloat16)

        if kv_head == 0:
            out_rows.finish(0)
            out_rows.finish(1)

    out_rows.finish(2)
    out_rows.got_partner()
    for s in range(3):
        out_rows.got(s)
    own_out.wait()

    own_rows = out_weights.shape[1]
    for lo in range(0, n_mp, 2):
        part = out_weights[lo : lo + 2].reshape(2 * own_rows, columns)
        total = tokens_ref[:, lo * own_rows : (lo + 2) * own_rows].astype(jnp.float32)
        for j in range(q_blocks):
            total += lax.dot_general(
                attended[j],
                part[:, j * wide : (j + 1) * wide],
                (((1,), (1,)), ((), ())),
                preferred_element_type=jnp.float32,
            )
        residual_ref[:, lo * own_rows : (lo + 2) * own_rows] = total.astype(jnp.bfloat16)

    ring.drain()
    kv_ring.drain()
    out_rows.drain()
    low_rows.drain()
    adapter_pair(core).wait_send()

    @pl.loop(1, n_dp)
    def _(k):
        adapter_copy(k, dp, lax.rem(dp + k, n_dp)).wait_send()


def front(tokens, gain, weight, down, up, lengths, request, out_weight):
    n_dp, n_mp = lax.axis_size("dp"), lax.axis_size("mp")
    rows, columns = tokens.shape
    depth, wide = weight.shape
    q_blocks = columns // wide
    rank = up.shape[1]
    window = min(n_mp * rows, rows + SPAN)
    dma = pltpu.SemaphoreType.DMA
    vmem = pl.BlockSpec(memory_space=pltpu.VMEM)
    return pl.pallas_call(
        front_kernel,
        in_specs=[vmem] * 8,
        out_specs=[vmem] * 2,
        out_shape=[
            jax.ShapeDtypeStruct((rows, columns), jnp.bfloat16),
            jax.ShapeDtypeStruct((n_mp, rows, 2 * wide), jnp.bfloat16),
        ],
        scratch_shapes=[
            pltpu.VMEM((n_mp, depth, wide), jnp.bfloat16),
            pltpu.VMEM((2, n_dp, rank, columns), jnp.bfloat16),
            pltpu.VMEM((n_mp,) + out_weight.shape, jnp.bfloat16),
            pltpu.VMEM((n_mp, rows, wide), jnp.float32),
            pltpu.VMEM((q_blocks, rows, wide), jnp.bfloat16),
            pltpu.VMEM((q_blocks, rows, wide), jnp.bfloat16),
            pltpu.VMEM((rows, window), jnp.float32),
            pltpu.VMEM((rows, columns), jnp.bfloat16),
            pltpu.VMEM((rows, n_dp * rank), jnp.bfloat16),
            pltpu.VMEM((2, rank, columns), jnp.bfloat16),
            dma((HOPS,)),
            dma((HOPS,)),
            dma((PASSES,)),
            dma((PASSES,)),
            dma((HOPS,)),
            dma((HOPS,)),
            dma((PASSES,)),
            dma((PASSES,)),
            dma((n_dp,)),
            dma((n_dp,)),
            dma((2,)),
            dma(()),
        ],
        compiler_params=pltpu.CompilerParams(
            collective_id=0, has_side_effects=True, vmem_limit_bytes=60 << 20
        ),
        name="front",
    )(tokens, gain, weight, down, up, lengths, request, out_weight)


ORDER = (0, 10, 11, 9, 14, 6, 2, 8, 5, 7, 13, 15, 1, 3, 4, 12)
PIECE = 16


def expert_kernel(
    residual_ref,
    gain_ref,
    router_ref,
    routes_ref,
    page_slots_ref,
    kv_hbm,
    up_hbm,
    down_hbm,
    out_ref,
    pool_ref,
    sent,
    arrived,
    produced,
    returned,
    up,
    down,
    active,
    back,
    total,
    ffn_ref,
    pages,
    places,
    high,
    rest,
    along_z,
    along_y,
    places_z,
    places_y,
    near_send,
    near_recv,
    table_send,
    table_recv,
    go_send,
    go_recv,
    back_send,
    back_recv,
    local_sem,
):
    dp = lax.axis_index("dp")
    n_local, n_dp, cap, columns = produced.shape
    side = SIDE
    half = columns // 2
    z, y = dp // side, lax.rem(dp, side)
    slots = n_dp * cap
    hidden = down.shape[1]
    rows = ffn_ref.shape[0]
    n_exp = n_local * n_dp
    tile = 512

    def toward(k):
        return lax.rem(z + k // side, side) * side + lax.rem(y + k % side, side)

    def source(k):
        return (
            lax.rem(z + side - k // side, side) * side + lax.rem(y + side - k % side, side)
        )

    def transposed(k):
        return k % side * side + k // side

    owners = [toward(transposed(pos)) for pos in range(n_dp)]

    barrier = pltpu.get_barrier_semaphore()

    @pl.loop(1, n_dp)
    def _(k):
        peer = lax.rem(dp + k, n_dp)
        pl.semaphore_signal(barrier, inc=1, device_id={"dp": peer}, device_id_type=MESH)

    up_copy = pltpu.make_async_copy(up_hbm, up, local_sem.at[0])
    down_copy = pltpu.make_async_copy(down_hbm, down, local_sem.at[1])
    kv_copy = pltpu.make_async_copy(kv_hbm, pages, local_sem.at[2])
    up_copy.start()
    down_copy.start()
    kv_copy.start()

    def spread(table, e, holders):
        return [
            jnp.broadcast_to(table[pl.ds(owner * n_local + e, 1), :], (cap, rows))
            for owner in holders
        ]

    count = lax.broadcasted_iota(jnp.int32, (cap, rows), 0).astype(jnp.float32)
    wanted = routes_ref[...]
    named = lax.broadcasted_iota(jnp.int32, (n_exp, rows), 0)
    hits = wanted[0:1] == named
    for k in range(1, routes_ref.shape[0]):
        hits = hits | (wanted[k : k + 1] == named)
    early = lax.broadcasted_iota(jnp.int32, (rows, rows), 0)
    late = lax.broadcasted_iota(jnp.int32, (rows, rows), 1)
    before = jnp.where(early < late, 1.0, 0.0).astype(jnp.bfloat16)
    marks = jnp.where(hits, 1.0, 0.0)
    ranks = jnp.dot(marks.astype(jnp.bfloat16), before, preferred_element_type=jnp.float32)
    places[...] = jnp.where(hits, ranks, -1.0)
    places_z[z] = places[...]
    places_y[y] = places[...]

    widened = residual_ref[...].astype(jnp.float32)
    inv_rms = lax.rsqrt(jnp.mean(widened * widened, axis=1, keepdims=True) + eps)
    ffn_ref[...] = (widened * inv_rms * gain_ref[...][None, :]).astype(jnp.bfloat16)
    along_z[z] = ffn_ref[:, :half]
    along_y[y] = ffn_ref[:, half:]

    def transfer(src, dst, send, recv, e, pos, piece, peer):
        part = pl.ds(piece * PIECE, PIECE)
        return pltpu.make_async_remote_copy(
            src_ref=src.at[e, pos, part],
            dst_ref=dst.at[e, pos, part],
            send_sem=send.at[e],
            recv_sem=recv.at[e],
            device_id={"dp": peer},
            device_id_type=MESH,
        )

    def whole(src, dst, send, recv, e):
        return pltpu.make_async_remote_copy(
            src_ref=src.at[e, 1:],
            dst_ref=dst.at[e, 1:],
            send_sem=send.at[e],
            recv_sem=recv.at[e],
            device_id={"dp": owners[1]},
            device_id_type=MESH,
        )

    fields = (along_z, along_y)
    tables = (places_z, places_y)
    index = (z, y)

    def peer_at(part, d):
        if part == 0:
            return lax.rem(z + d, side) * side + y
        return z * side + lax.rem(y + d, side)

    def near(ref, send, recv, part, d, back=False):
        step = side - d if back else 0
        spot = ref.at[lax.rem(index[part] + step, side)]
        i = part * (side - 1) + d - 1
        return pltpu.make_async_remote_copy(
            src_ref=spot,
            dst_ref=spot,
            send_sem=send.at[i],
            recv_sem=recv.at[i],
            device_id={"dp": peer_at(part, d)},
            device_id_type=MESH,
        )

    def landing(part, e, d, i):
        if part == 0:
            return arrived.at[e, d, i, :, pl.ds(0, half)]
        return arrived.at[e, i, d, :, pl.ds(half, half)]

    def leg(part, e, d, i):
        sem = (e * 2 + part) * (side - 1) + d - 1
        return pltpu.make_async_remote_copy(
            src_ref=sent.at[part, e, d, i],
            dst_ref=landing(part, e, d, i),
            send_sem=go_send.at[sem],
            recv_sem=go_recv.at[sem],
            device_id={"dp": peer_at(1 - part, d)},
            device_id_type=MESH,
        )

    def legs(part, e, d):
        sem = (e * 2 + part) * (side - 1) + d - 1
        return pltpu.make_async_remote_copy(
            src_ref=sent.at[part, e, d],
            dst_ref=landing(part, e, d, slice(None)),
            send_sem=go_send.at[sem],
            recv_sem=go_recv.at[sem],
            device_id={"dp": peer_at(1 - part, d)},
            device_id_type=MESH,
        )

    def pack(part, e, i):
        origin = lax.rem(index[part] + side - i, side)
        table = tables[part].at[origin]
        pick = jnp.concatenate(
            [
                jnp.where(row == count, 1.0, 0.0).astype(jnp.bfloat16)
                for row in spread(table, e, [peer_at(1 - part, d) for d in range(side)])
            ],
            axis=0,
        )
        got = jnp.dot(pick, fields[part][origin], preferred_element_type=jnp.float32)
        got = got.astype(jnp.bfloat16).reshape(side, cap, half)
        if part == 0:
            arrived[e, 0, i, :, :half] = got[0]
        else:
            arrived[e, i, 0, :, half:] = got[0]
        for d in range(1, side):
            sent[part, e, d, i] = got[d]

    def dispatch(part, e, i):
        for d in (2, 1, 3):
            leg(part, e, d, i).start()

    def compute(e):
        @pl.loop(0, hidden // 256)
        def _(j):
            gate_cols = pl.ds(pl.multiple_of(j * 256, 256), 256)
            up_cols = pl.ds(pl.multiple_of(hidden + j * 256, 256), 256)
            given = arrived[e].reshape(slots, columns)
            gate = jnp.dot(given, up[e, :, gate_cols], preferred_element_type=jnp.float32)
            lift = jnp.dot(given, up[e, :, up_cols], preferred_element_type=jnp.float32)
            active[:, gate_cols] = (jnp.maximum(gate, 0.0) * lift).astype(jnp.bfloat16)

        @pl.loop(0, columns // 256)
        def _(j):
            cols = pl.ds(pl.multiple_of(j * 256, 256), 256)
            made = jnp.dot(active[...], down[e, :, cols], preferred_element_type=jnp.float32)
            produced[e, :, :, cols] = made.astype(jnp.bfloat16).reshape(n_dp, cap, 256)

        returned[e, 0] = produced[e, 0]

    def give_back(e):
        for piece in range(cap // PIECE):
            for k in ORDER[1:]:
                pos, peer = transposed(k), source(k)
                transfer(produced, returned, back_send, back_recv, e, pos, piece, peer).start()

    def combine(e):
        @pl.loop(0, columns // tile)
        def _(j):
            cols = pl.ds(pl.multiple_of(j * tile, tile), tile)
            given = returned[e, :, :, cols].reshape(slots, tile)
            mixed = jnp.dot(back[e, 0], given, preferred_element_type=jnp.float32)
            mixed += jnp.dot(back[e, 1], given, preferred_element_type=jnp.float32)
            if e == 0:
                total[:, cols] = residual_ref[:, cols].astype(jnp.float32) + mixed
            else:
                out_ref[:, cols] = (total[:, cols] + mixed).astype(jnp.bfloat16)

    pl.semaphore_wait(barrier, n_dp - 1)
    for d in (1, 3, 2):
        for part in (0, 1):
            near(tables[part], table_send, table_recv, part, d).start()
            near(fields[part], near_send, near_recv, part, d).start()
    pack(0, 0, 0)
    pack(1, 0, 0)
    dispatch(0, 0, 0)
    waiting = (1, 0, 0)
    for d in (1, 3, 2):
        for part in (0, 1):
            near(tables[part], table_send, table_recv, part, d, True).wait_recv()
            near(fields[part], near_send, near_recv, part, d, True).wait_recv()
            pack(part, 0, d)
            dispatch(*waiting)
            waiting = (part, 0, d)
    for i in range(side):
        for part in (0, 1):
            pack(part, 1, i)
            dispatch(*waiting)
            waiting = (part, 1, i)
    logits = lax.dot_general(
        router_ref[...], ffn_ref[...], (((1,), (1,)), ((), ())), preferred_element_type=jnp.float32
    )
    dispatch(*waiting)
    peak = jnp.max(jnp.where(hits, logits, neg_fill), axis=0, keepdims=True)
    expl = jnp.where(hits, jnp.exp(jnp.where(hits, logits, peak) - peak), 0.0)
    shares = expl / jnp.sum(expl, axis=0, keepdims=True)
    high[...] = shares.astype(jnp.bfloat16).astype(jnp.float32)
    rest[...] = shares - high[...]
    for e in range(n_local):
        chosen = [row == count for row in spread(places, e, owners)]
        for i, table in enumerate((high, rest)):
            joined = jnp.concatenate(
                [jnp.where(c, row, 0.0) for c, row in zip(chosen, spread(table, e, owners))], axis=0
            )
            back[e, i] = joined.T.astype(jnp.bfloat16)

    kv_copy.wait()
    held = pool_ref.shape[0]
    order = lax.broadcasted_iota(jnp.int32, page_slots_ref.shape, 1)
    for i in range(held):
        mine = lax.axis_index("mp") * held + i

        def pick_page(p, page):
            slot = jnp.sum(jnp.where(order == p, page_slots_ref[...], 0), axis=1, keepdims=True)
            here = slot == mine
            return jnp.where(here, pages[p].astype(jnp.float32), page)

        page = lax.fori_loop(
            0, pages.shape[0], pick_page, jnp.zeros(pages.shape[1:], jnp.float32)
        )
        pool_ref[i] = page.astype(jnp.bfloat16)

    up_copy.wait()
    down_copy.wait()
    for e in range(n_local):
        for part in (0, 1):
            for d in range(1, side):
                legs(part, e, d).wait_recv()
        compute(e)
        give_back(e)
    for e in range(n_local):
        whole(produced, returned, back_send, back_recv, e).wait_recv()
        combine(e)
    for e in range(n_local):
        for part in (0, 1):
            for d in range(1, side):
                legs(part, e, d).wait_send()
        whole(produced, returned, back_send, back_recv, e).wait_send()
    for d in range(1, side):
        for part in (0, 1):
            near(tables[part], table_send, table_recv, part, d).wait_send()
            near(fields[part], near_send, near_recv, part, d).wait_send()


def experts(
    residual, gain, router, routes, page_slots, group_kv, held, gate_up_weight, down_weight
):
    rows, columns = residual.shape
    n_dp = lax.axis_size("dp")
    n_local, hidden = down_weight.shape[:2]
    n_exp = router.shape[0]
    dma = pltpu.SemaphoreType.DMA
    vmem = pl.BlockSpec(memory_space=pltpu.VMEM)
    hbm = pl.BlockSpec(memory_space=pl.ANY)
    block = (n_local, n_dp, CAP, columns)
    return pl.pallas_call(
        expert_kernel,
        in_specs=[vmem] * 5 + [hbm] * 3,
        out_specs=[vmem] * 2,
        out_shape=[
            jax.ShapeDtypeStruct((rows, columns), jnp.bfloat16),
            jax.ShapeDtypeStruct((held,) + group_kv.shape[1:], jnp.bfloat16),
        ],
        scratch_shapes=[
            pltpu.VMEM((2, n_local, SIDE, SIDE, CAP, columns // 2), jnp.bfloat16),
            pltpu.VMEM((n_local, SIDE, SIDE, CAP, columns), jnp.bfloat16),
            pltpu.VMEM(block, jnp.bfloat16),
            pltpu.VMEM(block, jnp.bfloat16),
            pltpu.VMEM(gate_up_weight.shape, jnp.bfloat16),
            pltpu.VMEM(down_weight.shape, jnp.bfloat16),
            pltpu.VMEM((n_dp * CAP, hidden), jnp.bfloat16),
            pltpu.VMEM((n_local, 2, rows, n_dp * CAP), jnp.bfloat16),
            pltpu.VMEM((rows, columns), jnp.float32),
            pltpu.VMEM((rows, columns), jnp.bfloat16),
            pltpu.VMEM(group_kv.shape, jnp.bfloat16),
            pltpu.VMEM((n_exp, rows), jnp.float32),
            pltpu.VMEM((n_exp, rows), jnp.float32),
            pltpu.VMEM((n_exp, rows), jnp.float32),
            pltpu.VMEM((SIDE, rows, columns // 2), jnp.bfloat16),
            pltpu.VMEM((SIDE, rows, columns // 2), jnp.bfloat16),
            pltpu.VMEM((SIDE, n_exp, rows), jnp.float32),
            pltpu.VMEM((SIDE, n_exp, rows), jnp.float32),
            dma((2 * SIDE - 2,)),
            dma((2 * SIDE - 2,)),
            dma((2 * SIDE - 2,)),
            dma((2 * SIDE - 2,)),
            dma((n_local * (2 * SIDE - 2),)),
            dma((n_local * (2 * SIDE - 2),)),
            dma((n_local,)),
            dma((n_local,)),
            dma((3,)),
        ],
        compiler_params=pltpu.CompilerParams(
            collective_id=1, has_side_effects=True, vmem_limit_bytes=60 << 20
        ),
        name="experts",
    )(residual, gain, router, routes, page_slots, group_kv, gate_up_weight, down_weight)


def shards(
    tokens,
    lengths,
    request_adapter,
    group_page_slots,
    routes,
    attention_gain,
    query_key_value_weight,
    adapter_down_weight,
    adapter_up_weight,
    output_weight,
    expert_norm_gain,
    router,
    expert_gate_up_weight,
    expert_down_weight,
):
    residual, group_kv = front(
        tokens,
        attention_gain,
        query_key_value_weight,
        adapter_down_weight.transpose(0, 2, 1),
        adapter_up_weight,
        lengths,
        request_adapter,
        output_weight.T,
    )
    pages_grp = group_page_slots.shape[1]
    layer_out, pool = experts(
        residual,
        expert_norm_gain,
        router.T,
        routes.T,
        group_page_slots,
        group_kv.reshape(pages_grp, PAGE, group_kv.shape[2]),
        tokens.shape[0] // PAGE,
        expert_gate_up_weight,
        expert_down_weight,
    )
    return (layer_out, pool)


def solution(mesh):
    return jax.shard_map(
        shards,
        mesh=mesh,
        in_specs=(
            P(("dp", "mp"), None),
            P("dp", None),
            P("dp", None),
            P("dp", None),
            P(("dp", "mp"), None),
            P(),
            P(None, "mp"),
            P("dp", None, None),
            P("dp", None, None),
            P(None, "mp"),
            P(),
            P(),
            P("dp", None, None),
            P("dp", None, None),
        ),
        out_specs=(P(("dp", "mp"), None), P(("dp", "mp"), None, None)),
        check_vma=False,
    )
```

```python
import jax
import jax.numpy as jnp
from jax import lax
from jax.experimental import pallas as pl
from jax.experimental.pallas import tpu as pltpu
from jax.sharding import PartitionSpec as P

HEAD_SIZE = 128
PAGE = 128
CAP = 48
SPAN = 1024

eps = 1e-06
neg_fill = -1e30


MESH = pl.DeviceIdType.MESH


class Ring:
    def __init__(self, buf, own, send, recv, span):
        me = lax.axis_index("mp")
        n = lax.axis_size("mp")
        chips = n // 2
        x, core = me // 2, lax.rem(me, 2)
        self.right = lax.rem(x + 1, chips) * 2 + core
        self.left = lax.rem(x + chips - 1, chips) * 2 + core
        self.far = lax.rem(x + 2, chips) * 2 + core
        self.me = me
        self.partner = x * 2 + 1 - core
        self.buf, self.own, self.send, self.recv = buf, own, send, recv
        self.half = span // 2

    def other(self, slot):
        return slot + 1 - 2 * lax.rem(slot, 2)

    def copy(self, i, slot, part, target, own=False):
        rows = pl.ds(part * self.half, self.half)
        return pltpu.make_async_remote_copy(
            src_ref=self.own.at[rows] if own else self.buf.at[slot, rows],
            dst_ref=self.buf.at[slot, rows],
            send_sem=self.send.at[i],
            recv_sem=self.recv.at[i],
            device_id={"mp": target},
            device_id_type=MESH,
        )

    def begin(self):
        me = self.me
        self.copy(0, me, 0, self.right, True).start()
        self.copy(1, me, 1, self.left, True).start()
        self.copy(2, me, 1, self.right, True).start()
        self.copy(3, me, 0, self.left, True).start()
        self.copy(4, me, 0, self.partner, True).start()
        self.copy(5, me, 1, self.partner, True).start()

    def got(self, i, slot, part):
        self.copy(i, slot, part, self.partner).wait_recv()

    def got_partner(self):
        self.got(4, self.partner, 0)
        self.got(5, self.partner, 1)

    def forward_near(self):
        self.got(0, self.left, 0)
        self.copy(6, self.left, 0, self.right).start()
        self.copy(7, self.left, 0, self.partner).start()
        self.got(1, self.right, 1)
        self.copy(8, self.right, 1, self.left).start()
        self.copy(9, self.right, 1, self.partner).start()

    def forward_rest(self):
        self.got(2, self.left, 1)
        self.copy(10, self.left, 1, self.partner).start()
        self.got(3, self.right, 0)
        self.copy(11, self.right, 0, self.partner).start()

    def got_near(self):
        self.got(7, self.other(self.left), 0)
        self.got(10, self.other(self.left), 1)
        self.got(9, self.other(self.right), 1)
        self.got(11, self.other(self.right), 0)

    def forward_far(self):
        self.got(6, self.far, 0)
        self.copy(12, self.far, 0, self.partner).start()
        self.got(8, self.far, 1)
        self.copy(13, self.far, 1, self.partner).start()

    def got_far(self):
        self.got(12, self.other(self.far), 0)
        self.got(13, self.other(self.far), 1)

    def drain(self):
        for i in range(14):
            self.copy(i, self.me, 0, self.partner, True).wait_send()


HOPS = 14
SIDE = 4


class Spread:
    def __init__(self, ring, buf, own, base, send, recv):
        dp = lax.axis_index("dp")
        self.index = (dp // SIDE, lax.rem(dp, SIDE))
        self.ring, self.buf, self.own, self.base = ring, buf, own, base
        self.chunk = (buf.shape[1] - base) // SIDE
        self.wide = buf.shape[2] // 2
        self.send, self.recv = send, recv
        self.slots = (ring.left, ring.right, ring.far)

    def piece(self, ref, part, index):
        rows = pl.ds(self.base + index * self.chunk, self.chunk)
        return ref.at[rows, pl.ds(part * self.wide, self.wide)]

    def across(self, i, slot, part, target, own=False):
        index = self.index[part]
        return pltpu.make_async_remote_copy(
            src_ref=self.piece(self.own if own else self.buf.at[slot], part, index),
            dst_ref=self.piece(self.buf.at[slot], part, index),
            send_sem=self.send.at[i],
            recv_sem=self.recv.at[i],
            device_id={"mp": target},
            device_id_type=MESH,
        )

    def along(self, s, part, d, back=False):
        z, y = self.index
        step = SIDE - d if back else d
        peer = (
            lax.rem(z + step, SIDE) * SIDE + y if part == 0 else z * SIDE + lax.rem(y + step, SIDE)
        )
        index = lax.rem(self.index[part] + step, SIDE) if back else self.index[part]
        ref = self.piece(self.buf.at[self.slots[s]], part, index)
        i = 6 + (s * 2 + part) * 3 + d - 1
        return pltpu.make_async_remote_copy(
            src_ref=ref,
            dst_ref=ref,
            send_sem=self.send.at[i],
            recv_sem=self.recv.at[i],
            device_id={"dp": peer},
            device_id_type=MESH,
        )

    def hand(self, i, slot, own=False):
        rows = pl.ds(self.base, SIDE * self.chunk)
        return pltpu.make_async_remote_copy(
            src_ref=self.own.at[rows] if own else self.buf.at[slot, rows],
            dst_ref=self.buf.at[slot, rows],
            send_sem=self.send.at[i],
            recv_sem=self.recv.at[i],
            device_id={"mp": self.ring.partner},
            device_id_type=MESH,
        )

    def begin(self):
        ring = self.ring
        self.across(0, ring.me, 0, ring.right, True).start()
        self.across(1, ring.me, 1, ring.left, True).start()
        self.across(2, ring.me, 1, ring.right, True).start()
        self.across(3, ring.me, 0, ring.left, True).start()
        self.hand(27, ring.me, True).start()

    def push(self, s, part):
        for d in (2, 1, 3):
            self.along(s, part, d).start()

    def near(self):
        ring = self.ring
        self.across(0, ring.left, 0, ring.right).wait_recv()
        self.across(4, ring.left, 0, ring.right).start()
        self.push(0, 0)
        self.across(1, ring.right, 1, ring.left).wait_recv()
        self.across(5, ring.right, 1, ring.left).start()
        self.push(1, 1)
        self.across(2, ring.left, 1, ring.right).wait_recv()
        self.push(0, 1)
        self.across(3, ring.right, 0, ring.left).wait_recv()
        self.push(1, 0)

    def distant(self):
        ring = self.ring
        self.across(4, ring.far, 0, ring.right).wait_recv()
        self.push(2, 0)
        self.across(5, ring.far, 1, ring.left).wait_recv()
        self.push(2, 1)

    def finish(self, s):
        for part in (0, 1):
            for d in (1, 2, 3):
                self.along(s, part, d, True).wait_recv()
        self.hand(24 + s, self.slots[s]).start()

    def got(self, s):
        self.hand(24 + s, self.ring.other(self.slots[s])).wait_recv()

    def got_partner(self):
        self.hand(27, self.ring.partner).wait_recv()

    def drain(self):
        ring = self.ring
        for i in range(6):
            self.across(i, ring.me, (0, 1, 1, 0, 0, 1)[i], ring.right, True).wait_send()
        for s in range(3):
            for part in (0, 1):
                for d in (1, 2, 3):
                    self.along(s, part, d).wait_send()
            self.hand(24 + s, self.slots[s]).wait_send()
        self.hand(27, ring.me, True).wait_send()


PASSES = 28


def front_kernel(
    tokens_ref,
    gain_ref,
    weight_ref,
    down_ref,
    up_ref,
    lengths_ref,
    request_ref,
    out_weight_ref,
    residual_ref,
    kv_ref,
    weights,
    adapters,
    out_weights,
    qkv,
    query,
    attended,
    bias,
    normed,
    middle,
    packed_ref,
    weight_send,
    weight_recv,
    low_send,
    low_recv,
    kv_send,
    kv_recv,
    out_send,
    out_recv,
    adapter_send,
    adapter_recv,
    pair_sem,
    local_sem,
):
    dp, mp = lax.axis_index("dp"), lax.axis_index("mp")
    n_dp = lax.axis_size("dp")
    n_mp = lax.axis_size("mp")
    rows, columns = tokens_ref.shape
    wide = weight_ref.shape[1]
    q_blocks = qkv.shape[0] - 2
    rank = up_ref.shape[1]

    depth = weight_ref.shape[0]
    core = lax.rem(mp, 2)
    ring = Ring(weights, weight_ref, weight_send, weight_recv, depth // 2)
    low_rows = Spread(ring, weights, weight_ref, depth // 2, low_send, low_recv)
    kv_ring = Ring(kv_ref, kv_ref.at[mp], kv_send, kv_recv, rows)
    out_rows = Spread(ring, out_weights, out_weight_ref, 0, out_send, out_recv)

    barrier = pltpu.get_barrier_semaphore()
    for peer in (ring.left, ring.right, ring.partner):
        pl.semaphore_signal(barrier, inc=1, device_id={"mp": peer}, device_id_type=MESH)

    @pl.loop(1, n_dp)
    def _(k):
        peer = lax.rem(dp + k, n_dp)
        pl.semaphore_signal(barrier, inc=1, device_id={"dp": peer}, device_id_type=MESH)

    pl.semaphore_wait(barrier, 3 + n_dp - 1)

    def adapter_copy(k, slot, peer):
        return pltpu.make_async_remote_copy(
            src_ref=packed_ref.at[core],
            dst_ref=adapters.at[core, slot],
            send_sem=adapter_send.at[k],
            recv_sem=adapter_recv.at[slot],
            device_id={"dp": peer},
            device_id_type=MESH,
        )

    def adapter_pair(kind):
        return pltpu.make_async_remote_copy(
            src_ref=adapters.at[kind],
            dst_ref=adapters.at[kind],
            send_sem=pair_sem.at[0],
            recv_sem=pair_sem.at[1],
            device_id={"mp": ring.partner},
            device_id_type=MESH,
        )

    low_rows.begin()
    ring.begin()

    packed_ref[0] = down_ref[0]
    packed_ref[1] = up_ref[0]
    own_out = pltpu.make_async_copy(out_weight_ref, out_weights.at[mp], local_sem)
    own_out.start()

    widened = tokens_ref[...].astype(jnp.float32)
    inv_rms = lax.rsqrt(jnp.mean(widened * widened, axis=1, keepdims=True) + eps)
    normed[...] = (widened * inv_rms * gain_ref[...][None, :]).astype(jnp.bfloat16)
    adapters[core, dp] = packed_ref[core]

    low_rows.near()

    @pl.loop(1, n_dp)
    def _(k):
        adapter_copy(k, dp, lax.rem(dp + k, n_dp)).start()

    place = lax.broadcasted_iota(jnp.int32, (rows, 1), 0) + mp * rows
    low = jnp.zeros((rows, 1), jnp.int32)
    adapter = jnp.zeros((rows, 1), jnp.int32) + request_ref[:, 0:1]
    ends = jnp.zeros((1, 1), jnp.int32)
    for r in range(1, lengths_ref.shape[1]):
        ends = ends + lengths_ref[:, r - 1 : r]
        passed = place >= ends
        low = jnp.where(passed, ends, low)
        adapter = jnp.where(passed, request_ref[:, r : r + 1], adapter)

    window = bias.shape[1]
    first = jnp.maximum(mp + 1 - window // rows, 0)
    key = lax.broadcasted_iota(jnp.int32, (rows, window), 1) + first * rows
    bias[...] = jnp.where((key >= low) & (key <= place), 0.0, neg_fill)

    def project(slot):
        qkv[slot] = jnp.dot(normed[...], weights[slot], preferred_element_type=jnp.float32)

    qkv[mp] = jnp.dot(normed[...], weight_ref[...], preferred_element_type=jnp.float32)
    low_rows.distant()
    ring.forward_near()
    ring.got_partner()
    low_rows.got_partner()
    project(ring.partner)
    low_rows.finish(0)
    low_rows.finish(1)
    ring.forward_rest()
    project(ring.left)
    project(ring.right)
    low_rows.finish(2)
    ring.forward_far()
    out_rows.begin()
    project(ring.far)
    ring.got_near()
    low_rows.got(0)
    low_rows.got(1)
    project(ring.other(ring.left))
    project(ring.other(ring.right))
    ring.got_far()
    low_rows.got(2)
    project(ring.other(ring.far))

    kv_ref[mp, :, :wide] = qkv[q_blocks].astype(jnp.bfloat16)
    kv_ref[mp, :, wide:] = qkv[q_blocks + 1].astype(jnp.bfloat16)

    @pl.loop(1, n_dp)
    def _(k):
        source = lax.rem(dp + k, n_dp)
        adapter_copy(k, source, source).wait_recv()

    adapter_pair(core).start()
    kv_ring.begin()
    adapter_pair(1 - core).wait_recv()

    down = adapters[0].reshape(n_dp * rank, columns)
    mid = lax.dot_general(
        normed[...], down, (((1,), (1,)), ((), ())), preferred_element_type=jnp.float32
    )
    owner = lax.broadcasted_iota(jnp.int32, (rows, n_dp * rank), 1) // rank
    middle[...] = jnp.where(owner == adapter, mid, 0.0).astype(jnp.bfloat16)

    def finish_query(j):
        up = adapters[1, :, :, j * wide : (j + 1) * wide].reshape(n_dp * rank, wide)
        extra = jnp.dot(middle[...], up, preferred_element_type=jnp.float32)
        query[j] = (qkv[j] + extra).astype(jnp.bfloat16)

    finish_query(0)
    finish_query(1)
    out_rows.near()
    kv_ring.forward_near()
    for j in range(2, q_blocks):
        finish_query(j)
    kv_ring.got_partner()
    kv_ring.forward_rest()
    out_rows.distant()
    kv_ring.got_near()
    kv_ring.forward_far()
    kv_ring.got_far()

    n_kv = 2
    share = q_blocks // n_kv
    for kv_head in range(n_kv):
        k_cols = slice(kv_head * HEAD_SIZE, (kv_head + 1) * HEAD_SIZE)
        v_cols = slice(wide + kv_head * HEAD_SIZE, wide + (kv_head + 1) * HEAD_SIZE)

        @pl.loop(0, share)
        def _(step):
            block = step + kv_head * share
            for lane in range(wide // HEAD_SIZE):
                cols = slice(lane * HEAD_SIZE, (lane + 1) * HEAD_SIZE)
                keys = kv_ref[pl.ds(first, window // rows), :, k_cols].reshape(window, HEAD_SIZE)
                values = kv_ref[pl.ds(first, window // rows), :, v_cols].reshape(window, HEAD_SIZE)
                scores = lax.dot_general(
                    query[block, :, cols],
                    keys,
                    (((1,), (1,)), ((), ())),
                    preferred_element_type=jnp.float32,
                )
                scores = scores + bias[...]
                row_max = jnp.max(scores, axis=1, keepdims=True)
                expd = jnp.exp((scores - row_max) * HEAD_SIZE ** (-0.5))
                total = jnp.sum(expd, axis=1, keepdims=True)
                mixed = jnp.dot(
                    expd.astype(jnp.bfloat16), values, preferred_element_type=jnp.float32
                )
                attended[block, :, cols] = (mixed / total).astype(jnp.bfloat16)

        if kv_head == 0:
            out_rows.finish(0)
            out_rows.finish(1)

    out_rows.finish(2)
    out_rows.got_partner()
    for s in range(3):
        out_rows.got(s)
    own_out.wait()

    own_rows = out_weights.shape[1]
    for lo in range(0, n_mp, 2):
        part = out_weights[lo : lo + 2].reshape(2 * own_rows, columns)
        total = tokens_ref[:, lo * own_rows : (lo + 2) * own_rows].astype(jnp.float32)
        for j in range(q_blocks):
            total += lax.dot_general(
                attended[j],
                part[:, j * wide : (j + 1) * wide],
                (((1,), (1,)), ((), ())),
                preferred_element_type=jnp.float32,
            )
        residual_ref[:, lo * own_rows : (lo + 2) * own_rows] = total.astype(jnp.bfloat16)

    ring.drain()
    kv_ring.drain()
    out_rows.drain()
    low_rows.drain()
    adapter_pair(core).wait_send()

    @pl.loop(1, n_dp)
    def _(k):
        adapter_copy(k, dp, lax.rem(dp + k, n_dp)).wait_send()


def front(tokens, gain, weight, down, up, lengths, request, out_weight):
    n_dp, n_mp = lax.axis_size("dp"), lax.axis_size("mp")
    rows, columns = tokens.shape
    depth, wide = weight.shape
    q_blocks = columns // wide
    rank = up.shape[1]
    window = min(n_mp * rows, rows + SPAN)
    dma = pltpu.SemaphoreType.DMA
    vmem = pl.BlockSpec(memory_space=pltpu.VMEM)
    return pl.pallas_call(
        front_kernel,
        in_specs=[vmem] * 8,
        out_specs=[vmem] * 2,
        out_shape=[
            jax.ShapeDtypeStruct((rows, columns), jnp.bfloat16),
            jax.ShapeDtypeStruct((n_mp, rows, 2 * wide), jnp.bfloat16),
        ],
        scratch_shapes=[
            pltpu.VMEM((n_mp, depth, wide), jnp.bfloat16),
            pltpu.VMEM((2, n_dp, rank, columns), jnp.bfloat16),
            pltpu.VMEM((n_mp,) + out_weight.shape, jnp.bfloat16),
            pltpu.VMEM((n_mp, rows, wide), jnp.float32),
            pltpu.VMEM((q_blocks, rows, wide), jnp.bfloat16),
            pltpu.VMEM((q_blocks, rows, wide), jnp.bfloat16),
            pltpu.VMEM((rows, window), jnp.float32),
            pltpu.VMEM((rows, columns), jnp.bfloat16),
            pltpu.VMEM((rows, n_dp * rank), jnp.bfloat16),
            pltpu.VMEM((2, rank, columns), jnp.bfloat16),
            dma((HOPS,)),
            dma((HOPS,)),
            dma((PASSES,)),
            dma((PASSES,)),
            dma((HOPS,)),
            dma((HOPS,)),
            dma((PASSES,)),
            dma((PASSES,)),
            dma((n_dp,)),
            dma((n_dp,)),
            dma((2,)),
            dma(()),
        ],
        compiler_params=pltpu.CompilerParams(
            collective_id=0, has_side_effects=True, vmem_limit_bytes=60 << 20
        ),
        name="front",
    )(tokens, gain, weight, down, up, lengths, request, out_weight)


def expert_kernel(
    residual_ref,
    gain_ref,
    router_ref,
    routes_ref,
    page_slots_ref,
    kv_hbm,
    up_hbm,
    down_hbm,
    out_ref,
    pool_ref,
    sent,
    arrived,
    produced,
    middle,
    folding,
    folded,
    up,
    down,
    active,
    back,
    total,
    ffn_ref,
    pages,
    along_z,
    along_y,
    places_z,
    places_y,
    shares_z,
    shares_y,
    near_send,
    near_recv,
    table_send,
    table_recv,
    share_send,
    share_recv,
    go_send,
    go_recv,
    back_send,
    back_recv,
    fold_send,
    fold_recv,
    local_sem,
):
    dp = lax.axis_index("dp")
    n_local, side, _, cap, columns = produced.shape
    n_dp = side * side
    half = columns // 2
    z, y = dp // side, lax.rem(dp, side)
    slots = n_dp * cap
    hidden = down.shape[1]
    rows = ffn_ref.shape[0]
    n_exp = n_local * n_dp
    tile = 512

    barrier = pltpu.get_barrier_semaphore()

    @pl.loop(1, n_dp)
    def _(k):
        peer = lax.rem(dp + k, n_dp)
        pl.semaphore_signal(barrier, inc=1, device_id={"dp": peer}, device_id_type=MESH)

    up_copy = pltpu.make_async_copy(up_hbm, up, local_sem.at[0])
    down_copy = pltpu.make_async_copy(down_hbm, down, local_sem.at[1])
    kv_copy = pltpu.make_async_copy(kv_hbm, pages, local_sem.at[2])
    up_copy.start()
    down_copy.start()
    kv_copy.start()

    def spread(table, e, holders):
        return [
            jnp.broadcast_to(table[pl.ds(owner * n_local + e, 1), :], (cap, rows))
            for owner in holders
        ]

    count = lax.broadcasted_iota(jnp.int32, (cap, rows), 0).astype(jnp.float32)
    wanted = routes_ref[...]
    named = lax.broadcasted_iota(jnp.int32, (n_exp, rows), 0)
    hits = wanted[0:1] == named
    for k in range(1, routes_ref.shape[0]):
        hits = hits | (wanted[k : k + 1] == named)
    early = lax.broadcasted_iota(jnp.int32, (rows, rows), 0)
    late = lax.broadcasted_iota(jnp.int32, (rows, rows), 1)
    before = jnp.where(early < late, 1.0, 0.0).astype(jnp.bfloat16)
    marks = jnp.where(hits, 1.0, 0.0)
    ranks = jnp.dot(marks.astype(jnp.bfloat16), before, preferred_element_type=jnp.float32)
    places = jnp.where(hits, ranks, -1.0)
    places_z[z] = places
    places_y[y] = places

    widened = residual_ref[...].astype(jnp.float32)
    inv_rms = lax.rsqrt(jnp.mean(widened * widened, axis=1, keepdims=True) + eps)
    ffn_ref[...] = (widened * inv_rms * gain_ref[...][None, :]).astype(jnp.bfloat16)
    along_z[z] = ffn_ref[:, :half]
    along_y[y] = ffn_ref[:, half:]

    fields = (along_z, along_y)
    tables = (places_z, places_y)
    weights = (shares_z, shares_y)
    index = (z, y)

    def peer_at(part, d):
        if part == 0:
            return lax.rem(z + d, side) * side + y
        return z * side + lax.rem(y + d, side)

    def near(ref, send, recv, part, d, back=False):
        step = side - d if back else 0
        spot = ref.at[lax.rem(index[part] + step, side)]
        i = part * (side - 1) + d - 1
        return pltpu.make_async_remote_copy(
            src_ref=spot,
            dst_ref=spot,
            send_sem=send.at[i],
            recv_sem=recv.at[i],
            device_id={"dp": peer_at(part, d)},
            device_id_type=MESH,
        )

    def landing(part, e, d, i):
        if part == 0:
            return arrived.at[e, d, i, :, pl.ds(0, half)]
        return arrived.at[e, i, d, :, pl.ds(half, half)]

    def leg(part, e, d, i):
        sem = (e * 2 + part) * (side - 1) + d - 1
        return pltpu.make_async_remote_copy(
            src_ref=sent.at[part, e, d, i],
            dst_ref=landing(part, e, d, i),
            send_sem=go_send.at[sem],
            recv_sem=go_recv.at[sem],
            device_id={"dp": peer_at(1 - part, d)},
            device_id_type=MESH,
        )

    def legs(part, e, d):
        sem = (e * 2 + part) * (side - 1) + d - 1
        return pltpu.make_async_remote_copy(
            src_ref=sent.at[part, e, d],
            dst_ref=landing(part, e, d, slice(None)),
            send_sem=go_send.at[sem],
            recv_sem=go_recv.at[sem],
            device_id={"dp": peer_at(1 - part, d)},
            device_id_type=MESH,
        )

    def pack(part, e, i):
        origin = lax.rem(index[part] + side - i, side)
        table = tables[part].at[origin]
        pick = jnp.concatenate(
            [
                jnp.where(row == count, 1.0, 0.0).astype(jnp.bfloat16)
                for row in spread(table, e, [peer_at(1 - part, d) for d in range(side)])
            ],
            axis=0,
        )
        got = jnp.dot(pick, fields[part][origin], preferred_element_type=jnp.float32)
        got = got.astype(jnp.bfloat16).reshape(side, cap, half)
        if part == 0:
            arrived[e, 0, i, :, :half] = got[0]
        else:
            arrived[e, i, 0, :, half:] = got[0]
        for d in range(1, side):
            sent[part, e, d, i] = got[d]

    def dispatch(part, e, i):
        for d in (2, 1, 3):
            leg(part, e, d, i).start()

    def compute(e):
        @pl.loop(0, hidden // 256)
        def _(j):
            gate_cols = pl.ds(pl.multiple_of(j * 256, 256), 256)
            up_cols = pl.ds(pl.multiple_of(hidden + j * 256, 256), 256)
            given = arrived[e].reshape(slots, columns)
            gate = jnp.dot(given, up[e, :, gate_cols], preferred_element_type=jnp.float32)
            lift = jnp.dot(given, up[e, :, up_cols], preferred_element_type=jnp.float32)
            active[:, gate_cols] = (jnp.maximum(gate, 0.0) * lift).astype(jnp.bfloat16)

        @pl.loop(0, columns // 256)
        def _(j):
            cols = pl.ds(pl.multiple_of(j * 256, 256), 256)
            made = jnp.dot(active[...], down[e, :, cols], preferred_element_type=jnp.float32)
            produced[e, :, :, :, cols] = made.astype(jnp.bfloat16).reshape(side, side, cap, 256)

        middle[0, e, 0] = produced[e, 0, :, :, :half]
        middle[1, e, 0] = produced[e, :, 0, :, half:]

    def give_back(part, e, d):
        if part == 0:
            made = produced.at[e, d, :, :, pl.ds(0, half)]
        else:
            made = produced.at[e, :, d, :, pl.ds(half, half)]
        sem = (e * 2 + part) * (side - 1) + d - 1
        return pltpu.make_async_remote_copy(
            src_ref=made,
            dst_ref=middle.at[part, e, d],
            send_sem=back_send.at[sem],
            recv_sem=back_recv.at[sem],
            device_id={"dp": peer_at(1 - part, side - d)},
            device_id_type=MESH,
        )

    def fold(part, i):
        sem = part * (side - 1) + i - 1
        return pltpu.make_async_remote_copy(
            src_ref=folding.at[part, i],
            dst_ref=folded.at[part, i],
            send_sem=fold_send.at[sem],
            recv_sem=fold_recv.at[sem],
            device_id={"dp": peer_at(part, side - i)},
            device_id_type=MESH,
        )

    def weigh(part, i):
        origin = lax.rem(index[part] + side - i, side)
        holders = [peer_at(1 - part, d) for d in range(side)]
        high, rest = [], []
        for e in range(n_local):
            spots = spread(tables[part].at[origin], e, holders)
            for spot, share in zip(spots, spread(weights[part].at[origin], e, holders)):
                chosen = jnp.where(spot == count, share, 0.0)
                top = chosen.astype(jnp.bfloat16).astype(jnp.float32)
                high.append(top)
                rest.append(chosen - top)
        back[part, i, 0] = jnp.concatenate(high, axis=0).T.astype(jnp.bfloat16)
        back[part, i, 1] = jnp.concatenate(rest, axis=0).T.astype(jnp.bfloat16)

    def partial(part, i):
        given = middle[part, :, :, i].reshape(n_local * side * cap, half)
        mixed = jnp.dot(back[part, i, 0], given, preferred_element_type=jnp.float32)
        return mixed + jnp.dot(back[part, i, 1], given, preferred_element_type=jnp.float32)

    pl.semaphore_wait(barrier, n_dp - 1)
    for d in (1, 3, 2):
        for part in (0, 1):
            near(tables[part], table_send, table_recv, part, d).start()
            near(fields[part], near_send, near_recv, part, d).start()
    logits = lax.dot_general(
        router_ref[...], ffn_ref[...], (((1,), (1,)), ((), ())), preferred_element_type=jnp.float32
    )
    peak = jnp.max(jnp.where(hits, logits, neg_fill), axis=0, keepdims=True)
    expl = jnp.where(hits, jnp.exp(jnp.where(hits, logits, peak) - peak), 0.0)
    shares = expl / jnp.sum(expl, axis=0, keepdims=True)
    shares_z[z] = shares
    shares_y[y] = shares
    pack(0, 0, 0)
    pack(1, 0, 0)
    for d in (1, 3, 2):
        for part in (0, 1):
            near(weights[part], share_send, share_recv, part, d).start()
    dispatch(0, 0, 0)
    waiting = (1, 0, 0)
    for d in (1, 3, 2):
        for part in (0, 1):
            near(tables[part], table_send, table_recv, part, d, True).wait_recv()
            near(fields[part], near_send, near_recv, part, d, True).wait_recv()
            pack(part, 0, d)
            dispatch(*waiting)
            waiting = (part, 0, d)
    for i in range(side):
        for part in (0, 1):
            pack(part, 1, i)
            dispatch(*waiting)
            waiting = (part, 1, i)
    weigh(0, 0)
    dispatch(*waiting)
    weigh(1, 0)
    for d in (1, 3, 2):
        for part in (0, 1):
            near(weights[part], share_send, share_recv, part, d, True).wait_recv()
            weigh(part, d)

    kv_copy.wait()
    held = pool_ref.shape[0]
    order = lax.broadcasted_iota(jnp.int32, page_slots_ref.shape, 1)
    for i in range(held):
        mine = lax.axis_index("mp") * held + i

        def pick_page(p, page):
            slot = jnp.sum(jnp.where(order == p, page_slots_ref[...], 0), axis=1, keepdims=True)
            here = slot == mine
            return jnp.where(here, pages[p].astype(jnp.float32), page)

        page = lax.fori_loop(
            0, pages.shape[0], pick_page, jnp.zeros(pages.shape[1:], jnp.float32)
        )
        pool_ref[i] = page.astype(jnp.bfloat16)

    up_copy.wait()
    down_copy.wait()
    for e in range(n_local):
        for part in (0, 1):
            for d in range(1, side):
                legs(part, e, d).wait_recv()
        compute(e)
        for d in (2, 1, 3):
            for part in (0, 1):
                give_back(part, e, d).start()
    for e in range(n_local):
        for d in range(1, side):
            for part in (0, 1):
                give_back(part, e, d).wait_recv()
    ready = None
    for i in (2, 1, 3):
        for part in (0, 1):
            folding[part, i] = partial(part, i).astype(jnp.bfloat16)
            if ready:
                fold(*ready).start()
            ready = (part, i)
    for part in (0, 1):
        cols = pl.ds(part * half, half)
        total[:, cols] = residual_ref[:, cols].astype(jnp.float32) + partial(part, 0)
        if ready:
            fold(*ready).start()
            ready = None
    for part in (0, 1):
        cols = pl.ds(part * half, half)
        for i in range(1, side):
            fold(part, i).wait_recv()
        mixed = total[:, cols]
        for i in range(1, side):
            mixed += folded[part, i].astype(jnp.float32)
        out_ref[:, cols] = mixed.astype(jnp.bfloat16)
    for part in (0, 1):
        for d in range(1, side):
            near(tables[part], table_send, table_recv, part, d).wait_send()
            near(fields[part], near_send, near_recv, part, d).wait_send()
            near(weights[part], share_send, share_recv, part, d).wait_send()
            fold(part, d).wait_send()
            for e in range(n_local):
                legs(part, e, d).wait_send()
                give_back(part, e, d).wait_send()


def experts(
    residual, gain, router, routes, page_slots, group_kv, held, gate_up_weight, down_weight
):
    rows, columns = residual.shape
    n_dp = lax.axis_size("dp")
    n_local, hidden = down_weight.shape[:2]
    n_exp = router.shape[0]
    dma = pltpu.SemaphoreType.DMA
    vmem = pl.BlockSpec(memory_space=pltpu.VMEM)
    hbm = pl.BlockSpec(memory_space=pl.ANY)
    return pl.pallas_call(
        expert_kernel,
        in_specs=[vmem] * 5 + [hbm] * 3,
        out_specs=[vmem] * 2,
        out_shape=[
            jax.ShapeDtypeStruct((rows, columns), jnp.bfloat16),
            jax.ShapeDtypeStruct((held,) + group_kv.shape[1:], jnp.bfloat16),
        ],
        scratch_shapes=[
            pltpu.VMEM((2, n_local, SIDE, SIDE, CAP, columns // 2), jnp.bfloat16),
            pltpu.VMEM((n_local, SIDE, SIDE, CAP, columns), jnp.bfloat16),
            pltpu.VMEM((n_local, SIDE, SIDE, CAP, columns), jnp.bfloat16),
            pltpu.VMEM((2, n_local, SIDE, SIDE, CAP, columns // 2), jnp.bfloat16),
            pltpu.VMEM((2, SIDE, rows, columns // 2), jnp.bfloat16),
            pltpu.VMEM((2, SIDE, rows, columns // 2), jnp.bfloat16),
            pltpu.VMEM(gate_up_weight.shape, jnp.bfloat16),
            pltpu.VMEM(down_weight.shape, jnp.bfloat16),
            pltpu.VMEM((n_dp * CAP, hidden), jnp.bfloat16),
            pltpu.VMEM((2, SIDE, 2, rows, n_local * SIDE * CAP), jnp.bfloat16),
            pltpu.VMEM((rows, columns), jnp.float32),
            pltpu.VMEM((rows, columns), jnp.bfloat16),
            pltpu.VMEM(group_kv.shape, jnp.bfloat16),
            pltpu.VMEM((SIDE, rows, columns // 2), jnp.bfloat16),
            pltpu.VMEM((SIDE, rows, columns // 2), jnp.bfloat16),
            pltpu.VMEM((SIDE, n_exp, rows), jnp.float32),
            pltpu.VMEM((SIDE, n_exp, rows), jnp.float32),
            pltpu.VMEM((SIDE, n_exp, rows), jnp.float32),
            pltpu.VMEM((SIDE, n_exp, rows), jnp.float32),
            dma((2 * SIDE - 2,)),
            dma((2 * SIDE - 2,)),
            dma((2 * SIDE - 2,)),
            dma((2 * SIDE - 2,)),
            dma((2 * SIDE - 2,)),
            dma((2 * SIDE - 2,)),
            dma((n_local * (2 * SIDE - 2),)),
            dma((n_local * (2 * SIDE - 2),)),
            dma((n_local * (2 * SIDE - 2),)),
            dma((n_local * (2 * SIDE - 2),)),
            dma((2 * SIDE - 2,)),
            dma((2 * SIDE - 2,)),
            dma((3,)),
        ],
        compiler_params=pltpu.CompilerParams(
            collective_id=1, has_side_effects=True, vmem_limit_bytes=60 << 20
        ),
        name="experts",
    )(residual, gain, router, routes, page_slots, group_kv, gate_up_weight, down_weight)


def shards(
    tokens,
    lengths,
    request_adapter,
    group_page_slots,
    routes,
    attention_gain,
    query_key_value_weight,
    adapter_down_weight,
    adapter_up_weight,
    output_weight,
    expert_norm_gain,
    router,
    expert_gate_up_weight,
    expert_down_weight,
):
    residual, group_kv = front(
        tokens,
        attention_gain,
        query_key_value_weight,
        adapter_down_weight.transpose(0, 2, 1),
        adapter_up_weight,
        lengths,
        request_adapter,
        output_weight.T,
    )
    pages_grp = group_page_slots.shape[1]
    layer_out, pool = experts(
        residual,
        expert_norm_gain,
        router.T,
        routes.T,
        group_page_slots,
        group_kv.reshape(pages_grp, PAGE, group_kv.shape[2]),
        tokens.shape[0] // PAGE,
        expert_gate_up_weight,
        expert_down_weight,
    )
    return (layer_out, pool)


def solution(mesh):
    return jax.shard_map(
        shards,
        mesh=mesh,
        in_specs=(
            P(("dp", "mp"), None),
            P("dp", None),
            P("dp", None),
            P("dp", None),
            P(("dp", "mp"), None),
            P(),
            P(None, "mp"),
            P("dp", None, None),
            P("dp", None, None),
            P(None, "mp"),
            P(),
            P(),
            P("dp", None, None),
            P("dp", None, None),
        ),
        out_specs=(P(("dp", "mp"), None), P(("dp", "mp"), None, None)),
        check_vma=False,
    )
```

```python
import math

import jax
import jax.numpy as jnp
from jax import lax
from jax.experimental import pallas as pl
from jax.experimental.pallas import tpu as pltpu
from jax.sharding import PartitionSpec as P

HEAD_SIZE = 128
PAGE = 128
CAP = 48
SPAN = 1024

eps = 1e-06
neg_fill = -1e30


MESH = pl.DeviceIdType.MESH


class Ring:
    def __init__(self, buf, own, send, recv, span):
        me = lax.axis_index("mp")
        n = lax.axis_size("mp")
        chips = n // 2
        x, core = me // 2, lax.rem(me, 2)
        self.right = lax.rem(x + 1, chips) * 2 + core
        self.left = lax.rem(x + chips - 1, chips) * 2 + core
        self.far = lax.rem(x + 2, chips) * 2 + core
        self.me = me
        self.partner = x * 2 + 1 - core
        self.buf, self.own, self.send, self.recv = buf, own, send, recv
        self.half = span // 2

    def other(self, slot):
        return slot + 1 - 2 * lax.rem(slot, 2)

    def copy(self, i, slot, part, target, own=False):
        rows = pl.ds(part * self.half, self.half)
        return pltpu.make_async_remote_copy(
            src_ref=self.own.at[rows] if own else self.buf.at[slot, rows],
            dst_ref=self.buf.at[slot, rows],
            send_sem=self.send.at[i],
            recv_sem=self.recv.at[i],
            device_id={"mp": target},
            device_id_type=MESH,
        )

    def begin(self):
        me = self.me
        self.copy(0, me, 0, self.right, True).start()
        self.copy(1, me, 1, self.left, True).start()
        self.copy(2, me, 1, self.right, True).start()
        self.copy(3, me, 0, self.left, True).start()
        self.copy(4, me, 0, self.partner, True).start()
        self.copy(5, me, 1, self.partner, True).start()

    def got(self, i, slot, part):
        self.copy(i, slot, part, self.partner).wait_recv()

    def got_partner(self):
        self.got(4, self.partner, 0)
        self.got(5, self.partner, 1)

    def forward_near(self):
        self.got(0, self.left, 0)
        self.copy(6, self.left, 0, self.right).start()
        self.copy(7, self.left, 0, self.partner).start()
        self.got(1, self.right, 1)
        self.copy(8, self.right, 1, self.left).start()
        self.copy(9, self.right, 1, self.partner).start()

    def forward_rest(self):
        self.got(2, self.left, 1)
        self.copy(10, self.left, 1, self.partner).start()
        self.got(3, self.right, 0)
        self.copy(11, self.right, 0, self.partner).start()

    def got_near(self):
        self.got(7, self.other(self.left), 0)
        self.got(10, self.other(self.left), 1)
        self.got(9, self.other(self.right), 1)
        self.got(11, self.other(self.right), 0)

    def forward_far(self):
        self.got(6, self.far, 0)
        self.copy(12, self.far, 0, self.partner).start()
        self.got(8, self.far, 1)
        self.copy(13, self.far, 1, self.partner).start()

    def got_far(self):
        self.got(12, self.other(self.far), 0)
        self.got(13, self.other(self.far), 1)

    def drain(self):
        for i in range(14):
            self.copy(i, self.me, 0, self.partner, True).wait_send()


HOPS = 14
SIDE = 4


class Spread:
    def __init__(self, ring, buf, own, base, send, recv):
        dp = lax.axis_index("dp")
        self.index = (dp // SIDE, lax.rem(dp, SIDE))
        self.ring, self.buf, self.own, self.base = ring, buf, own, base
        self.chunk = (buf.shape[1] - base) // SIDE
        self.wide = buf.shape[2] // 2
        self.send, self.recv = send, recv
        self.slots = (ring.left, ring.right, ring.far)

    def piece(self, ref, part, index):
        rows = pl.ds(self.base + index * self.chunk, self.chunk)
        return ref.at[rows, pl.ds(part * self.wide, self.wide)]

    def across(self, i, slot, part, target, own=False):
        index = self.index[part]
        return pltpu.make_async_remote_copy(
            src_ref=self.piece(self.own if own else self.buf.at[slot], part, index),
            dst_ref=self.piece(self.buf.at[slot], part, index),
            send_sem=self.send.at[i],
            recv_sem=self.recv.at[i],
            device_id={"mp": target},
            device_id_type=MESH,
        )

    def along(self, s, part, d, back=False):
        z, y = self.index
        step = SIDE - d if back else d
        peer = (
            lax.rem(z + step, SIDE) * SIDE + y if part == 0 else z * SIDE + lax.rem(y + step, SIDE)
        )
        index = lax.rem(self.index[part] + step, SIDE) if back else self.index[part]
        ref = self.piece(self.buf.at[self.slots[s]], part, index)
        i = 6 + (s * 2 + part) * 3 + d - 1
        return pltpu.make_async_remote_copy(
            src_ref=ref,
            dst_ref=ref,
            send_sem=self.send.at[i],
            recv_sem=self.recv.at[i],
            device_id={"dp": peer},
            device_id_type=MESH,
        )

    def hand(self, i, slot, own=False):
        rows = pl.ds(self.base, SIDE * self.chunk)
        return pltpu.make_async_remote_copy(
            src_ref=self.own.at[rows] if own else self.buf.at[slot, rows],
            dst_ref=self.buf.at[slot, rows],
            send_sem=self.send.at[i],
            recv_sem=self.recv.at[i],
            device_id={"mp": self.ring.partner},
            device_id_type=MESH,
        )

    def begin(self):
        ring = self.ring
        self.across(0, ring.me, 0, ring.right, True).start()
        self.across(1, ring.me, 1, ring.left, True).start()
        self.across(2, ring.me, 1, ring.right, True).start()
        self.across(3, ring.me, 0, ring.left, True).start()
        self.hand(27, ring.me, True).start()

    def push(self, s, part):
        for d in (2, 1, 3):
            self.along(s, part, d).start()

    def near(self):
        ring = self.ring
        self.across(0, ring.left, 0, ring.right).wait_recv()
        self.across(4, ring.left, 0, ring.right).start()
        self.push(0, 0)
        self.across(1, ring.right, 1, ring.left).wait_recv()
        self.across(5, ring.right, 1, ring.left).start()
        self.push(1, 1)
        self.across(2, ring.left, 1, ring.right).wait_recv()
        self.push(0, 1)
        self.across(3, ring.right, 0, ring.left).wait_recv()
        self.push(1, 0)

    def distant(self):
        ring = self.ring
        self.across(4, ring.far, 0, ring.right).wait_recv()
        self.push(2, 0)
        self.across(5, ring.far, 1, ring.left).wait_recv()
        self.push(2, 1)

    def finish(self, s):
        for part in (0, 1):
            for d in (1, 2, 3):
                self.along(s, part, d, True).wait_recv()
        self.hand(24 + s, self.slots[s]).start()

    def got(self, s):
        self.hand(24 + s, self.ring.other(self.slots[s])).wait_recv()

    def got_partner(self):
        self.hand(27, self.ring.partner).wait_recv()

    def drain(self):
        ring = self.ring
        for i in range(6):
            self.across(i, ring.me, (0, 1, 1, 0, 0, 1)[i], ring.right, True).wait_send()
        for s in range(3):
            for part in (0, 1):
                for d in (1, 2, 3):
                    self.along(s, part, d).wait_send()
            self.hand(24 + s, self.slots[s]).wait_send()
        self.hand(27, ring.me, True).wait_send()


PASSES = 28


def front_kernel(
    tokens_ref,
    gain_ref,
    weight_ref,
    down_ref,
    up_ref,
    lengths_ref,
    request_ref,
    out_weight_ref,
    residual_ref,
    kv_ref,
    weights,
    adapters,
    out_weights,
    qkv,
    query,
    attended,
    bias,
    normed,
    middle,
    packed_ref,
    weight_send,
    weight_recv,
    low_send,
    low_recv,
    kv_send,
    kv_recv,
    out_send,
    out_recv,
    adapter_send,
    adapter_recv,
    pair_sem,
    local_sem,
):
    dp, mp = lax.axis_index("dp"), lax.axis_index("mp")
    n_dp = lax.axis_size("dp")
    n_mp = lax.axis_size("mp")
    rows, columns = tokens_ref.shape
    wide = weight_ref.shape[1]
    q_blocks = qkv.shape[0] - 2
    rank = up_ref.shape[1]

    depth = weight_ref.shape[0]
    core = lax.rem(mp, 2)
    ring = Ring(weights, weight_ref, weight_send, weight_recv, depth // 2)
    low_rows = Spread(ring, weights, weight_ref, depth // 2, low_send, low_recv)
    kv_ring = Ring(kv_ref, kv_ref.at[mp], kv_send, kv_recv, rows)
    out_rows = Spread(ring, out_weights, out_weight_ref, 0, out_send, out_recv)

    barrier = pltpu.get_barrier_semaphore()
    for peer in (ring.left, ring.right, ring.partner):
        pl.semaphore_signal(barrier, inc=1, device_id={"mp": peer}, device_id_type=MESH)

    @pl.loop(1, n_dp)
    def _(k):
        peer = lax.rem(dp + k, n_dp)
        pl.semaphore_signal(barrier, inc=1, device_id={"dp": peer}, device_id_type=MESH)

    pl.semaphore_wait(barrier, 3 + n_dp - 1)

    def adapter_copy(k, slot, peer):
        return pltpu.make_async_remote_copy(
            src_ref=packed_ref.at[core],
            dst_ref=adapters.at[core, slot],
            send_sem=adapter_send.at[k],
            recv_sem=adapter_recv.at[slot],
            device_id={"dp": peer},
            device_id_type=MESH,
        )

    def adapter_pair(kind):
        return pltpu.make_async_remote_copy(
            src_ref=adapters.at[kind],
            dst_ref=adapters.at[kind],
            send_sem=pair_sem.at[0],
            recv_sem=pair_sem.at[1],
            device_id={"mp": ring.partner},
            device_id_type=MESH,
        )

    low_rows.begin()
    ring.begin()

    packed_ref[0] = down_ref[0]
    packed_ref[1] = up_ref[0]
    own_out = pltpu.make_async_copy(out_weight_ref, out_weights.at[mp], local_sem)
    own_out.start()

    widened = tokens_ref[...].astype(jnp.float32)
    inv_rms = lax.rsqrt(jnp.mean(widened * widened, axis=1, keepdims=True) + eps)
    normed[...] = (widened * inv_rms * gain_ref[...][None, :]).astype(jnp.bfloat16)
    adapters[core, dp] = packed_ref[core]

    low_rows.near()

    @pl.loop(1, n_dp)
    def _(k):
        adapter_copy(k, dp, lax.rem(dp + k, n_dp)).start()

    place = lax.broadcasted_iota(jnp.int32, (rows, 1), 0) + mp * rows
    low = jnp.zeros((rows, 1), jnp.int32)
    adapter = jnp.zeros((rows, 1), jnp.int32) + request_ref[:, 0:1]
    ends = jnp.zeros((1, 1), jnp.int32)
    for r in range(1, lengths_ref.shape[1]):
        ends = ends + lengths_ref[:, r - 1 : r]
        passed = place >= ends
        low = jnp.where(passed, ends, low)
        adapter = jnp.where(passed, request_ref[:, r : r + 1], adapter)

    window = bias.shape[1]
    first = jnp.maximum(mp + 1 - window // rows, 0)
    key = lax.broadcasted_iota(jnp.int32, (rows, window), 1) + first * rows
    bias[...] = jnp.where((key >= low) & (key <= place), 0.0, neg_fill)

    def project(slot):
        qkv[slot] = jnp.dot(normed[...], weights[slot], preferred_element_type=jnp.float32)

    qkv[mp] = jnp.dot(normed[...], weight_ref[...], preferred_element_type=jnp.float32)
    low_rows.distant()
    ring.forward_near()
    ring.got_partner()
    low_rows.got_partner()
    project(ring.partner)
    low_rows.finish(0)
    low_rows.finish(1)
    ring.forward_rest()
    project(ring.left)
    project(ring.right)
    low_rows.finish(2)
    ring.forward_far()
    out_rows.begin()
    project(ring.far)
    ring.got_near()
    low_rows.got(0)
    low_rows.got(1)
    project(ring.other(ring.left))
    project(ring.other(ring.right))
    ring.got_far()
    low_rows.got(2)
    project(ring.other(ring.far))

    kv_ref[mp, :, :wide] = qkv[q_blocks].astype(jnp.bfloat16)
    kv_ref[mp, :, wide:] = qkv[q_blocks + 1].astype(jnp.bfloat16)

    @pl.loop(1, n_dp)
    def _(k):
        source = lax.rem(dp + k, n_dp)
        adapter_copy(k, source, source).wait_recv()

    adapter_pair(core).start()
    kv_ring.begin()
    adapter_pair(1 - core).wait_recv()

    down = adapters[0].reshape(n_dp * rank, columns)
    mid = lax.dot_general(
        normed[...], down, (((1,), (1,)), ((), ())), preferred_element_type=jnp.float32
    )
    owner = lax.broadcasted_iota(jnp.int32, (rows, n_dp * rank), 1) // rank
    middle[...] = jnp.where(owner == adapter, mid, 0.0).astype(jnp.bfloat16)

    def finish_query(j):
        up = adapters[1, :, :, j * wide : (j + 1) * wide].reshape(n_dp * rank, wide)
        extra = jnp.dot(middle[...], up, preferred_element_type=jnp.float32)
        query[j] = (qkv[j] + extra).astype(jnp.bfloat16)

    finish_query(0)
    finish_query(1)
    out_rows.near()
    kv_ring.forward_near()
    for j in range(2, q_blocks):
        finish_query(j)
    kv_ring.got_partner()
    kv_ring.forward_rest()
    out_rows.distant()
    kv_ring.got_near()
    kv_ring.forward_far()
    kv_ring.got_far()

    n_kv = 2
    share = q_blocks // n_kv
    for kv_head in range(n_kv):
        k_cols = slice(kv_head * HEAD_SIZE, (kv_head + 1) * HEAD_SIZE)
        v_cols = slice(wide + kv_head * HEAD_SIZE, wide + (kv_head + 1) * HEAD_SIZE)

        @pl.loop(0, share)
        def _(step):
            block = step + kv_head * share
            for lane in range(wide // HEAD_SIZE):
                cols = slice(lane * HEAD_SIZE, (lane + 1) * HEAD_SIZE)
                keys = kv_ref[pl.ds(first, window // rows), :, k_cols].reshape(window, HEAD_SIZE)
                values = kv_ref[pl.ds(first, window // rows), :, v_cols].reshape(window, HEAD_SIZE)
                scores = lax.dot_general(
                    query[block, :, cols],
                    keys,
                    (((1,), (1,)), ((), ())),
                    preferred_element_type=jnp.float32,
                )
                scores = scores + bias[...]
                row_max = jnp.max(scores, axis=1, keepdims=True)
                expd = jnp.exp2((scores - row_max) * (HEAD_SIZE ** (-0.5) * math.log2(math.e)))
                total = jnp.sum(expd, axis=1, keepdims=True)
                mixed = jnp.dot(
                    expd.astype(jnp.bfloat16), values, preferred_element_type=jnp.float32
                )
                attended[block, :, cols] = (mixed / total).astype(jnp.bfloat16)

        if kv_head == 0:
            out_rows.finish(0)
            out_rows.finish(1)

    out_rows.finish(2)
    out_rows.got_partner()
    for s in range(3):
        out_rows.got(s)
    own_out.wait()

    own_rows = out_weights.shape[1]
    for lo in range(0, n_mp, 2):
        part = out_weights[lo : lo + 2].reshape(2 * own_rows, columns)
        total = tokens_ref[:, lo * own_rows : (lo + 2) * own_rows].astype(jnp.float32)
        for j in range(q_blocks):
            total += lax.dot_general(
                attended[j],
                part[:, j * wide : (j + 1) * wide],
                (((1,), (1,)), ((), ())),
                preferred_element_type=jnp.float32,
            )
        residual_ref[:, lo * own_rows : (lo + 2) * own_rows] = total.astype(jnp.bfloat16)

    ring.drain()
    kv_ring.drain()
    out_rows.drain()
    low_rows.drain()
    adapter_pair(core).wait_send()

    @pl.loop(1, n_dp)
    def _(k):
        adapter_copy(k, dp, lax.rem(dp + k, n_dp)).wait_send()


def front(tokens, gain, weight, down, up, lengths, request, out_weight):
    n_dp, n_mp = lax.axis_size("dp"), lax.axis_size("mp")
    rows, columns = tokens.shape
    depth, wide = weight.shape
    q_blocks = columns // wide
    rank = up.shape[1]
    window = min(n_mp * rows, rows + SPAN)
    dma = pltpu.SemaphoreType.DMA
    vmem = pl.BlockSpec(memory_space=pltpu.VMEM)
    return pl.pallas_call(
        front_kernel,
        in_specs=[vmem] * 8,
        out_specs=[vmem] * 2,
        out_shape=[
            jax.ShapeDtypeStruct((rows, columns), jnp.bfloat16),
            jax.ShapeDtypeStruct((n_mp, rows, 2 * wide), jnp.bfloat16),
        ],
        scratch_shapes=[
            pltpu.VMEM((n_mp, depth, wide), jnp.bfloat16),
            pltpu.VMEM((2, n_dp, rank, columns), jnp.bfloat16),
            pltpu.VMEM((n_mp,) + out_weight.shape, jnp.bfloat16),
            pltpu.VMEM((n_mp, rows, wide), jnp.float32),
            pltpu.VMEM((q_blocks, rows, wide), jnp.bfloat16),
            pltpu.VMEM((q_blocks, rows, wide), jnp.bfloat16),
            pltpu.VMEM((rows, window), jnp.float32),
            pltpu.VMEM((rows, columns), jnp.bfloat16),
            pltpu.VMEM((rows, n_dp * rank), jnp.bfloat16),
            pltpu.VMEM((2, rank, columns), jnp.bfloat16),
            dma((HOPS,)),
            dma((HOPS,)),
            dma((PASSES,)),
            dma((PASSES,)),
            dma((HOPS,)),
            dma((HOPS,)),
            dma((PASSES,)),
            dma((PASSES,)),
            dma((n_dp,)),
            dma((n_dp,)),
            dma((2,)),
            dma(()),
        ],
        compiler_params=pltpu.CompilerParams(
            collective_id=0, has_side_effects=True, vmem_limit_bytes=60 << 20
        ),
        name="front",
    )(tokens, gain, weight, down, up, lengths, request, out_weight)


def expert_kernel(
    residual_ref,
    gain_ref,
    router_ref,
    routes_ref,
    page_slots_ref,
    kv_hbm,
    up_hbm,
    down_hbm,
    out_ref,
    pool_ref,
    sent,
    arrived,
    produced,
    middle,
    folding,
    folded,
    up,
    down,
    active,
    back,
    total,
    ffn_ref,
    pages,
    along_z,
    along_y,
    places_z,
    places_y,
    shares_z,
    shares_y,
    near_send,
    near_recv,
    table_send,
    table_recv,
    share_send,
    share_recv,
    go_send,
    go_recv,
    back_send,
    back_recv,
    fold_send,
    fold_recv,
    local_sem,
):
    dp = lax.axis_index("dp")
    n_local, side, _, cap, columns = produced.shape
    n_dp = side * side
    half = columns // 2
    z, y = dp // side, lax.rem(dp, side)
    slots = n_dp * cap
    hidden = down.shape[1]
    rows = ffn_ref.shape[0]
    n_exp = n_local * n_dp
    tile = 512

    barrier = pltpu.get_barrier_semaphore()

    @pl.loop(1, n_dp)
    def _(k):
        peer = lax.rem(dp + k, n_dp)
        pl.semaphore_signal(barrier, inc=1, device_id={"dp": peer}, device_id_type=MESH)

    up_copy = pltpu.make_async_copy(up_hbm, up, local_sem.at[0])
    down_copy = pltpu.make_async_copy(down_hbm, down, local_sem.at[1])
    kv_copy = pltpu.make_async_copy(kv_hbm, pages, local_sem.at[2])
    up_copy.start()
    down_copy.start()
    kv_copy.start()

    def spread(table, e, holders):
        return [
            jnp.broadcast_to(table[pl.ds(owner * n_local + e, 1), :], (cap, rows))
            for owner in holders
        ]

    count = lax.broadcasted_iota(jnp.int32, (cap, rows), 0).astype(jnp.float32)
    wanted = routes_ref[...]
    named = lax.broadcasted_iota(jnp.int32, (n_exp, rows), 0)
    hits = wanted[0:1] == named
    for k in range(1, routes_ref.shape[0]):
        hits = hits | (wanted[k : k + 1] == named)
    early = lax.broadcasted_iota(jnp.int32, (rows, rows), 0)
    late = lax.broadcasted_iota(jnp.int32, (rows, rows), 1)
    before = jnp.where(early < late, 1.0, 0.0).astype(jnp.bfloat16)
    marks = jnp.where(hits, 1.0, 0.0)
    ranks = jnp.dot(marks.astype(jnp.bfloat16), before, preferred_element_type=jnp.float32)
    places = jnp.where(hits, ranks, -1.0)
    places_z[z] = places
    places_y[y] = places

    widened = residual_ref[...].astype(jnp.float32)
    inv_rms = lax.rsqrt(jnp.mean(widened * widened, axis=1, keepdims=True) + eps)
    ffn_ref[...] = (widened * inv_rms * gain_ref[...][None, :]).astype(jnp.bfloat16)
    along_z[z] = ffn_ref[:, :half]
    along_y[y] = ffn_ref[:, half:]

    fields = (along_z, along_y)
    tables = (places_z, places_y)
    weights = (shares_z, shares_y)
    index = (z, y)

    def peer_at(part, d):
        if part == 0:
            return lax.rem(z + d, side) * side + y
        return z * side + lax.rem(y + d, side)

    def near(ref, send, recv, part, d, back=False):
        step = side - d if back else 0
        spot = ref.at[lax.rem(index[part] + step, side)]
        i = part * (side - 1) + d - 1
        return pltpu.make_async_remote_copy(
            src_ref=spot,
            dst_ref=spot,
            send_sem=send.at[i],
            recv_sem=recv.at[i],
            device_id={"dp": peer_at(part, d)},
            device_id_type=MESH,
        )

    def landing(part, e, d, i):
        if part == 0:
            return arrived.at[e, d, i, :, pl.ds(0, half)]
        return arrived.at[e, i, d, :, pl.ds(half, half)]

    def leg(part, e, d, i):
        sem = (e * 2 + part) * (side - 1) + d - 1
        return pltpu.make_async_remote_copy(
            src_ref=sent.at[part, e, d, i],
            dst_ref=landing(part, e, d, i),
            send_sem=go_send.at[sem],
            recv_sem=go_recv.at[sem],
            device_id={"dp": peer_at(1 - part, d)},
            device_id_type=MESH,
        )

    def legs(part, e, d):
        sem = (e * 2 + part) * (side - 1) + d - 1
        return pltpu.make_async_remote_copy(
            src_ref=sent.at[part, e, d],
            dst_ref=landing(part, e, d, slice(None)),
            send_sem=go_send.at[sem],
            recv_sem=go_recv.at[sem],
            device_id={"dp": peer_at(1 - part, d)},
            device_id_type=MESH,
        )

    def pack(part, e, i):
        origin = lax.rem(index[part] + side - i, side)
        table = tables[part].at[origin]
        pick = jnp.concatenate(
            [
                jnp.where(row == count, 1.0, 0.0).astype(jnp.bfloat16)
                for row in spread(table, e, [peer_at(1 - part, d) for d in range(side)])
            ],
            axis=0,
        )
        got = jnp.dot(pick, fields[part][origin], preferred_element_type=jnp.float32)
        got = got.astype(jnp.bfloat16).reshape(side, cap, half)
        if part == 0:
            arrived[e, 0, i, :, :half] = got[0]
        else:
            arrived[e, i, 0, :, half:] = got[0]
        for d in range(1, side):
            sent[part, e, d, i] = got[d]

    def dispatch(part, e, i):
        for d in (2, 1, 3):
            leg(part, e, d, i).start()

    def compute(e):
        @pl.loop(0, hidden // 256)
        def _(j):
            gate_cols = pl.ds(pl.multiple_of(j * 256, 256), 256)
            up_cols = pl.ds(pl.multiple_of(hidden + j * 256, 256), 256)
            given = arrived[e].reshape(slots, columns)
            gate = jnp.dot(given, up[e, :, gate_cols], preferred_element_type=jnp.float32)
            lift = jnp.dot(given, up[e, :, up_cols], preferred_element_type=jnp.float32)
            active[:, gate_cols] = (jnp.maximum(gate, 0.0) * lift).astype(jnp.bfloat16)

        @pl.loop(0, columns // 256)
        def _(j):
            cols = pl.ds(pl.multiple_of(j * 256, 256), 256)
            made = jnp.dot(active[...], down[e, :, cols], preferred_element_type=jnp.float32)
            produced[e, :, :, :, cols] = made.astype(jnp.bfloat16).reshape(side, side, cap, 256)

        middle[0, e, 0] = produced[e, 0, :, :, :half]
        middle[1, e, 0] = produced[e, :, 0, :, half:]

    def give_back(part, e, d, i):
        if part == 0:
            made = produced.at[e, d, i, :, pl.ds(0, half)]
        else:
            made = produced.at[e, i, d, :, pl.ds(half, half)]
        sem = (e * 2 + part) * side + i
        return pltpu.make_async_remote_copy(
            src_ref=made,
            dst_ref=middle.at[part, e, d, i],
            send_sem=back_send.at[sem],
            recv_sem=back_recv.at[sem],
            device_id={"dp": peer_at(1 - part, side - d)},
            device_id_type=MESH,
        )

    def given_back(part, e, i):
        others = slice(1, side)
        if part == 0:
            made = produced.at[e, others, i, :, pl.ds(0, half)]
        else:
            made = produced.at[e, i, others, :, pl.ds(half, half)]
        sem = (e * 2 + part) * side + i
        return pltpu.make_async_remote_copy(
            src_ref=made,
            dst_ref=middle.at[part, e, others, i],
            send_sem=back_send.at[sem],
            recv_sem=back_recv.at[sem],
            device_id={"dp": peer_at(1 - part, 1)},
            device_id_type=MESH,
        )

    def fold(part, i):
        sem = part * (side - 1) + i - 1
        return pltpu.make_async_remote_copy(
            src_ref=folding.at[part, i],
            dst_ref=folded.at[part, i],
            send_sem=fold_send.at[sem],
            recv_sem=fold_recv.at[sem],
            device_id={"dp": peer_at(part, side - i)},
            device_id_type=MESH,
        )

    def weigh(part, i):
        origin = lax.rem(index[part] + side - i, side)
        holders = [peer_at(1 - part, d) for d in range(side)]
        high, rest = [], []
        for e in range(n_local):
            spots = spread(tables[part].at[origin], e, holders)
            for spot, share in zip(spots, spread(weights[part].at[origin], e, holders)):
                chosen = jnp.where(spot == count, share, 0.0)
                top = chosen.astype(jnp.bfloat16).astype(jnp.float32)
                high.append(top)
                rest.append(chosen - top)
        back[part, i, 0] = jnp.concatenate(high, axis=0).T.astype(jnp.bfloat16)
        back[part, i, 1] = jnp.concatenate(rest, axis=0).T.astype(jnp.bfloat16)

    def partial(part, i):
        given = middle[part, :, :, i].reshape(n_local * side * cap, half)
        mixed = jnp.dot(back[part, i, 0], given, preferred_element_type=jnp.float32)
        return mixed + jnp.dot(back[part, i, 1], given, preferred_element_type=jnp.float32)

    pl.semaphore_wait(barrier, n_dp - 1)
    for d in (1, 3, 2):
        for part in (0, 1):
            near(tables[part], table_send, table_recv, part, d).start()
            near(fields[part], near_send, near_recv, part, d).start()
    logits = lax.dot_general(
        router_ref[...], ffn_ref[...], (((1,), (1,)), ((), ())), preferred_element_type=jnp.float32
    )
    peak = jnp.max(jnp.where(hits, logits, neg_fill), axis=0, keepdims=True)
    expl = jnp.where(hits, jnp.exp(jnp.where(hits, logits, peak) - peak), 0.0)
    shares = expl / jnp.sum(expl, axis=0, keepdims=True)
    shares_z[z] = shares
    shares_y[y] = shares
    pack(0, 0, 0)
    pack(1, 0, 0)
    for d in (1, 3, 2):
        for part in (0, 1):
            near(weights[part], share_send, share_recv, part, d).start()
    dispatch(0, 0, 0)
    waiting = (1, 0, 0)
    for d in (1, 3, 2):
        for part in (0, 1):
            near(tables[part], table_send, table_recv, part, d, True).wait_recv()
            near(fields[part], near_send, near_recv, part, d, True).wait_recv()
            pack(part, 0, d)
            dispatch(*waiting)
            waiting = (part, 0, d)
    for i in range(side):
        for part in (0, 1):
            pack(part, 1, i)
            dispatch(*waiting)
            waiting = (part, 1, i)
    weigh(0, 0)
    dispatch(*waiting)
    weigh(1, 0)
    for d in (1, 3, 2):
        for part in (0, 1):
            near(weights[part], share_send, share_recv, part, d, True).wait_recv()
            weigh(part, d)

    kv_copy.wait()
    held = pool_ref.shape[0]
    order = lax.broadcasted_iota(jnp.int32, page_slots_ref.shape, 1)
    for i in range(held):
        mine = lax.axis_index("mp") * held + i

        def pick_page(p, page):
            slot = jnp.sum(jnp.where(order == p, page_slots_ref[...], 0), axis=1, keepdims=True)
            here = slot == mine
            return jnp.where(here, pages[p].astype(jnp.float32), page)

        page = lax.fori_loop(
            0, pages.shape[0], pick_page, jnp.zeros(pages.shape[1:], jnp.float32)
        )
        pool_ref[i] = page.astype(jnp.bfloat16)

    up_copy.wait()
    down_copy.wait()
    for e in range(n_local):
        for part in (0, 1):
            for d in range(1, side):
                legs(part, e, d).wait_recv()
        compute(e)
        for i in (2, 1, 3, 0):
            for d in (2, 1, 3):
                for part in (0, 1):
                    give_back(part, e, d, i).start()
    ready = None
    for i in (2, 1, 3):
        for part in (0, 1):
            for e in range(n_local):
                given_back(part, e, i).wait_recv()
            folding[part, i] = partial(part, i).astype(jnp.bfloat16)
            if ready:
                fold(*ready).start()
            ready = (part, i)
    for part in (0, 1):
        for e in range(n_local):
            given_back(part, e, 0).wait_recv()
        cols = pl.ds(part * half, half)
        total[:, cols] = residual_ref[:, cols].astype(jnp.float32) + partial(part, 0)
        if ready:
            fold(*ready).start()
            ready = None
    for part in (0, 1):
        cols = pl.ds(part * half, half)
        for i in range(1, side):
            fold(part, i).wait_recv()
        mixed = total[:, cols]
        for i in range(1, side):
            mixed += folded[part, i].astype(jnp.float32)
        out_ref[:, cols] = mixed.astype(jnp.bfloat16)
    for part in (0, 1):
        for d in range(1, side):
            near(tables[part], table_send, table_recv, part, d).wait_send()
            near(fields[part], near_send, near_recv, part, d).wait_send()
            near(weights[part], share_send, share_recv, part, d).wait_send()
            fold(part, d).wait_send()
            for e in range(n_local):
                legs(part, e, d).wait_send()
        for e in range(n_local):
            for i in range(side):
                given_back(part, e, i).wait_send()


def experts(
    residual, gain, router, routes, page_slots, group_kv, held, gate_up_weight, down_weight
):
    rows, columns = residual.shape
    n_dp = lax.axis_size("dp")
    n_local, hidden = down_weight.shape[:2]
    n_exp = router.shape[0]
    dma = pltpu.SemaphoreType.DMA
    vmem = pl.BlockSpec(memory_space=pltpu.VMEM)
    hbm = pl.BlockSpec(memory_space=pl.ANY)
    return pl.pallas_call(
        expert_kernel,
        in_specs=[vmem] * 5 + [hbm] * 3,
        out_specs=[vmem] * 2,
        out_shape=[
            jax.ShapeDtypeStruct((rows, columns), jnp.bfloat16),
            jax.ShapeDtypeStruct((held,) + group_kv.shape[1:], jnp.bfloat16),
        ],
        scratch_shapes=[
            pltpu.VMEM((2, n_local, SIDE, SIDE, CAP, columns // 2), jnp.bfloat16),
            pltpu.VMEM((n_local, SIDE, SIDE, CAP, columns), jnp.bfloat16),
            pltpu.VMEM((n_local, SIDE, SIDE, CAP, columns), jnp.bfloat16),
            pltpu.VMEM((2, n_local, SIDE, SIDE, CAP, columns // 2), jnp.bfloat16),
            pltpu.VMEM((2, SIDE, rows, columns // 2), jnp.bfloat16),
            pltpu.VMEM((2, SIDE, rows, columns // 2), jnp.bfloat16),
            pltpu.VMEM(gate_up_weight.shape, jnp.bfloat16),
            pltpu.VMEM(down_weight.shape, jnp.bfloat16),
            pltpu.VMEM((n_dp * CAP, hidden), jnp.bfloat16),
            pltpu.VMEM((2, SIDE, 2, rows, n_local * SIDE * CAP), jnp.bfloat16),
            pltpu.VMEM((rows, columns), jnp.float32),
            pltpu.VMEM((rows, columns), jnp.bfloat16),
            pltpu.VMEM(group_kv.shape, jnp.bfloat16),
            pltpu.VMEM((SIDE, rows, columns // 2), jnp.bfloat16),
            pltpu.VMEM((SIDE, rows, columns // 2), jnp.bfloat16),
            pltpu.VMEM((SIDE, n_exp, rows), jnp.float32),
            pltpu.VMEM((SIDE, n_exp, rows), jnp.float32),
            pltpu.VMEM((SIDE, n_exp, rows), jnp.float32),
            pltpu.VMEM((SIDE, n_exp, rows), jnp.float32),
            dma((2 * SIDE - 2,)),
            dma((2 * SIDE - 2,)),
            dma((2 * SIDE - 2,)),
            dma((2 * SIDE - 2,)),
            dma((2 * SIDE - 2,)),
            dma((2 * SIDE - 2,)),
            dma((n_local * (2 * SIDE - 2),)),
            dma((n_local * (2 * SIDE - 2),)),
            dma((n_local * 2 * SIDE,)),
            dma((n_local * 2 * SIDE,)),
            dma((2 * SIDE - 2,)),
            dma((2 * SIDE - 2,)),
            dma((3,)),
        ],
        compiler_params=pltpu.CompilerParams(
            collective_id=1, has_side_effects=True, vmem_limit_bytes=60 << 20
        ),
        name="experts",
    )(residual, gain, router, routes, page_slots, group_kv, gate_up_weight, down_weight)


def finish_kernel(layer_ref, pool_ref, layer_out_ref, pool_out_ref):
    layer_out_ref[...] = layer_ref[...]
    pool_out_ref[...] = pool_ref[...]


def finish(layer_out, pool):
    vmem = pl.BlockSpec(memory_space=pltpu.VMEM)
    return pl.pallas_call(
        finish_kernel,
        in_specs=[vmem] * 2,
        out_specs=[vmem] * 2,
        out_shape=[
            jax.ShapeDtypeStruct(layer_out.shape, layer_out.dtype),
            jax.ShapeDtypeStruct(pool.shape, pool.dtype),
        ],
        name="finish",
    )(layer_out, pool)


def shards(
    tokens,
    lengths,
    request_adapter,
    group_page_slots,
    routes,
    attention_gain,
    query_key_value_weight,
    adapter_down_weight,
    adapter_up_weight,
    output_weight,
    expert_norm_gain,
    router,
    expert_gate_up_weight,
    expert_down_weight,
):
    residual, group_kv = front(
        tokens,
        attention_gain,
        query_key_value_weight,
        adapter_down_weight.transpose(0, 2, 1),
        adapter_up_weight,
        lengths,
        request_adapter,
        output_weight.T,
    )
    pages_grp = group_page_slots.shape[1]
    layer_out, pool = experts(
        residual,
        expert_norm_gain,
        router.T,
        routes.T,
        group_page_slots,
        group_kv.reshape(pages_grp, PAGE, group_kv.shape[2]),
        tokens.shape[0] // PAGE,
        expert_gate_up_weight,
        expert_down_weight,
    )
    return tuple(finish(layer_out, pool))


def solution(mesh):
    return jax.shard_map(
        shards,
        mesh=mesh,
        in_specs=(
            P(("dp", "mp"), None),
            P("dp", None),
            P("dp", None),
            P("dp", None),
            P(("dp", "mp"), None),
            P(),
            P(None, "mp"),
            P("dp", None, None),
            P("dp", None, None),
            P(None, "mp"),
            P(),
            P(),
            P("dp", None, None),
            P("dp", None, None),
        ),
        out_specs=(P(("dp", "mp"), None), P(("dp", "mp"), None, None)),
        check_vma=False,
    )
```
